128 devices in a mesh: lon: 32 (over x_hi, z, y), ch: 4 (over x_lo, core).
Axes of the slice: x: 4 (x_hi: 2, x_lo: 2; x = x_hi * 2 + x_lo), y: 4, z: 4, core: 2. Of those that a mesh axis runs over, the one named last changes fastest.
Arguments:
- ocean_state: bfloat16 [400, 64, 4096], P('ch', None, 'lon'), may hold values from -6 to 6
- sea_mask: int32 [64, 4096], P(None, 'lon'), may hold values 0 or 1
- kernel: float32 [400, 49], P('ch'), may hold values from -0.875 to 0.875
- conv_bias: float32 [400], P('ch'), may hold values from -3 to 3
- norm_gain: float32 [400], replicated, may hold values from 0.1 to 1.9
- norm_bias: float32 [400], replicated, may hold values from -2 to 2
- weight_in: bfloat16 [400, 1600], replicated, may hold values from -0.3125 to 0.3125
- bias_in: float32 [1600], replicated, may hold values from -3 to 3
- weight_out: bfloat16 [1600, 400], replicated, may hold values from -0.15625 to 0.15625
- bias_out: float32 [400], replicated, may hold values from -3 to 3
- layer_scale: float32 [400], P('ch'), may hold values from 0.5 to 2
- cotangent: bfloat16 [400, 64, 4096], P('ch', None, 'lon'), may hold values from -6 to 6
Outputs:
- updated: bfloat16 [400, 64, 4096], P('ch', None, 'lon')
- grad_state: bfloat16 [400, 64, 4096], P('ch', None, 'lon')
- grad_weight_in: float32 [400, 1600], replicated
- grad_weight_out: float32 [1600, 400], replicated
The draws below stay inside these ranges and needn't reach their ends.
Inputs may be any that keep to these rules, and one draw needn't show every extreme that they name: `sea_mask`: 1 marks an ocean cell, 0 a land cell.
All inputs are finite; a program needn't handle non-finite values. No bound on the sum of `sea_mask` on one device may be relied on, other than what follows from the above.
Results may differ from the reference program's by a relative error of at most 0.0077.
Values may be sent and summed in bfloat16 or wider, within the bound.
No kernel may reach another device: no remote copies, remote signals or barrier semaphores. Data moves between devices by JAX's collectives and lax.ppermute only.
A program may use at most 192 MiB of HBM per device.

```python
import math
import jax
import jax.numpy as jnp
from jax import lax

C = 400
HID = 1600
KW = 7
ROWS = 64
LON = 4096


def plant(drawn, own_key, low, largest):
    longest = drawn.shape.index(max(drawn.shape))
    spots = []
    for shift in (0, 1):
        where = [jax.random.randint(jax.random.fold_in(own_key, axis), (), 0, length) for axis, length in enumerate(drawn.shape)]
        where[longest] = (where[longest] + shift) % drawn.shape[longest]
        spots.append(tuple(where))
    return drawn.at[spots[0]].set(low).at[spots[1]].set(largest)


def level_of(stream_key, dims, shards, low, largest):
    gain, own = 1.0, jax.random.fold_in(stream_key, 6)
    for position, shards_of in shards:
        heights = jnp.exp(jax.random.uniform(jax.random.fold_in(own, position), (shards_of,), jnp.float32, low / len(shards), largest / len(shards)))
        gain = gain * jnp.repeat(heights, dims[position] // shards_of).reshape([-1 if axis == position else 1 for axis in range(len(dims))])
    return gain


def gaussian(own_key, shape, deviation, bound, pieces=(), kind=jnp.bfloat16):
    values = jax.random.normal(own_key, shape, jnp.float32) * deviation
    if len(pieces) > 0:
        values = level_of(own_key, shape, pieces, -0.22, 0.18) * values
    return jnp.clip(values, min=-bound, max=bound).astype(kind)


def setup_inputs(seed: int = 0) -> dict:
    streams_of = jax.random.split(jax.random.key(seed), 13)
    return {
        "ocean_state": gaussian(streams_of[0], (C, ROWS, LON), 1.0, 6.0, ((0, 4), (2, 32))),
        "sea_mask": plant((jax.random.randint(streams_of[1], (ROWS, LON), 0, 4) < 3).astype(jnp.int32), jax.random.fold_in(streams_of[1], 1), 0, 1),
        "kernel": gaussian(streams_of[2], (C, KW * KW), (KW * KW) ** -0.5, 0.875, ((0, 4),), jnp.float32),
        "conv_bias": gaussian(streams_of[3], (C,), 0.5, 3.0, ((0, 4),), jnp.float32),
        "norm_gain": jnp.clip(1.0 + 0.18 * jax.random.normal(streams_of[4], (C,), jnp.float32), 0.1, 1.9),
        "norm_bias": gaussian(streams_of[5], (C,), 0.3, 2.0, (), jnp.float32),
        "weight_in": gaussian(streams_of[6], (C, HID), C ** -0.5, 0.3125),
        "bias_in": gaussian(streams_of[7], (HID,), 0.5, 3.0, (), jnp.float32),
        "weight_out": gaussian(streams_of[8], (HID, C), HID ** -0.5, 0.15625),
        "bias_out": gaussian(streams_of[9], (C,), 0.5, 3.0, (), jnp.float32),
        "layer_scale": jnp.clip(jnp.exp(math.log(2.0) - 1.3862944 * jax.random.uniform(streams_of[10], (C,), jnp.float32) ** level_of(streams_of[10], (C,), ((0, 4),), -0.2, 0.2)), 0.5, 2.0),
        "cotangent": gaussian(streams_of[11], (C, ROWS, LON), 1.0, 6.0, ((0, 4), (2, 32))),
    }


root_coef = math.sqrt(2.0 / math.pi)
cubic_coef = 0.044715
norm_eps = 1e-06

def gelu_parts(pre_act):
    inner_arg = root_coef * (pre_act + cubic_coef * pre_act * pre_act * pre_act)
    tangent = jnp.tanh(inner_arg)
    gelu_value = 0.5 * pre_act * (1.0 + tangent)
    gelu_slope = 0.5 * (1.0 + tangent) + 0.5 * pre_act * (1.0 - tangent * tangent) * root_coef * (1.0 + 3.0 * cubic_coef * pre_act * pre_act)
    return (gelu_value, gelu_slope)

def depth_taps(padded, kernel, row_count, lon_cells):
    tap_total = jnp.zeros((padded.shape[0], row_count, lon_cells), jnp.float32)
    for row_off in range(KW):
        for col_off in range(KW):
            tap_total = tap_total + kernel[:, row_off * KW + col_off][:, None, None] * padded[:, row_off:row_off + row_count, col_off:col_off + lon_cells]
    return tap_total

def depth_back(padded_grad, kernel, row_count, lon_cells):
    span = KW - 1
    tap_total = jnp.zeros((padded_grad.shape[0], row_count, lon_cells), jnp.float32)
    for row_off in range(KW):
        for col_off in range(KW):
            tap_total = tap_total + kernel[:, row_off * KW + col_off][:, None, None] * padded_grad[:, span - row_off:span - row_off + row_count, span - col_off:span - col_off + lon_cells]
    return tap_total

def block_math(conv_cells, grad_cells, norm_gain, norm_bias, weight_in, bias_in, weight_out, bias_out):
    full_width = conv_cells.shape[0]
    values = conv_cells.astype(jnp.float32)
    mean_val = lax.optimization_barrier(jnp.sum(values, axis=0)) / full_width
    square = lax.optimization_barrier(jnp.sum(values * values, axis=0)) / full_width
    inv_std = lax.rsqrt(square - mean_val * mean_val + norm_eps)
    centred = (values - mean_val) * inv_std
    normed = (centred * norm_gain[:, None] + norm_bias[:, None]).astype(jnp.bfloat16)
    pre_act = jnp.dot(weight_in.T, normed, preferred_element_type=jnp.float32) + bias_in[:, None]
    gelu_value, gelu_slope = gelu_parts(pre_act)
    activation = gelu_value.astype(jnp.bfloat16)
    branch = (jnp.dot(weight_out.T, activation, preferred_element_type=jnp.float32) + bias_out[:, None]).astype(jnp.bfloat16)
    grad_act = jnp.dot(weight_out, grad_cells, preferred_element_type=jnp.float32)
    grad_pre = (grad_act * gelu_slope).astype(jnp.bfloat16)
    part_out = jnp.dot(activation, grad_cells.T, preferred_element_type=jnp.float32)
    part_in = jnp.dot(normed, grad_pre.T, preferred_element_type=jnp.float32)
    grad_normed = jnp.dot(weight_in, grad_pre, preferred_element_type=jnp.float32)
    scaled_grad = grad_normed * norm_gain[:, None]
    mean_first = lax.optimization_barrier(jnp.sum(scaled_grad, axis=0)) / full_width
    mean_second = lax.optimization_barrier(jnp.sum(scaled_grad * centred, axis=0)) / full_width
    grad_conv = (inv_std * (scaled_grad - mean_first - centred * mean_second)).astype(jnp.bfloat16)
    return (branch, grad_conv, part_in, part_out)

def wrap_pad(array_f):
    rim_width = KW // 2
    wrapped = jnp.concatenate([array_f[:, :, -rim_width:], array_f, array_f[:, :, :rim_width]], axis=2)
    return jnp.pad(wrapped, ((0, 0), (rim_width, rim_width), (0, 0)))

def reference(ocean_state, sea_mask, kernel, conv_bias, norm_gain, norm_bias, weight_in, bias_in, weight_out, bias_out, layer_scale, cotangent):
    chan_count, row_count, lon_cells = ocean_state.shape
    state_f = ocean_state.astype(jnp.float32)
    padded = wrap_pad(state_f)
    conv_out = (depth_taps(padded, kernel, row_count, lon_cells) + conv_bias[:, None, None]).astype(jnp.bfloat16)
    mask_f = sea_mask.astype(jnp.float32)[None]
    grad_out = cotangent.astype(jnp.float32) * mask_f
    grad_branch = (grad_out * layer_scale[:, None, None]).astype(jnp.bfloat16)
    hid_count = weight_in.shape[1]

    def row_step(running, row_items):
        conv_row, grad_row = row_items
        branch, grad_conv, part_in, part_out = block_math(conv_row, grad_row, norm_gain, norm_bias, weight_in, bias_in, weight_out, bias_out)
        return ((running[0] + part_in, running[1] + part_out), (branch, grad_conv))
    zero_sums = (jnp.zeros((chan_count, hid_count), jnp.float32), jnp.zeros((hid_count, chan_count), jnp.float32))
    sums_out, rows_out = lax.scan(row_step, zero_sums, (jnp.transpose(conv_out, (1, 0, 2)), jnp.transpose(grad_branch, (1, 0, 2))))
    branch = jnp.transpose(rows_out[0], (1, 0, 2))
    grad_conv = jnp.transpose(rows_out[1], (1, 0, 2))
    updated = (mask_f * (state_f + layer_scale[:, None, None] * branch.astype(jnp.float32))).astype(jnp.bfloat16)
    padded_grad = wrap_pad(grad_conv.astype(jnp.float32))
    grad_state = (grad_out + depth_back(padded_grad, kernel, row_count, lon_cells)).astype(jnp.bfloat16)
    grad_scale = 1.0 / math.sqrt(row_count * lon_cells)
    return (updated, grad_state, sums_out[0] * grad_scale, sums_out[1] * grad_scale)
```

```python
import math

import jax
import jax.numpy as jnp
from jax import lax
from jax.experimental import pallas as pl
from jax.experimental.pallas import tpu as pltpu
from jax.sharding import PartitionSpec as P

KW = 7
RIM = KW // 2
C = 400
HID = 1600
ROWS = 64
LANES = 128
LC = 100
CP = 104
QR = 16
GROUP = 8
BF = jnp.bfloat16
F32 = jnp.float32

root_coef = math.sqrt(2.0 / math.pi)
cubic_coef = 0.044715
norm_eps = 1e-06


def dotg(a, b, ca, cb):
    return lax.dot_general(a, b, (((ca,), (cb,)), ((), ())), preferred_element_type=F32)


def ch_swap(x, k):
    return lax.ppermute(x, "ch", [(i, i ^ k) for i in range(4)])


def lon_shift(x, d):
    return lax.ppermute(x, "lon", [(i, (i + d) % 32) for i in range(32)])


def lon_swap(x, k):
    return lax.ppermute(x, "lon", [(i, i ^ k) for i in range(32)])


def share_kernel(me_ref, cot_ref, mask_ref, scale_ref, out_ref):
    cells = cot_ref[...].astype(F32)
    cells = jnp.concatenate([cells, jnp.zeros((CP - LC, QR, LANES), F32)], axis=0)
    cells = jnp.swapaxes(cells, 0, 1)
    mask = mask_ref[...].astype(F32)
    out_ref[...] = ((cells * mask[:, None, :]) * scale_ref[...][None]).astype(BF)


def branch_share(me, cotangent, sea_mask, scale, k):
    return pl.pallas_call(
        share_kernel,
        out_shape=jax.ShapeDtypeStruct((QR, CP, LANES), BF),
        grid_spec=pltpu.PrefetchScalarGridSpec(
            num_scalar_prefetch=1,
            grid=(1,),
            in_specs=[
                pl.BlockSpec((LC, QR, LANES), lambda i, me: (0, me[0] ^ k, 0)),
                pl.BlockSpec((QR, LANES), lambda i, me: (me[0] ^ k, 0)),
                pl.BlockSpec((CP, 1), lambda i, me: (0, 0)),
            ],
            out_specs=pl.BlockSpec((QR, CP, LANES), lambda i, me: (0, 0, 0)),
        ),
        compiler_params=pltpu.CompilerParams(vmem_limit_bytes=32 << 20),
        name="branch_share",
    )(me, cotangent, sea_mask, scale)


def conv_channel(cells, rim, pattern, lane, band):
    moved = []
    for off in range(-RIM, RIM + 1):
        if off == 0:
            moved.append(cells.astype(BF))
        else:
            edge = lane < off if off > 0 else lane >= LANES + off
            moved.append(pltpu.roll(jnp.where(edge, rim, cells), (-off) % LANES, 1).astype(BF))
    stacked = jnp.concatenate(moved, axis=0)
    tiles = []
    for t in range(4):
        row = jnp.broadcast_to(pattern[t : t + 1, :], (ROWS, LANES))
        row = pltpu.roll(row, 0, 1, stride=1, stride_axis=0)
        tiles.append(jnp.where(band, row, 0.0).astype(BF))
    banded = jnp.concatenate(tiles, axis=1)[:, : KW * ROWS]
    return jnp.dot(banded, stacked, preferred_element_type=F32)


def masks():
    lane = lax.broadcasted_iota(jnp.int32, (ROWS, LANES), 1)
    row = lax.broadcasted_iota(jnp.int32, (ROWS, LANES), 0)
    away = (lane & (ROWS - 1)) - row
    return lane, (away >= -RIM) & (away <= RIM)


def forward_kernel(me_ref, state_ref, rim_ref, pat_ref, bias_ref, o0, o1, o2, o3, held):
    step = pl.program_id(0)
    lane, band = masks()
    outs = []
    for c in range(GROUP):
        total = conv_channel(
            state_ref[c].astype(F32), rim_ref[c].astype(F32), pat_ref[c], lane, band
        )
        total = total + bias_ref[c]
        outs.append(jnp.where(step * GROUP + c < LC, total, 0.0))
    held[...] = jnp.swapaxes(jnp.stack(outs, 0), 0, 1).reshape(4, QR, GROUP, LANES)
    me = me_ref[0]
    for k, out in enumerate((o0, o1, o2, o3)):
        out[...] = held[me ^ k].astype(BF)


def conv_forward(me, state, rim, pattern, bias):
    share = jax.ShapeDtypeStruct((QR, CP, LANES), BF)
    return pl.pallas_call(
        forward_kernel,
        out_shape=[share] * 4,
        grid_spec=pltpu.PrefetchScalarGridSpec(
            num_scalar_prefetch=1,
            grid=(CP // GROUP,),
            in_specs=[
                pl.BlockSpec((GROUP, ROWS, LANES), lambda i, me: (i, 0, 0)),
                pl.BlockSpec((GROUP, ROWS, LANES), lambda i, me: (i, 0, 0)),
                pl.BlockSpec((GROUP, 4, LANES), lambda i, me: (i, 0, 0)),
                pl.BlockSpec((GROUP, 1, LANES), lambda i, me: (i, 0, 0)),
            ],
            out_specs=[pl.BlockSpec((QR, GROUP, LANES), lambda i, me: (0, i, 0))] * 4,
            scratch_shapes=[pltpu.VMEM((4, QR, GROUP, LANES), F32)],
        ),
        compiler_params=pltpu.CompilerParams(vmem_limit_bytes=32 << 20),
        name="conv_forward",
    )(me, state, rim, pattern, bias)


def backward_kernel(
    me_ref, g0, g1, g2, g3, r0, r1, r2, r3, pat_ref, cot_ref, mask_ref, out_ref, held, held_rim
):
    lane, band = masks()
    me = me_ref[0]
    for k, (cells, rim) in enumerate(((g0, r0), (g1, r1), (g2, r2), (g3, r3))):
        held[me ^ k] = cells[...].astype(F32)
        held_rim[me ^ k] = rim[...].astype(F32)
    cells = jnp.swapaxes(held[...].reshape(ROWS, GROUP, LANES), 0, 1)
    rims = jnp.swapaxes(held_rim[...].reshape(ROWS, GROUP, LANES), 0, 1)
    mask = mask_ref[...].astype(F32)
    for c in range(GROUP):
        total = conv_channel(cells[c], rims[c], pat_ref[c], lane, band)
        out_ref[c] = (cot_ref[c].astype(F32) * mask + total).astype(BF)


def conv_backward(me, grads, rims, pattern, cotangent, sea_mask):
    piece = pl.BlockSpec((QR, GROUP, LANES), lambda i, me: (0, i, 0))
    return pl.pallas_call(
        backward_kernel,
        out_shape=jax.ShapeDtypeStruct((LC, ROWS, LANES), BF),
        grid_spec=pltpu.PrefetchScalarGridSpec(
            num_scalar_prefetch=1,
            grid=(CP // GROUP,),
            in_specs=[piece] * 8
            + [
                pl.BlockSpec((GROUP, 4, LANES), lambda i, me: (i, 0, 0)),
                pl.BlockSpec((GROUP, ROWS, LANES), lambda i, me: (i, 0, 0)),
                pl.BlockSpec((ROWS, LANES), lambda i, me: (0, 0)),
            ],
            out_specs=pl.BlockSpec((GROUP, ROWS, LANES), lambda i, me: (i, 0, 0)),
            scratch_shapes=[pltpu.VMEM((4, QR, GROUP, LANES), F32)] * 2,
        ),
        compiler_params=pltpu.CompilerParams(vmem_limit_bytes=32 << 20),
        name="conv_backward",
    )(me, *grads, *rims, pattern, cotangent, sea_mask)


CHUNK = 4
CELLS = CHUNK * LANES
HT = 400


def mlp_kernel(*refs):
    me_ref, core_ref = refs[:2]
    xs, gs = refs[2:6], refs[6:10]
    win_t, win, wout, wout_t, vec, bias_in = refs[10:16]
    brs, gcs = refs[16:20], refs[20:24]
    wgrad = refs[24]
    x_all, g_all, act, gpre, sum_in, sum_out = refs[25:]
    step = pl.program_id(0)
    me = me_ref[0]
    for k in range(4):
        x = xs[k][...]
        g = gs[k][...]
        for r in range(CHUNK):
            x_all[me ^ k, :, r * LANES : (r + 1) * LANES] = x[r].astype(F32)
            g_all[me ^ k, :, r * LANES : (r + 1) * LANES] = g[r].astype(F32)
    gain = vec[:, 0:1]
    values = x_all[...].reshape(4 * CP, CELLS)
    mean_val = jnp.sum(values, axis=0, keepdims=True) / C
    square = jnp.sum(values * values, axis=0, keepdims=True) / C
    inv_std = lax.rsqrt(square - mean_val * mean_val + norm_eps)
    normed = ((values - mean_val) * inv_std * gain + vec[:, 1:2]).astype(BF)
    grads = g_all[...].reshape(4 * CP, CELLS).astype(BF)
    for t in range(HID // HT):
        rows = slice(t * HT, (t + 1) * HT)
        pre = jnp.dot(win_t[rows, :], normed, preferred_element_type=F32) + bias_in[rows, :]
        gact = jnp.dot(wout[rows, :], grads, preferred_element_type=F32)
        sq = pre * pre
        tangent = jnp.tanh(pre * (root_coef + (root_coef * cubic_coef) * sq))
        half = 0.5 + 0.5 * tangent
        value = pre * half
        slope = half + value * (1.0 - half) * (
            2.0 * root_coef + (6.0 * root_coef * cubic_coef) * sq
        )
        act[rows, :] = value.astype(BF)
        gpre[rows, :] = (gact * slope).astype(BF)
    branch = jnp.dot(wout_t[...], act[...], preferred_element_type=F32) + vec[:, 2:3]
    x_grad = jnp.dot(win[...], gpre[...], preferred_element_type=F32) * gain
    centred = (x_all[...].reshape(4 * CP, CELLS) - mean_val) * inv_std
    first = jnp.sum(x_grad, axis=0, keepdims=True) / C
    second = jnp.sum(x_grad * centred, axis=0, keepdims=True) / C
    x_grad = inv_std * (x_grad - first - centred * second)
    x_all[...] = x_grad.reshape(4, CP, CELLS)
    g_all[...] = branch.reshape(4, CP, CELLS)
    for k in range(4):
        for r in range(CHUNK):
            gcs[k][r] = x_all[me ^ k, :, r * LANES : (r + 1) * LANES].astype(BF)
            brs[k][r] = g_all[me ^ k, :, r * LANES : (r + 1) * LANES].astype(BF)
    part_in = dotg(gpre[...], normed, 1, 1)
    part_out = dotg(act[...], grads, 1, 1)

    @pl.when(step == 0)
    def _():
        sum_in[...] = part_in
        sum_out[...] = part_out

    @pl.when(step > 0)
    def _():
        sum_in[...] += part_in
        sum_out[...] += part_out

    @pl.when(step == pl.num_programs(0) - 1)
    def _():
        core = core_ref[0]
        wgrad[core] = sum_in[...].astype(BF)
        wgrad[1 - core] = sum_out[...].astype(BF)


def mlp(me, core, xs, gs, weights, vec, bias_in):
    piece = pl.BlockSpec((CHUNK, CP, LANES), lambda i, me, core: (i, 0, 0))

    def whole(shape):
        return pl.BlockSpec(
            shape, lambda i, me, core: (0,) * len(shape), pipeline_mode=pl.Buffered(1)
        )

    share = jax.ShapeDtypeStruct((QR, CP, LANES), BF)
    outs = pl.pallas_call(
        mlp_kernel,
        out_shape=[share] * 8 + [jax.ShapeDtypeStruct((2, HID, 4 * CP), BF)],
        grid_spec=pltpu.PrefetchScalarGridSpec(
            num_scalar_prefetch=2,
            grid=(QR // CHUNK,),
            in_specs=[piece] * 8
            + [
                whole((HID, 4 * CP)),
                whole((4 * CP, HID)),
                whole((HID, 4 * CP)),
                whole((4 * CP, HID)),
                whole((4 * CP, 3)),
                whole((HID, 1)),
            ],
            out_specs=[piece] * 8 + [whole((2, HID, 4 * CP))],
            scratch_shapes=[
                pltpu.VMEM((4, CP, CELLS), F32),
                pltpu.VMEM((4, CP, CELLS), F32),
                pltpu.VMEM((HID, CELLS), BF),
                pltpu.VMEM((HID, CELLS), BF),
                pltpu.VMEM((HID, 4 * CP), F32),
                pltpu.VMEM((HID, 4 * CP), F32),
            ],
        ),
        compiler_params=pltpu.CompilerParams(vmem_limit_bytes=56 << 20),
        name="mlp",
    )(me, core, *xs, *gs, *weights, vec, bias_in)
    return outs[:4], outs[4:8], outs[8]


def update_kernel(me_ref, b0, b1, b2, b3, state_ref, mask_ref, scale_ref, out_ref):
    k = pl.program_id(0)

    def write(piece):
        branch = piece[...].astype(F32) * scale_ref[...][None]
        branch = jnp.swapaxes(branch, 0, 1)[:LC]
        mask = mask_ref[...].astype(F32)
        out_ref[...] = (mask[None] * (state_ref[...].astype(F32) + branch)).astype(BF)

    for i, piece in enumerate((b0, b1, b2, b3)):
        pl.when(k == i)(lambda piece=piece: write(piece))


def update(me, pieces, state, sea_mask, scale):
    whole = pl.BlockSpec((QR, CP, LANES), lambda i, me: (0, 0, 0), pipeline_mode=pl.Buffered(1))
    return pl.pallas_call(
        update_kernel,
        out_shape=jax.ShapeDtypeStruct((LC, ROWS, LANES), BF),
        grid_spec=pltpu.PrefetchScalarGridSpec(
            num_scalar_prefetch=1,
            grid=(4,),
            in_specs=[whole] * 4
            + [
                pl.BlockSpec((LC, QR, LANES), lambda i, me: (0, me[0] ^ i, 0)),
                pl.BlockSpec((QR, LANES), lambda i, me: (me[0] ^ i, 0)),
                pl.BlockSpec((CP, 1), lambda i, me: (0, 0)),
            ],
            out_specs=pl.BlockSpec((LC, QR, LANES), lambda i, me: (0, me[0] ^ i, 0)),
        ),
        compiler_params=pltpu.CompilerParams(vmem_limit_bytes=32 << 20),
        name="update",
    )(me, *pieces, state, sea_mask, scale)


def tap_patterns(kernel):
    lane = jnp.arange(4 * LANES)
    tile, pos = lane // LANES, lane % LANES
    away = jnp.where(pos % ROWS < ROWS // 2, pos % ROWS, pos % ROWS - ROWS)
    side = ((pos - away) // ROWS) % 2
    col = 2 * tile + side
    tap = jnp.where((jnp.abs(away) <= RIM) & (col < KW), (away + RIM) * KW + col, -1)
    pick = (jnp.arange(KW * KW)[:, None] == tap[None, :]).astype(BF)
    return jnp.dot(kernel.astype(BF), pick, preferred_element_type=F32).reshape(LC, 4, LANES)


def edge_picks():
    row = jnp.arange(8)[:, None]
    lane = jnp.arange(LANES)[None, :]
    head = ((row < RIM) & (lane == row)).astype(BF)
    tail = ((row < RIM) & (lane == LANES - RIM + row)).astype(BF)
    return head, tail


def rims(cells2d):
    head, tail = edge_picks()
    first = dotg(head, cells2d, 1, 1).astype(BF)
    last = dotg(tail, cells2d, 1, 1).astype(BF)
    from_right = lon_shift(first, -1)
    from_left = lon_shift(last, 1)
    return dotg(
        jnp.concatenate([from_right, from_left], 0), jnp.concatenate([head, tail], 0), 0, 0
    ).astype(BF)


def reduce_gradients(wgrad, lon):
    y, z = lon & 3, (lon >> 2) & 3
    mine = wgrad[0].astype(F32) + ch_swap(wgrad[1], 1).astype(F32)
    mine = mine.reshape(4, HID // 4, 4 * CP)
    wire = mine.astype(BF)
    total = lax.dynamic_index_in_dim(mine, y, 0, False)
    for k in (1, 2, 3):
        total = total + lon_swap(
            lax.dynamic_index_in_dim(wire, y ^ k, 0, False), k
        ).astype(F32)

    def strip(a, i):
        return lax.dynamic_slice_in_dim(a, jnp.minimum(i * 104, 296), 104, 0)

    wire = total.astype(BF)
    part = strip(total, z)
    for k in (1, 2, 3):
        part = part + lon_swap(strip(wire, z ^ k), 4 * k).astype(F32)
    wire = part.astype(BF)
    part = (
        (wire.astype(F32) + lon_swap(wire, 16).astype(F32))
        + (ch_swap(wire, 2).astype(F32) + both_swap(wire).astype(F32))
    ).astype(BF)
    others = [part] + [lon_swap(part, 4 * k) for k in (1, 2, 3)]
    strips = jnp.stack(others)
    block = jnp.zeros((HID // 4, 4 * CP), BF)
    for k in range(4):
        block = lax.dynamic_update_slice_in_dim(
            block,
            lax.dynamic_index_in_dim(strips, z ^ k, 0, False),
            min(k * 104, 296),
            0,
        )
    blocks = jnp.stack([block] + [lon_swap(block, k) for k in (1, 2, 3)])
    full = jnp.concatenate([lax.dynamic_index_in_dim(blocks, y ^ k, 0, False) for k in range(4)], 0)
    return full, ch_swap(full, 1)


def both_swap(x):
    return lax.ppermute(x, ("lon", "ch"), [(i, i ^ (16 * 4 + 2)) for i in range(128)])


def body(
    ocean_state,
    sea_mask,
    kernel,
    conv_bias,
    norm_gain,
    norm_bias,
    weight_in,
    bias_in,
    weight_out,
    bias_out,
    layer_scale,
    cotangent,
):
    ch = lax.axis_index("ch")
    lon = lax.axis_index("lon")
    me = ch.reshape(1)
    core = (ch & 1).reshape(1)
    scale = jnp.pad(layer_scale, (0, CP - LC)).reshape(CP, 1)

    sent = {k: branch_share(me, cotangent, sea_mask, scale, k) for k in (2, 3, 1, 0)}
    gs = [sent[0]] + [ch_swap(sent[k], k) for k in (1, 2, 3)]

    chan = jnp.arange(C)
    pad = ((chan // LC * CP + chan % LC)[:, None] == jnp.arange(4 * CP)[None, :]).astype(BF)
    win = dotg(pad, weight_in, 0, 0).astype(BF)
    win_t = dotg(weight_in, pad, 0, 0).astype(BF)
    wout = dotg(weight_out, pad, 1, 0).astype(BF)
    wout_t = dotg(pad, weight_out, 0, 1).astype(BF)
    vec = jnp.stack([norm_gain, norm_bias, bias_out], 1).reshape(4, LC, 3)
    vec = jnp.pad(vec, ((0, 0), (0, CP - LC), (0, 0))).reshape(4 * CP, 3)

    state_rim = rims(ocean_state.reshape(LC * ROWS, LANES)).reshape(LC, ROWS, LANES)
    bias = jnp.broadcast_to(conv_bias[:, None, None], (LC, 1, LANES))
    conv = conv_forward(me, ocean_state, state_rim, tap_patterns(kernel), bias)
    xs = [conv[0]] + [ch_swap(conv[k], k) for k in (1, 2, 3)]

    branch, grad, wgrad = mlp(
        me, core, xs, gs, (win_t, win, wout, wout_t), vec, bias_in.reshape(HID, 1)
    )

    grads = [grad[0]] + [ch_swap(grad[k], k) for k in (1, 2, 3)]
    pieces = [branch[0]] + [ch_swap(branch[k], k) for k in (1, 2, 3)]

    every = jnp.concatenate(grads, 0).reshape(4 * QR * CP, LANES)
    grad_rims = rims(every).reshape(4, QR, CP, LANES)
    grad_state = conv_backward(
        me,
        grads,
        [grad_rims[k] for k in range(4)],
        tap_patterns(kernel[:, ::-1]),
        cotangent,
        sea_mask,
    )
    updated = update(me, pieces, ocean_state, sea_mask, scale)

    full, other = reduce_gradients(wgrad, lon)
    first = (ch & 1) == 0
    grad_in = jnp.where(first, full, other)
    grad_out = jnp.where(first, other, full)
    grad_scale = 1.0 / math.sqrt(ROWS * LANES * lax.axis_size("lon"))
    return (
        updated,
        grad_state,
        dotg(pad, grad_in, 1, 1) * grad_scale,
        dotg(grad_out, pad, 1, 1) * grad_scale,
    )


def solution(mesh):
    return jax.shard_map(
        body,
        mesh=mesh,
        in_specs=(
            P("ch", None, "lon"),
            P(None, "lon"),
            P("ch", None),
            P("ch"),
            P(),
            P(),
            P(),
            P(),
            P(),
            P(),
            P("ch"),
            P("ch", None, "lon"),
        ),
        out_specs=(P("ch", None, "lon"), P("ch", None, "lon"), P(), P()),
        check_vma=False,
    )
```

```python
import math

import jax
import jax.numpy as jnp
from jax import lax
from jax.experimental import pallas as pl
from jax.experimental.pallas import tpu as pltpu
from jax.sharding import PartitionSpec as P

KW = 7
RIM = KW // 2
C = 400
HID = 1600
ROWS = 64
LANES = 128
LC = 100
CP = 104
QR = 16
GROUP = 8
BF = jnp.bfloat16
F32 = jnp.float32

root_coef = math.sqrt(2.0 / math.pi)
cubic_coef = 0.044715
norm_eps = 1e-06


def dotg(a, b, ca, cb):
    return lax.dot_general(a, b, (((ca,), (cb,)), ((), ())), preferred_element_type=F32)


def cost(micros):
    return pl.CostEstimate(flops=0, bytes_accessed=int(micros * 3.3e6), transcendentals=0)


def ch_swap(x, k):
    return lax.ppermute(x, "ch", [(i, i ^ k) for i in range(4)])


def lon_shift(x, d):
    return lax.ppermute(x, "lon", [(i, (i + d) % 32) for i in range(32)])


def lon_swap(x, k):
    return lax.ppermute(x, "lon", [(i, i ^ k) for i in range(32)])


def share_kernel(me_ref, cot_ref, mask_ref, scale_ref, out_ref):
    cells = cot_ref[...].astype(F32)
    cells = jnp.concatenate([cells, jnp.zeros((CP - LC, QR, LANES), F32)], axis=0)
    cells = jnp.swapaxes(cells, 0, 1)
    mask = mask_ref[...].astype(F32)
    out_ref[...] = ((cells * mask[:, None, :]) * scale_ref[...][None]).astype(BF)


def branch_share(me, cotangent, sea_mask, scale, k):
    return pl.pallas_call(
        share_kernel,
        out_shape=jax.ShapeDtypeStruct((QR, CP, LANES), BF),
        grid_spec=pltpu.PrefetchScalarGridSpec(
            num_scalar_prefetch=1,
            grid=(1,),
            in_specs=[
                pl.BlockSpec((LC, QR, LANES), lambda i, me: (0, me[0] ^ k, 0)),
                pl.BlockSpec((QR, LANES), lambda i, me: (me[0] ^ k, 0)),
                pl.BlockSpec((CP, 1), lambda i, me: (0, 0)),
            ],
            out_specs=pl.BlockSpec((QR, CP, LANES), lambda i, me: (0, 0, 0)),
        ),
        compiler_params=pltpu.CompilerParams(vmem_limit_bytes=32 << 20),
        cost_estimate=cost(1.2),
        name="branch_share",
    )(me, cotangent, sea_mask, scale)


def conv_channel(cells, rim, pattern, lane, band):
    moved = []
    for off in range(-RIM, RIM + 1):
        if off == 0:
            moved.append(cells.astype(BF))
        else:
            edge = lane < off if off > 0 else lane >= LANES + off
            moved.append(pltpu.roll(jnp.where(edge, rim, cells), (-off) % LANES, 1).astype(BF))
    stacked = jnp.concatenate(moved, axis=0)
    tiles = []
    for t in range(4):
        row = jnp.broadcast_to(pattern[t : t + 1, :], (ROWS, LANES))
        row = pltpu.roll(row, 0, 1, stride=1, stride_axis=0)
        tiles.append(jnp.where(band, row, 0.0).astype(BF))
    banded = jnp.concatenate(tiles, axis=1)[:, : KW * ROWS]
    return jnp.dot(banded, stacked, preferred_element_type=F32)


def masks():
    lane = lax.broadcasted_iota(jnp.int32, (ROWS, LANES), 1)
    row = lax.broadcasted_iota(jnp.int32, (ROWS, LANES), 0)
    away = (lane & (ROWS - 1)) - row
    return lane, (away >= -RIM) & (away <= RIM)


def forward_kernel(me_ref, state_ref, rim_ref, pat_ref, bias_ref, o0, o1, o2, o3, held):
    step = pl.program_id(0)
    lane, band = masks()
    outs = []
    for c in range(GROUP):
        total = conv_channel(
            state_ref[c].astype(F32), rim_ref[c].astype(F32), pat_ref[c], lane, band
        )
        total = total + bias_ref[c]
        outs.append(jnp.where(step * GROUP + c < LC, total, 0.0))
    held[...] = jnp.swapaxes(jnp.stack(outs, 0), 0, 1).reshape(4, QR, GROUP, LANES)
    me = me_ref[0]
    for k, out in enumerate((o0, o1, o2, o3)):
        out[...] = held[me ^ k].astype(BF)


def conv_forward(me, state, rim, pattern, bias):
    share = jax.ShapeDtypeStruct((QR, CP, LANES), BF)
    return pl.pallas_call(
        forward_kernel,
        out_shape=[share] * 4,
        grid_spec=pltpu.PrefetchScalarGridSpec(
            num_scalar_prefetch=1,
            grid=(CP // GROUP,),
            in_specs=[
                pl.BlockSpec((GROUP, ROWS, LANES), lambda i, me: (i, 0, 0)),
                pl.BlockSpec((GROUP, ROWS, LANES), lambda i, me: (i, 0, 0)),
                pl.BlockSpec((GROUP, 4, LANES), lambda i, me: (i, 0, 0)),
                pl.BlockSpec((GROUP, 1, LANES), lambda i, me: (i, 0, 0)),
            ],
            out_specs=[pl.BlockSpec((QR, GROUP, LANES), lambda i, me: (0, i, 0))] * 4,
            scratch_shapes=[pltpu.VMEM((4, QR, GROUP, LANES), F32)],
        ),
        compiler_params=pltpu.CompilerParams(vmem_limit_bytes=32 << 20),
        cost_estimate=cost(9),
        name="conv_forward",
    )(me, state, rim, pattern, bias)


def backward_kernel(
    me_ref, g0, g1, g2, g3, r0, r1, r2, r3, pat_ref, cot_ref, mask_ref, out_ref, held, held_rim
):
    lane, band = masks()
    me = me_ref[0]
    for k, (cells, rim) in enumerate(((g0, r0), (g1, r1), (g2, r2), (g3, r3))):
        held[me ^ k] = cells[...].astype(F32)
        held_rim[me ^ k] = rim[...].astype(F32)
    cells = jnp.swapaxes(held[...].reshape(ROWS, GROUP, LANES), 0, 1)
    rims = jnp.swapaxes(held_rim[...].reshape(ROWS, GROUP, LANES), 0, 1)
    mask = mask_ref[...].astype(F32)
    for c in range(GROUP):
        total = conv_channel(cells[c], rims[c], pat_ref[c], lane, band)
        out_ref[c] = (cot_ref[c].astype(F32) * mask + total).astype(BF)


def conv_backward(me, grads, rims, pattern, cotangent, sea_mask):
    piece = pl.BlockSpec((QR, GROUP, LANES), lambda i, me: (0, i, 0))
    return pl.pallas_call(
        backward_kernel,
        out_shape=jax.ShapeDtypeStruct((LC, ROWS, LANES), BF),
        grid_spec=pltpu.PrefetchScalarGridSpec(
            num_scalar_prefetch=1,
            grid=(CP // GROUP,),
            in_specs=[piece] * 8
            + [
                pl.BlockSpec((GROUP, 4, LANES), lambda i, me: (i, 0, 0)),
                pl.BlockSpec((GROUP, ROWS, LANES), lambda i, me: (i, 0, 0)),
                pl.BlockSpec((ROWS, LANES), lambda i, me: (0, 0)),
            ],
            out_specs=pl.BlockSpec((GROUP, ROWS, LANES), lambda i, me: (i, 0, 0)),
            scratch_shapes=[pltpu.VMEM((4, QR, GROUP, LANES), F32)] * 2,
        ),
        compiler_params=pltpu.CompilerParams(vmem_limit_bytes=32 << 20),
        cost_estimate=cost(10),
        name="conv_backward",
    )(me, *grads, *rims, pattern, cotangent, sea_mask)


CHUNK = 8
CELLS = CHUNK * LANES
HT = 400
PIECE = 328
WIRE = 16 * PIECE


def mlp_kernel(*refs):
    me_ref, core_ref = refs[:2]
    xs, gs = refs[2:6], refs[6:10]
    win_t, win, wout, wout_t, vec, bias_in = refs[10:16]
    brs, gcs = refs[16:20], refs[20:24]
    keep, send = refs[24:26]
    x_all, g_all, act, gpre, sums = refs[26:]
    step = pl.program_id(0)
    me = me_ref[0]
    for k in range(4):
        x = xs[k][...]
        g = gs[k][...]
        for r in range(CHUNK):
            x_all[me ^ k, :, r * LANES : (r + 1) * LANES] = x[r].astype(F32)
            g_all[me ^ k, :, r * LANES : (r + 1) * LANES] = g[r].astype(F32)
    gain = vec[:, 0:1]
    values = x_all[...].reshape(4 * CP, CELLS)
    mean_val = jnp.sum(values, axis=0, keepdims=True) / C
    square = jnp.sum(values * values, axis=0, keepdims=True) / C
    inv_std = lax.rsqrt(square - mean_val * mean_val + norm_eps)
    normed = ((values - mean_val) * inv_std * gain + vec[:, 1:2]).astype(BF)
    grads = g_all[...].reshape(4 * CP, CELLS).astype(BF)
    for t in range(HID // HT):
        rows = slice(t * HT, (t + 1) * HT)
        pre = jnp.dot(win_t[rows, :], normed, preferred_element_type=F32) + bias_in[rows, :]
        gact = jnp.dot(wout[rows, :], grads, preferred_element_type=F32)
        sq = pre * pre
        tangent = jnp.tanh(pre * (root_coef + (root_coef * cubic_coef) * sq))
        half = 0.5 + 0.5 * tangent
        value = pre * half
        slope = half + value * (1.0 - half) * (
            2.0 * root_coef + (6.0 * root_coef * cubic_coef) * sq
        )
        act[rows, :] = value.astype(BF)
        gpre[rows, :] = (gact * slope).astype(BF)
    branch = jnp.dot(wout_t[...], act[...], preferred_element_type=F32) + vec[:, 2:3]
    x_grad = jnp.dot(win[...], gpre[...], preferred_element_type=F32) * gain
    centred = (x_all[...].reshape(4 * CP, CELLS) - mean_val) * inv_std
    first = jnp.sum(x_grad, axis=0, keepdims=True) / C
    second = jnp.sum(x_grad * centred, axis=0, keepdims=True) / C
    x_grad = inv_std * (x_grad - first - centred * second)
    x_all[...] = x_grad.reshape(4, CP, CELLS)
    g_all[...] = branch.reshape(4, CP, CELLS)
    for k in range(4):
        for r in range(CHUNK):
            gcs[k][r] = x_all[me ^ k, :, r * LANES : (r + 1) * LANES].astype(BF)
            brs[k][r] = g_all[me ^ k, :, r * LANES : (r + 1) * LANES].astype(BF)
    part_in = dotg(gpre[...], normed, 1, 1)
    part_out = dotg(act[...], grads, 1, 1)

    @pl.when(step == 0)
    def _():
        sums[0] = part_in
        sums[1] = part_out

    @pl.when(step > 0)
    def _():
        sums[0] += part_in
        sums[1] += part_out

    @pl.when(step == pl.num_programs(0) - 1)
    def _():
        core = core_ref[0]
        for out, slot in ((keep, core), (send, 1 - core)):
            for t in range(3):
                out[t * HID : (t + 1) * HID, :] = sums[slot, :, t * LANES : (t + 1) * LANES].astype(BF)
            rest = [
                sums[slot, q * 400 : (q + 1) * 400, 3 * LANES : 4 * CP] for q in range(4)
            ]
            out[3 * HID : 3 * HID + 400, :] = jnp.concatenate(rest, axis=1).astype(BF)
            out[3 * HID + 400 :, :] = jnp.zeros((WIRE - 3 * HID - 400, LANES), BF)


def mlp(me, core, xs, gs, weights, vec, bias_in):
    piece = pl.BlockSpec((CHUNK, CP, LANES), lambda i, me, core: (i, 0, 0))

    def whole(shape):
        return pl.BlockSpec(
            shape, lambda i, me, core: (0,) * len(shape), pipeline_mode=pl.Buffered(1)
        )

    share = jax.ShapeDtypeStruct((QR, CP, LANES), BF)
    outs = pl.pallas_call(
        mlp_kernel,
        out_shape=[share] * 8 + [jax.ShapeDtypeStruct((WIRE, LANES), BF)] * 2,
        grid_spec=pltpu.PrefetchScalarGridSpec(
            num_scalar_prefetch=2,
            grid=(QR // CHUNK,),
            in_specs=[piece] * 8
            + [
                whole((HID, 4 * CP)),
                whole((4 * CP, HID)),
                whole((HID, 4 * CP)),
                whole((4 * CP, HID)),
                whole((4 * CP, 3)),
                whole((HID, 1)),
            ],
            out_specs=[piece] * 8 + [whole((WIRE, LANES))] * 2,
            scratch_shapes=[
                pltpu.VMEM((4, CP, CELLS), F32),
                pltpu.VMEM((4, CP, CELLS), F32),
                pltpu.VMEM((HID, CELLS), BF),
                pltpu.VMEM((HID, CELLS), BF),
                pltpu.VMEM((2, HID, 4 * CP), F32),
            ],
        ),
        compiler_params=pltpu.CompilerParams(vmem_limit_bytes=56 << 20),
        cost_estimate=cost(34),
        name="mlp",
    )(me, core, *xs, *gs, *weights, vec, bias_in)
    return outs[:4], outs[4:8], outs[8], outs[9]


def update_kernel(me_ref, b0, b1, b2, b3, state_ref, mask_ref, scale_ref, out_ref):
    k = pl.program_id(0)

    def write(piece):
        branch = piece[...].astype(F32) * scale_ref[...][None]
        branch = jnp.swapaxes(branch, 0, 1)[:LC]
        mask = mask_ref[...].astype(F32)
        out_ref[...] = (mask[None] * (state_ref[...].astype(F32) + branch)).astype(BF)

    for i, piece in enumerate((b0, b1, b2, b3)):
        pl.when(k == i)(lambda piece=piece: write(piece))


def update(me, pieces, state, sea_mask, scale):
    whole = pl.BlockSpec((QR, CP, LANES), lambda i, me: (0, 0, 0), pipeline_mode=pl.Buffered(1))
    return pl.pallas_call(
        update_kernel,
        out_shape=jax.ShapeDtypeStruct((LC, ROWS, LANES), BF),
        grid_spec=pltpu.PrefetchScalarGridSpec(
            num_scalar_prefetch=1,
            grid=(4,),
            in_specs=[whole] * 4
            + [
                pl.BlockSpec((LC, QR, LANES), lambda i, me: (0, me[0] ^ i, 0)),
                pl.BlockSpec((QR, LANES), lambda i, me: (me[0] ^ i, 0)),
                pl.BlockSpec((CP, 1), lambda i, me: (0, 0)),
            ],
            out_specs=pl.BlockSpec((LC, QR, LANES), lambda i, me: (0, me[0] ^ i, 0)),
        ),
        compiler_params=pltpu.CompilerParams(vmem_limit_bytes=32 << 20),
        cost_estimate=cost(4.4),
        name="update",
    )(me, *pieces, state, sea_mask, scale)


def weights_kernel(one, two, pad, one_out, one_t, two_out, two_t):
    for source, out, turned in ((one, one_out, one_t), (two, two_out, two_t)):
        padded = dotg(pad[...], source[...], 0, 0)
        out[...] = padded.astype(BF)
        turned[...] = padded.T.astype(BF)


def padded_weights(one, two, pad):
    vmem = pl.BlockSpec(memory_space=pltpu.VMEM)
    flat = jax.ShapeDtypeStruct((4 * CP, HID), BF)
    turned = jax.ShapeDtypeStruct((HID, 4 * CP), BF)
    return pl.pallas_call(
        weights_kernel,
        out_shape=[flat, turned, flat, turned],
        in_specs=[vmem] * 3,
        out_specs=[vmem] * 4,
        compiler_params=pltpu.CompilerParams(vmem_limit_bytes=48 << 20),
        cost_estimate=cost(5),
        name="padded_weights",
    )(one, two, pad)


def tap_patterns(kernel):
    lane = jnp.arange(4 * LANES)
    tile, pos = lane // LANES, lane % LANES
    away = jnp.where(pos % ROWS < ROWS // 2, pos % ROWS, pos % ROWS - ROWS)
    side = ((pos - away) // ROWS) % 2
    col = 2 * tile + side
    tap = jnp.where((jnp.abs(away) <= RIM) & (col < KW), (away + RIM) * KW + col, -1)
    pick = (jnp.arange(KW * KW)[:, None] == tap[None, :]).astype(BF)
    return jnp.dot(kernel.astype(BF), pick, preferred_element_type=F32).reshape(LC, 4, LANES)


def edge_picks():
    row = jnp.arange(8)[:, None]
    lane = jnp.arange(LANES)[None, :]
    head = ((row < RIM) & (lane == row)).astype(BF)
    tail = ((row < RIM) & (lane == LANES - RIM + row)).astype(BF)
    return head, tail


def edges_kernel(cells, pick, *refs):
    both = dotg(pick[...], cells[...], 1, 1)
    refs[-2][...] = both[:8].astype(BF)
    refs[-1][...] = both[8:].astype(BF)


def edges(cells2d, picks, after=()):
    vmem = pl.BlockSpec(memory_space=pltpu.VMEM)
    out = jax.ShapeDtypeStruct((8, cells2d.shape[0]), BF)
    return pl.pallas_call(
        edges_kernel,
        out_shape=[out, out],
        in_specs=[vmem, vmem] + [pl.BlockSpec(memory_space=pl.ANY)] * len(after),
        out_specs=[vmem, vmem],
        compiler_params=pltpu.CompilerParams(vmem_limit_bytes=32 << 20),
        cost_estimate=cost(1.5),
        name="edges",
    )(cells2d, picks, *after)


def rims(cells2d, after=()):
    picks = jnp.concatenate(edge_picks(), 0)
    first, last = edges(cells2d, picks, after)
    from_right = lon_shift(first, -1)
    from_left = lon_shift(last, 1)
    both = [from_right, from_left]
    return dotg(jnp.concatenate(both, 0), picks, 0, 0).astype(BF), both


PLANES = [[16 * half + i for i in range(16)] for half in range(2)]


def plane_exchange(pieces):
    return lax.all_to_all(pieces, "lon", 0, 0, axis_index_groups=PLANES)


def total_kernel(*refs):
    total = refs[0][0].astype(F32)
    for i in range(1, 16):
        total = total + refs[0][i].astype(F32)
    refs[-1][...] = total.astype(BF)


def plane_total(pieces, after):
    vmem = pl.BlockSpec(memory_space=pltpu.VMEM)
    return pl.pallas_call(
        total_kernel,
        out_shape=jax.ShapeDtypeStruct((PIECE, LANES), BF),
        in_specs=[vmem] + [pl.BlockSpec(memory_space=pl.ANY)] * len(after),
        out_specs=vmem,
        cost_estimate=cost(1.2),
        name="plane_total",
    )(pieces, *after)


def copies_kernel(*refs):
    for i in range(16):
        refs[-1][i] = refs[0][...]


def plane_copies(part, after):
    vmem = pl.BlockSpec(memory_space=pltpu.VMEM)
    return pl.pallas_call(
        copies_kernel,
        out_shape=jax.ShapeDtypeStruct((16, PIECE, LANES), BF),
        in_specs=[vmem] + [pl.BlockSpec(memory_space=pl.ANY)] * len(after),
        out_specs=vmem,
        cost_estimate=cost(1),
        name="plane_copies",
    )(part, *after)


def reduce_gradients(keep, send, early, late):
    mine = keep.astype(F32) + ch_swap(send, 1).astype(F32)
    mine = plane_exchange(mine.astype(BF).reshape(16, PIECE, LANES))
    wire = plane_total(mine, early)
    part = (
        (wire.astype(F32) + lon_swap(wire, 16).astype(F32))
        + (ch_swap(wire, 2).astype(F32) + both_swap(wire).astype(F32))
    ).astype(BF)
    return plane_exchange(plane_copies(part, late)).reshape(WIRE, LANES)


def finish_kernel(core_ref, own, other, pad, grad_in, grad_out, held):
    core = core_ref[0]
    for wire, slot in ((own, core), (other, 1 - core)):
        for t in range(3):
            held[slot, :, t * LANES : (t + 1) * LANES] = wire[t * HID : (t + 1) * HID, :]
        rest = wire[3 * HID : 3 * HID + 400, :]
        for q in range(4):
            held[slot, q * 400 : (q + 1) * 400, 3 * LANES :] = rest[:, q * 32 : (q + 1) * 32]
    factor = 1.0 / math.sqrt(ROWS * LANES * 32)
    grad_in[...] = dotg(pad[...], held[0], 1, 1) * factor
    grad_out[...] = dotg(pad[...], held[1], 1, 1) * factor


def finish(core, own, other, pad):
    vmem = pl.BlockSpec(memory_space=pltpu.VMEM)
    return pl.pallas_call(
        finish_kernel,
        out_shape=[
            jax.ShapeDtypeStruct((C, HID), F32),
            jax.ShapeDtypeStruct((C, HID), F32),
        ],
        in_specs=[pl.BlockSpec(memory_space=pltpu.SMEM)] + [vmem] * 3,
        out_specs=[vmem] * 2,
        scratch_shapes=[pltpu.VMEM((2, HID, 4 * CP), BF)],
        compiler_params=pltpu.CompilerParams(vmem_limit_bytes=32 << 20),
        cost_estimate=cost(6),
        name="finish",
    )(core, own, other, pad)


def both_swap(x):
    return lax.ppermute(x, ("lon", "ch"), [(i, i ^ (16 * 4 + 2)) for i in range(128)])


def body(
    ocean_state,
    sea_mask,
    kernel,
    conv_bias,
    norm_gain,
    norm_bias,
    weight_in,
    bias_in,
    weight_out,
    bias_out,
    layer_scale,
    cotangent,
):
    ch = lax.axis_index("ch")
    me = ch.reshape(1)
    core = (ch & 1).reshape(1)
    scale = jnp.pad(layer_scale, (0, CP - LC)).reshape(CP, 1)

    sent = {k: branch_share(me, cotangent, sea_mask, scale, k) for k in (2, 3, 1, 0)}
    gs = [sent[0]] + [ch_swap(sent[k], k) for k in (1, 2, 3)]

    chan = jnp.arange(C)
    pad = ((chan // LC * CP + chan % LC)[:, None] == jnp.arange(4 * CP)[None, :]).astype(BF)
    win, win_t, wout_t, wout = padded_weights(weight_in, weight_out.T, pad)
    vec = jnp.stack([norm_gain, norm_bias, bias_out], 1).reshape(4, LC, 3)
    vec = jnp.pad(vec, ((0, 0), (0, CP - LC), (0, 0))).reshape(4 * CP, 3)

    state_rim, _ = rims(ocean_state.reshape(LC * ROWS, LANES), (sent[2], sent[3]))
    state_rim = state_rim.reshape(LC, ROWS, LANES)
    bias = jnp.broadcast_to(conv_bias[:, None, None], (LC, 1, LANES))
    conv = conv_forward(me, ocean_state, state_rim, tap_patterns(kernel), bias)
    xs = [conv[0]] + [ch_swap(conv[k], k) for k in (1, 2, 3)]

    branch, grad, keep, send = mlp(
        me, core, xs, gs, (win_t, win, wout, wout_t), vec, bias_in.reshape(HID, 1)
    )

    grads = [grad[0]] + [ch_swap(grad[k], k) for k in (1, 2, 3)]
    pieces = [branch[0]] + [ch_swap(branch[k], k) for k in (1, 2, 3)]

    every = jnp.concatenate(grads, 0).reshape(4 * QR * CP, LANES)
    grad_rims, arrived = rims(every)
    grad_rims = grad_rims.reshape(4, QR, CP, LANES)
    own = reduce_gradients(keep, send, arrived, pieces)

    grad_state = conv_backward(
        me,
        grads,
        [grad_rims[k] for k in range(4)],
        tap_patterns(kernel[:, ::-1]),
        cotangent,
        sea_mask,
    )
    updated = update(me, pieces, ocean_state, sea_mask, scale)

    own, grad_state, updated = lax.optimization_barrier((own, grad_state, updated))
    grad_in, grad_out = finish(core, own, ch_swap(own, 1), pad)
    return updated, grad_state, grad_in, grad_out.T


def solution(mesh):
    return jax.shard_map(
        body,
        mesh=mesh,
        in_specs=(
            P("ch", None, "lon"),
            P(None, "lon"),
            P("ch", None),
            P("ch"),
            P(),
            P(),
            P(),
            P(),
            P(),
            P(),
            P("ch"),
            P("ch", None, "lon"),
        ),
        out_specs=(P("ch", None, "lon"), P("ch", None, "lon"), P(), P()),
        check_vma=False,
    )
```

```python
import math

import jax
import jax.numpy as jnp
from jax import lax
from jax.experimental import pallas as pl
from jax.experimental.pallas import tpu as pltpu
from jax.sharding import PartitionSpec as P

KW = 7
RIM = KW // 2
C = 400
HID = 1600
ROWS = 64
LANES = 128
LC = 100
CP = 104
QR = 16
GROUP = 8
BF = jnp.bfloat16
F32 = jnp.float32

root_coef = math.sqrt(2.0 / math.pi)
cubic_coef = 0.044715
norm_eps = 1e-06


def dotg(a, b, ca, cb):
    return lax.dot_general(a, b, (((ca,), (cb,)), ((), ())), preferred_element_type=F32)


def cost(micros):
    return pl.CostEstimate(flops=0, bytes_accessed=int(micros * 3.3e6), transcendentals=0)


def ch_swap(x, k):
    return lax.ppermute(x, "ch", [(i, i ^ k) for i in range(4)])


def lon_shift(x, d):
    return lax.ppermute(x, "lon", [(i, (i + d) % 32) for i in range(32)])


def lon_swap(x, k):
    return lax.ppermute(x, "lon", [(i, i ^ k) for i in range(32)])


def share_kernel(me_ref, cot_ref, mask_ref, scale_ref, *refs):
    out_ref = refs[-1]
    cells = cot_ref[...].astype(F32)
    cells = jnp.concatenate([cells, jnp.zeros((CP - LC, QR, LANES), F32)], axis=0)
    cells = jnp.swapaxes(cells, 0, 1)
    mask = mask_ref[...].astype(F32)
    out_ref[...] = ((cells * mask[:, None, :]) * scale_ref[...][None]).astype(BF)


def branch_share(me, cotangent, sea_mask, scale, k, after):
    return pl.pallas_call(
        share_kernel,
        out_shape=jax.ShapeDtypeStruct((QR, CP, LANES), BF),
        grid_spec=pltpu.PrefetchScalarGridSpec(
            num_scalar_prefetch=1,
            grid=(1,),
            in_specs=[
                pl.BlockSpec((LC, QR, LANES), lambda i, me: (0, me[0] ^ k, 0)),
                pl.BlockSpec((QR, LANES), lambda i, me: (me[0] ^ k, 0)),
                pl.BlockSpec((CP, 1), lambda i, me: (0, 0)),
            ]
            + [pl.BlockSpec(memory_space=pl.ANY)] * len(after),
            out_specs=pl.BlockSpec((QR, CP, LANES), lambda i, me: (0, 0, 0)),
        ),
        compiler_params=pltpu.CompilerParams(vmem_limit_bytes=32 << 20),
        cost_estimate=cost(1.2),
        name="branch_share",
    )(me, cotangent, sea_mask, scale, *after)


def conv_channel(cells, rim, pattern, lane, band):
    moved = []
    for off in range(-RIM, RIM + 1):
        if off == 0:
            moved.append(cells.astype(BF))
        else:
            edge = lane < off if off > 0 else lane >= LANES + off
            moved.append(pltpu.roll(jnp.where(edge, rim, cells), (-off) % LANES, 1).astype(BF))
    stacked = jnp.concatenate(moved, axis=0)
    tiles = []
    for t in range(4):
        row = jnp.broadcast_to(pattern[t : t + 1, :], (ROWS, LANES))
        row = pltpu.roll(row, 0, 1, stride=1, stride_axis=0)
        tiles.append(jnp.where(band, row, 0.0).astype(BF))
    banded = jnp.concatenate(tiles, axis=1)[:, : KW * ROWS]
    return jnp.dot(banded, stacked, preferred_element_type=F32)


def masks():
    lane = lax.broadcasted_iota(jnp.int32, (ROWS, LANES), 1)
    row = lax.broadcasted_iota(jnp.int32, (ROWS, LANES), 0)
    away = (lane & (ROWS - 1)) - row
    return lane, (away >= -RIM) & (away <= RIM)


def forward_kernel(me_ref, state_ref, rim_ref, pat_ref, bias_ref, o0, o1, o2, o3, held):
    step = pl.program_id(0)
    lane, band = masks()
    outs = []
    for c in range(GROUP):
        total = conv_channel(
            state_ref[c].astype(F32), rim_ref[c].astype(F32), pat_ref[c], lane, band
        )
        total = total + bias_ref[c]
        outs.append(jnp.where(step * GROUP + c < LC, total, 0.0))
    held[...] = jnp.swapaxes(jnp.stack(outs, 0), 0, 1).reshape(4, QR, GROUP, LANES)
    me = me_ref[0]
    for k, out in enumerate((o0, o1, o2, o3)):
        out[...] = held[me ^ k].astype(BF)


def conv_forward(me, state, rim, pattern, bias):
    share = jax.ShapeDtypeStruct((QR, CP, LANES), BF)
    return pl.pallas_call(
        forward_kernel,
        out_shape=[share] * 4,
        grid_spec=pltpu.PrefetchScalarGridSpec(
            num_scalar_prefetch=1,
            grid=(CP // GROUP,),
            in_specs=[
                pl.BlockSpec((GROUP, ROWS, LANES), lambda i, me: (i, 0, 0)),
                pl.BlockSpec((GROUP, ROWS, LANES), lambda i, me: (i, 0, 0)),
                pl.BlockSpec((GROUP, 4, LANES), lambda i, me: (i, 0, 0)),
                pl.BlockSpec((GROUP, 1, LANES), lambda i, me: (i, 0, 0)),
            ],
            out_specs=[pl.BlockSpec((QR, GROUP, LANES), lambda i, me: (0, i, 0))] * 4,
            scratch_shapes=[pltpu.VMEM((4, QR, GROUP, LANES), F32)],
        ),
        compiler_params=pltpu.CompilerParams(vmem_limit_bytes=32 << 20),
        cost_estimate=cost(9),
        name="conv_forward",
    )(me, state, rim, pattern, bias)


def backward_kernel(
    me_ref, g0, g1, g2, g3, r0, r1, r2, r3, pat_ref, cot_ref, mask_ref, out_ref, held, held_rim
):
    lane, band = masks()
    me = me_ref[0]
    for k, (cells, rim) in enumerate(((g0, r0), (g1, r1), (g2, r2), (g3, r3))):
        held[me ^ k] = cells[...].astype(F32)
        held_rim[me ^ k] = rim[...].astype(F32)
    cells = jnp.swapaxes(held[...].reshape(ROWS, GROUP, LANES), 0, 1)
    rims = jnp.swapaxes(held_rim[...].reshape(ROWS, GROUP, LANES), 0, 1)
    mask = mask_ref[...].astype(F32)
    for c in range(GROUP):
        total = conv_channel(cells[c], rims[c], pat_ref[c], lane, band)
        out_ref[c] = (cot_ref[c].astype(F32) * mask + total).astype(BF)


def conv_backward(me, grads, rims, pattern, cotangent, sea_mask):
    piece = pl.BlockSpec((QR, GROUP, LANES), lambda i, me: (0, i, 0))
    return pl.pallas_call(
        backward_kernel,
        out_shape=jax.ShapeDtypeStruct((LC, ROWS, LANES), BF),
        grid_spec=pltpu.PrefetchScalarGridSpec(
            num_scalar_prefetch=1,
            grid=(CP // GROUP,),
            in_specs=[piece] * 8
            + [
                pl.BlockSpec((GROUP, 4, LANES), lambda i, me: (i, 0, 0)),
                pl.BlockSpec((GROUP, ROWS, LANES), lambda i, me: (i, 0, 0)),
                pl.BlockSpec((ROWS, LANES), lambda i, me: (0, 0)),
            ],
            out_specs=pl.BlockSpec((GROUP, ROWS, LANES), lambda i, me: (i, 0, 0)),
            scratch_shapes=[pltpu.VMEM((4, QR, GROUP, LANES), F32)] * 2,
        ),
        compiler_params=pltpu.CompilerParams(vmem_limit_bytes=32 << 20),
        cost_estimate=cost(10),
        name="conv_backward",
    )(me, *grads, *rims, pattern, cotangent, sea_mask)


CHUNK = 8
CELLS = CHUNK * LANES
HT = 400
PIECE = 328
WIRE = 16 * PIECE


def mlp_kernel(*refs):
    me_ref, core_ref = refs[:2]
    xs, gs = refs[2:6], refs[6:10]
    win_t, win, wout, wout_t, vec, bias_in = refs[10:16]
    brs, gcs = refs[16:20], refs[20:24]
    keep, send = refs[24:26]
    x_all, g_all, act, gpre, sums = refs[26:]
    step = pl.program_id(0)
    me = me_ref[0]
    for k in range(4):
        x = xs[k][...]
        g = gs[k][...]
        for r in range(CHUNK):
            x_all[me ^ k, :, r * LANES : (r + 1) * LANES] = x[r].astype(F32)
            g_all[me ^ k, :, r * LANES : (r + 1) * LANES] = g[r].astype(F32)
    gain = vec[:, 0:1]
    values = x_all[...].reshape(4 * CP, CELLS)
    mean_val = jnp.sum(values, axis=0, keepdims=True) / C
    square = jnp.sum(values * values, axis=0, keepdims=True) / C
    inv_std = lax.rsqrt(square - mean_val * mean_val + norm_eps)
    normed = ((values - mean_val) * inv_std * gain + vec[:, 1:2]).astype(BF)
    grads = g_all[...].reshape(4 * CP, CELLS).astype(BF)
    for t in range(HID // HT):
        rows = slice(t * HT, (t + 1) * HT)
        pre = jnp.dot(win_t[rows, :], normed, preferred_element_type=F32) + bias_in[rows, :]
        gact = jnp.dot(wout[rows, :], grads, preferred_element_type=F32)
        sq = pre * pre
        tangent = jnp.tanh(pre * (root_coef + (root_coef * cubic_coef) * sq))
        half = 0.5 + 0.5 * tangent
        value = pre * half
        slope = half + value * (1.0 - half) * (
            2.0 * root_coef + (6.0 * root_coef * cubic_coef) * sq
        )
        act[rows, :] = value.astype(BF)
        gpre[rows, :] = (gact * slope).astype(BF)
    branch = jnp.dot(wout_t[...], act[...], preferred_element_type=F32) + vec[:, 2:3]
    x_grad = jnp.dot(win[...], gpre[...], preferred_element_type=F32) * gain
    centred = (x_all[...].reshape(4 * CP, CELLS) - mean_val) * inv_std
    first = jnp.sum(x_grad, axis=0, keepdims=True) / C
    second = jnp.sum(x_grad * centred, axis=0, keepdims=True) / C
    x_grad = inv_std * (x_grad - first - centred * second)
    x_all[...] = x_grad.reshape(4, CP, CELLS)
    g_all[...] = branch.reshape(4, CP, CELLS)
    for k in range(4):
        for r in range(CHUNK):
            gcs[k][r] = x_all[me ^ k, :, r * LANES : (r + 1) * LANES].astype(BF)
            brs[k][r] = g_all[me ^ k, :, r * LANES : (r + 1) * LANES].astype(BF)
    part_in = dotg(gpre[...], normed, 1, 1)
    part_out = dotg(act[...], grads, 1, 1)

    @pl.when(step == 0)
    def _():
        sums[0] = part_in
        sums[1] = part_out

    @pl.when(step > 0)
    def _():
        sums[0] += part_in
        sums[1] += part_out

    @pl.when(step == pl.num_programs(0) - 1)
    def _():
        core = core_ref[0]
        for out, slot in ((keep, core), (send, 1 - core)):
            for t in range(3):
                out[t * HID : (t + 1) * HID, :] = sums[slot, :, t * LANES : (t + 1) * LANES].astype(BF)
            rest = [
                sums[slot, q * 400 : (q + 1) * 400, 3 * LANES : 4 * CP] for q in range(4)
            ]
            out[3 * HID : 3 * HID + 400, :] = jnp.concatenate(rest, axis=1).astype(BF)
            out[3 * HID + 400 :, :] = jnp.zeros((WIRE - 3 * HID - 400, LANES), BF)


def mlp(me, core, xs, gs, weights, vec, bias_in):
    piece = pl.BlockSpec((CHUNK, CP, LANES), lambda i, me, core: (i, 0, 0))

    def whole(shape):
        return pl.BlockSpec(
            shape, lambda i, me, core: (0,) * len(shape), pipeline_mode=pl.Buffered(1)
        )

    share = jax.ShapeDtypeStruct((QR, CP, LANES), BF)
    outs = pl.pallas_call(
        mlp_kernel,
        out_shape=[share] * 8 + [jax.ShapeDtypeStruct((WIRE, LANES), BF)] * 2,
        grid_spec=pltpu.PrefetchScalarGridSpec(
            num_scalar_prefetch=2,
            grid=(QR // CHUNK,),
            in_specs=[piece] * 8
            + [
                whole((HID, 4 * CP)),
                whole((4 * CP, HID)),
                whole((HID, 4 * CP)),
                whole((4 * CP, HID)),
                whole((4 * CP, 3)),
                whole((HID, 1)),
            ],
            out_specs=[piece] * 8 + [whole((WIRE, LANES))] * 2,
            scratch_shapes=[
                pltpu.VMEM((4, CP, CELLS), F32),
                pltpu.VMEM((4, CP, CELLS), F32),
                pltpu.VMEM((HID, CELLS), BF),
                pltpu.VMEM((HID, CELLS), BF),
                pltpu.VMEM((2, HID, 4 * CP), F32),
            ],
        ),
        compiler_params=pltpu.CompilerParams(vmem_limit_bytes=56 << 20),
        cost_estimate=cost(34),
        name="mlp",
    )(me, core, *xs, *gs, *weights, vec, bias_in)
    return outs[:4], outs[4:8], outs[8], outs[9]


def update_kernel(me_ref, b0, b1, b2, b3, state_ref, mask_ref, scale_ref, out_ref):
    k = pl.program_id(0)

    def write(piece):
        branch = piece[...].astype(F32) * scale_ref[...][None]
        branch = jnp.swapaxes(branch, 0, 1)[:LC]
        mask = mask_ref[...].astype(F32)
        out_ref[...] = (mask[None] * (state_ref[...].astype(F32) + branch)).astype(BF)

    for i, piece in enumerate((b0, b1, b2, b3)):
        pl.when(k == i)(lambda piece=piece: write(piece))


def update(me, pieces, state, sea_mask, scale):
    whole = pl.BlockSpec((QR, CP, LANES), lambda i, me: (0, 0, 0), pipeline_mode=pl.Buffered(1))
    return pl.pallas_call(
        update_kernel,
        out_shape=jax.ShapeDtypeStruct((LC, ROWS, LANES), BF),
        grid_spec=pltpu.PrefetchScalarGridSpec(
            num_scalar_prefetch=1,
            grid=(4,),
            in_specs=[whole] * 4
            + [
                pl.BlockSpec((LC, QR, LANES), lambda i, me: (0, me[0] ^ i, 0)),
                pl.BlockSpec((QR, LANES), lambda i, me: (me[0] ^ i, 0)),
                pl.BlockSpec((CP, 1), lambda i, me: (0, 0)),
            ],
            out_specs=pl.BlockSpec((LC, QR, LANES), lambda i, me: (0, me[0] ^ i, 0)),
        ),
        compiler_params=pltpu.CompilerParams(vmem_limit_bytes=32 << 20),
        cost_estimate=cost(4.4),
        name="update",
    )(me, *pieces, state, sea_mask, scale)


def weights_kernel(one, two, pad, one_out, one_t, two_out, two_t):
    for source, out, turned in ((one, one_out, one_t), (two, two_out, two_t)):
        padded = dotg(pad[...], source[...], 0, 0)
        out[...] = padded.astype(BF)
        turned[...] = padded.T.astype(BF)


def padded_weights(one, two, pad):
    vmem = pl.BlockSpec(memory_space=pltpu.VMEM)
    flat = jax.ShapeDtypeStruct((4 * CP, HID), BF)
    turned = jax.ShapeDtypeStruct((HID, 4 * CP), BF)
    return pl.pallas_call(
        weights_kernel,
        out_shape=[flat, turned, flat, turned],
        in_specs=[vmem] * 3,
        out_specs=[vmem] * 4,
        compiler_params=pltpu.CompilerParams(vmem_limit_bytes=48 << 20),
        cost_estimate=cost(5),
        name="padded_weights",
    )(one, two, pad)


def tap_patterns(kernel):
    lane = jnp.arange(4 * LANES)
    tile, pos = lane // LANES, lane % LANES
    away = jnp.where(pos % ROWS < ROWS // 2, pos % ROWS, pos % ROWS - ROWS)
    side = ((pos - away) // ROWS) % 2
    col = 2 * tile + side
    tap = jnp.where((jnp.abs(away) <= RIM) & (col < KW), (away + RIM) * KW + col, -1)
    pick = (jnp.arange(KW * KW)[:, None] == tap[None, :]).astype(BF)
    return jnp.dot(kernel.astype(BF), pick, preferred_element_type=F32).reshape(LC, 4, LANES)


def edge_picks():
    row = jnp.arange(8)[:, None]
    lane = jnp.arange(LANES)[None, :]
    head = ((row < RIM) & (lane == row)).astype(BF)
    tail = ((row < RIM) & (lane == LANES - RIM + row)).astype(BF)
    return head, tail


def edge_kernel(cells, pick, *refs):
    refs[-1][...] = dotg(pick[...], cells[...], 1, 1).astype(BF)


def edge(cells2d, pick, after=()):
    vmem = pl.BlockSpec(memory_space=pltpu.VMEM)
    return pl.pallas_call(
        edge_kernel,
        out_shape=jax.ShapeDtypeStruct((8, cells2d.shape[0]), BF),
        in_specs=[vmem, vmem] + [pl.BlockSpec(memory_space=pl.ANY)] * len(after),
        out_specs=vmem,
        compiler_params=pltpu.CompilerParams(vmem_limit_bytes=32 << 20),
        cost_estimate=cost(1),
        name="edge",
    )(cells2d, pick, *after)


def rims(first, last):
    both = jnp.concatenate([lon_shift(first, -1), lon_shift(last, 1)], 0)
    return dotg(both, jnp.concatenate(edge_picks(), 0), 0, 0).astype(BF)


PLANES = [[16 * half + i for i in range(16)] for half in range(2)]


def plane_exchange(pieces):
    return lax.all_to_all(pieces, "lon", 0, 0, axis_index_groups=PLANES)


def total_kernel(*refs):
    total = refs[0][0].astype(F32)
    for i in range(1, 16):
        total = total + refs[0][i].astype(F32)
    refs[-1][...] = total.astype(BF)


def plane_total(pieces, after):
    vmem = pl.BlockSpec(memory_space=pltpu.VMEM)
    return pl.pallas_call(
        total_kernel,
        out_shape=jax.ShapeDtypeStruct((PIECE, LANES), BF),
        in_specs=[vmem] + [pl.BlockSpec(memory_space=pl.ANY)] * len(after),
        out_specs=vmem,
        cost_estimate=cost(1.2),
        name="plane_total",
    )(pieces, *after)


def copies_kernel(part, out):
    for i in range(16):
        out[i] = part[...]


def plane_copies(part):
    vmem = pl.BlockSpec(memory_space=pltpu.VMEM)
    return pl.pallas_call(
        copies_kernel,
        out_shape=jax.ShapeDtypeStruct((16, PIECE, LANES), BF),
        in_specs=[vmem],
        out_specs=vmem,
        cost_estimate=cost(1),
        name="plane_copies",
    )(part)


def reduce_gradients(keep, send, after):
    mine = keep.astype(F32) + ch_swap(send, 1).astype(F32)
    mine = plane_exchange(mine.astype(BF).reshape(16, PIECE, LANES))
    wire = plane_total(mine, after)
    part = (
        (wire.astype(F32) + lon_swap(wire, 16).astype(F32))
        + (ch_swap(wire, 2).astype(F32) + both_swap(wire).astype(F32))
    ).astype(BF)
    return plane_exchange(plane_copies(part)).reshape(WIRE, LANES)


def finish_kernel(core_ref, own, other, pad, grad_in, grad_out, held):
    core = core_ref[0]
    for wire, slot in ((own, core), (other, 1 - core)):
        for t in range(3):
            held[slot, :, t * LANES : (t + 1) * LANES] = wire[t * HID : (t + 1) * HID, :]
        rest = wire[3 * HID : 3 * HID + 400, :]
        for q in range(4):
            held[slot, q * 400 : (q + 1) * 400, 3 * LANES :] = rest[:, q * 32 : (q + 1) * 32]
    factor = 1.0 / math.sqrt(ROWS * LANES * 32)
    grad_in[...] = dotg(pad[...], held[0], 1, 1) * factor
    grad_out[...] = dotg(pad[...], held[1], 1, 1) * factor


def finish(core, own, other, pad):
    vmem = pl.BlockSpec(memory_space=pltpu.VMEM)
    return pl.pallas_call(
        finish_kernel,
        out_shape=[
            jax.ShapeDtypeStruct((C, HID), F32),
            jax.ShapeDtypeStruct((C, HID), F32),
        ],
        in_specs=[pl.BlockSpec(memory_space=pltpu.SMEM)] + [vmem] * 3,
        out_specs=[vmem] * 2,
        scratch_shapes=[pltpu.VMEM((2, HID, 4 * CP), BF)],
        compiler_params=pltpu.CompilerParams(vmem_limit_bytes=32 << 20),
        cost_estimate=cost(6),
        name="finish",
    )(core, own, other, pad)


def both_swap(x):
    return lax.ppermute(x, ("lon", "ch"), [(i, i ^ (16 * 4 + 2)) for i in range(128)])


def body(
    ocean_state,
    sea_mask,
    kernel,
    conv_bias,
    norm_gain,
    norm_bias,
    weight_in,
    bias_in,
    weight_out,
    bias_out,
    layer_scale,
    cotangent,
):
    ch = lax.axis_index("ch")
    me = ch.reshape(1)
    core = (ch & 1).reshape(1)
    scale = jnp.pad(layer_scale, (0, CP - LC)).reshape(CP, 1)

    head, tail = edge_picks()
    state2d = ocean_state.reshape(LC * ROWS, LANES)
    sent = {}
    first = edge(state2d, head)
    sent[2] = branch_share(me, cotangent, sea_mask, scale, 2, (first,))
    last = edge(state2d, tail, (sent[2],))
    sent[3] = branch_share(me, cotangent, sea_mask, scale, 3, (last,))
    sent[1] = branch_share(me, cotangent, sea_mask, scale, 1, (sent[3],))
    sent[0] = branch_share(me, cotangent, sea_mask, scale, 0, (sent[1],))
    gs = [sent[0]] + [ch_swap(sent[k], k) for k in (1, 2, 3)]

    chan = jnp.arange(C)
    pad = ((chan // LC * CP + chan % LC)[:, None] == jnp.arange(4 * CP)[None, :]).astype(BF)
    win, win_t, wout_t, wout = padded_weights(weight_in, weight_out.T, pad)
    vec = jnp.stack([norm_gain, norm_bias, bias_out], 1).reshape(4, LC, 3)
    vec = jnp.pad(vec, ((0, 0), (0, CP - LC), (0, 0))).reshape(4 * CP, 3)

    state_rim = rims(first, last).reshape(LC, ROWS, LANES)
    bias = jnp.broadcast_to(conv_bias[:, None, None], (LC, 1, LANES))
    conv = conv_forward(me, ocean_state, state_rim, tap_patterns(kernel), bias)
    xs = [conv[0]] + [ch_swap(conv[k], k) for k in (1, 2, 3)]

    branch, grad, keep, send = mlp(
        me, core, xs, gs, (win_t, win, wout, wout_t), vec, bias_in.reshape(HID, 1)
    )

    grads = [grad[0]] + [ch_swap(grad[k], k) for k in (1, 2, 3)]
    pieces = [branch[0]] + [ch_swap(branch[k], k) for k in (1, 2, 3)]

    every = jnp.concatenate(grads, 0).reshape(4 * QR * CP, LANES)
    grad_rims = rims(edge(every, head), edge(every, tail)).reshape(4, QR, CP, LANES)
    own = reduce_gradients(keep, send, grads[1:] + pieces[1:])

    grad_state = conv_backward(
        me,
        grads,
        [grad_rims[k] for k in range(4)],
        tap_patterns(kernel[:, ::-1]),
        cotangent,
        sea_mask,
    )
    updated = update(me, pieces, ocean_state, sea_mask, scale)

    own, grad_state, updated = lax.optimization_barrier((own, grad_state, updated))
    grad_in, grad_out = finish(core, own, ch_swap(own, 1), pad)
    return updated, grad_state, grad_in, grad_out.T


def solution(mesh):
    return jax.shard_map(
        body,
        mesh=mesh,
        in_specs=(
            P("ch", None, "lon"),
            P(None, "lon"),
            P("ch", None),
            P("ch"),
            P(),
            P(),
            P(),
            P(),
            P(),
            P(),
            P("ch"),
            P("ch", None, "lon"),
        ),
        out_specs=(P("ch", None, "lon"), P("ch", None, "lon"), P(), P()),
        check_vma=False,
    )
```

```python
import functools
import math

import jax
import jax.numpy as jnp
from jax import lax
from jax.experimental import pallas as pl
from jax.experimental.pallas import tpu as pltpu
from jax.sharding import PartitionSpec as P

KW = 7
RIM = KW // 2
C = 400
HID = 1600
ROWS = 64
LANES = 128
LC = 100
CP = 104
QR = 16
HR = 8
GROUP = 8
BF = jnp.bfloat16
F32 = jnp.float32

root_coef = math.sqrt(2.0 / math.pi)
cubic_coef = 0.044715
norm_eps = 1e-06


def dotg(a, b, ca, cb):
    return lax.dot_general(a, b, (((ca,), (cb,)), ((), ())), preferred_element_type=F32)


def cost(micros):
    return pl.CostEstimate(flops=0, bytes_accessed=int(micros * 3.3e6), transcendentals=0)


def ch_swap(x, k):
    return lax.ppermute(x, "ch", [(i, i ^ k) for i in range(4)])


def lon_shift(x, d):
    return lax.ppermute(x, "lon", [(i, (i + d) % 32) for i in range(32)])


def lon_swap(x, k):
    return lax.ppermute(x, "lon", [(i, i ^ k) for i in range(32)])


def share_kernel(me_ref, cot_ref, mask_ref, scale_ref, *refs):
    out_ref = refs[-1]
    cells = cot_ref[...].astype(F32)
    cells = jnp.concatenate([cells, jnp.zeros((CP - LC, QR, LANES), F32)], axis=0)
    cells = jnp.swapaxes(cells, 0, 1)
    mask = mask_ref[...].astype(F32)
    out_ref[...] = ((cells * mask[:, None, :]) * scale_ref[...][None]).astype(BF)


def branch_share(me, cotangent, sea_mask, scale, k, after):
    return pl.pallas_call(
        share_kernel,
        out_shape=jax.ShapeDtypeStruct((QR, CP, LANES), BF),
        grid_spec=pltpu.PrefetchScalarGridSpec(
            num_scalar_prefetch=1,
            grid=(1,),
            in_specs=[
                pl.BlockSpec((LC, QR, LANES), lambda i, me: (0, me[0] ^ k, 0)),
                pl.BlockSpec((QR, LANES), lambda i, me: (me[0] ^ k, 0)),
                pl.BlockSpec((CP, 1), lambda i, me: (0, 0)),
            ]
            + [pl.BlockSpec(memory_space=pl.ANY)] * len(after),
            out_specs=pl.BlockSpec((QR, CP, LANES), lambda i, me: (0, 0, 0)),
        ),
        compiler_params=pltpu.CompilerParams(vmem_limit_bytes=32 << 20),
        cost_estimate=cost(1.2),
        name="branch_share",
    )(me, cotangent, sea_mask, scale, *after)


def conv_channel(cells, rim, pattern, lane, band):
    moved = []
    for off in range(-RIM, RIM + 1):
        if off == 0:
            moved.append(cells.astype(BF))
        else:
            edge = lane < off if off > 0 else lane >= LANES + off
            moved.append(pltpu.roll(jnp.where(edge, rim, cells), (-off) % LANES, 1).astype(BF))
    stacked = jnp.concatenate(moved, axis=0)
    tiles = []
    for t in range(4):
        row = jnp.broadcast_to(pattern[t : t + 1, :], (ROWS, LANES))
        row = pltpu.roll(row, 0, 1, stride=1, stride_axis=0)
        tiles.append(jnp.where(band, row, 0.0).astype(BF))
    banded = jnp.concatenate(tiles, axis=1)[:, : KW * ROWS]
    return jnp.dot(banded, stacked, preferred_element_type=F32)


def masks():
    lane = lax.broadcasted_iota(jnp.int32, (ROWS, LANES), 1)
    row = lax.broadcasted_iota(jnp.int32, (ROWS, LANES), 0)
    away = (lane & (ROWS - 1)) - row
    return lane, (away >= -RIM) & (away <= RIM)


def forward_kernel(me_ref, state_ref, rim_ref, pat_ref, bias_ref, *refs):
    held = refs[-1]
    step = pl.program_id(0)
    lane, band = masks()
    outs = []
    for c in range(GROUP):
        total = conv_channel(
            state_ref[c].astype(F32), rim_ref[c].astype(F32), pat_ref[c], lane, band
        )
        total = total + bias_ref[c]
        outs.append(jnp.where(step * GROUP + c < LC, total, 0.0))
    held[...] = jnp.swapaxes(jnp.stack(outs, 0), 0, 1).reshape(4, QR, GROUP, LANES)
    me = me_ref[0]
    for k in range(4):
        share = held[me ^ k].astype(BF)
        refs[k][...] = share[:HR]
        refs[4 + k][...] = share[HR:]


def conv_forward(me, state, rim, pattern, bias):
    share = jax.ShapeDtypeStruct((HR, CP, LANES), BF)
    return pl.pallas_call(
        forward_kernel,
        out_shape=[share] * 8,
        grid_spec=pltpu.PrefetchScalarGridSpec(
            num_scalar_prefetch=1,
            grid=(CP // GROUP,),
            in_specs=[
                pl.BlockSpec((GROUP, ROWS, LANES), lambda i, me: (i, 0, 0)),
                pl.BlockSpec((GROUP, ROWS, LANES), lambda i, me: (i, 0, 0)),
                pl.BlockSpec((GROUP, 4, LANES), lambda i, me: (i, 0, 0)),
                pl.BlockSpec((GROUP, 1, LANES), lambda i, me: (i, 0, 0)),
            ],
            out_specs=[pl.BlockSpec((HR, GROUP, LANES), lambda i, me: (0, i, 0))] * 8,
            scratch_shapes=[pltpu.VMEM((4, QR, GROUP, LANES), F32)],
        ),
        compiler_params=pltpu.CompilerParams(vmem_limit_bytes=32 << 20),
        cost_estimate=cost(9),
        name="conv_forward",
    )(me, state, rim, pattern, bias)


def backward_kernel(me_ref, *refs):
    pieces = refs[:8]
    rims_in, pat_ref, cot_ref, mask_ref, out_ref, held, held_rim = refs[8:]
    lane, band = masks()
    me = me_ref[0]
    for k in range(4):
        held[me ^ k, :HR] = pieces[k][...].astype(F32)
        held[me ^ k, HR:] = pieces[4 + k][...].astype(F32)
        held_rim[me ^ k, :HR] = rims_in[k].astype(F32)
        held_rim[me ^ k, HR:] = rims_in[4 + k].astype(F32)
    cells = jnp.swapaxes(held[...].reshape(ROWS, GROUP, LANES), 0, 1)
    rims = jnp.swapaxes(held_rim[...].reshape(ROWS, GROUP, LANES), 0, 1)
    mask = mask_ref[...].astype(F32)
    for c in range(GROUP):
        total = conv_channel(cells[c], rims[c], pat_ref[c], lane, band)
        out_ref[c] = (cot_ref[c].astype(F32) * mask + total).astype(BF)


def conv_backward(me, pieces, rims, pattern, cotangent, sea_mask):
    return pl.pallas_call(
        backward_kernel,
        out_shape=jax.ShapeDtypeStruct((LC, ROWS, LANES), BF),
        grid_spec=pltpu.PrefetchScalarGridSpec(
            num_scalar_prefetch=1,
            grid=(CP // GROUP,),
            in_specs=[pl.BlockSpec((HR, GROUP, LANES), lambda i, me: (0, i, 0))] * 8
            + [
                pl.BlockSpec((8, HR, GROUP, LANES), lambda i, me: (0, 0, i, 0)),
                pl.BlockSpec((GROUP, 4, LANES), lambda i, me: (i, 0, 0)),
                pl.BlockSpec((GROUP, ROWS, LANES), lambda i, me: (i, 0, 0)),
                pl.BlockSpec((ROWS, LANES), lambda i, me: (0, 0)),
            ],
            out_specs=pl.BlockSpec((GROUP, ROWS, LANES), lambda i, me: (i, 0, 0)),
            scratch_shapes=[pltpu.VMEM((4, QR, GROUP, LANES), F32)] * 2,
        ),
        compiler_params=pltpu.CompilerParams(vmem_limit_bytes=32 << 20),
        cost_estimate=cost(10),
        name="conv_backward",
    )(me, *pieces, rims, pattern, cotangent, sea_mask)


SUB = 4
CELLS = SUB * LANES
HT = 400
PIECE = 328
WIRE = 16 * PIECE


def mlp_kernel(half, me_ref, *refs):
    xs, gs = refs[:4], refs[4:8]
    win_t, win, wout, wout_t, vec, bias_in = refs[8:14]
    refs = refs[-10:]
    grad_out, branch_out = refs[:4], refs[4:8]
    hidden, cells = refs[8:]
    me = me_ref[0]

    def gather(pieces, first):
        return jnp.concatenate(
            [
                jnp.concatenate([p[first + r].astype(F32) for r in range(SUB)], axis=1)
                for p in pieces
            ],
            axis=0,
        )

    def part(j, _):
        lanes = pl.ds(pl.multiple_of(j * CELLS, CELLS), CELLS)
        gain = vec[:, 0:1]
        values = gather(xs, j * SUB)
        mean_val = jnp.sum(values, axis=0, keepdims=True) / C
        square = jnp.sum(values * values, axis=0, keepdims=True) / C
        inv_std = lax.rsqrt(square - mean_val * mean_val + norm_eps)
        normed = (values - mean_val) * inv_std * gain + vec[:, 1:2]
        grads = gather(gs, half * HR + j * SUB)
        for k in range(4):
            cells[0, me ^ k, :, lanes] = normed[k * CP : (k + 1) * CP].astype(BF)
            cells[1, me ^ k, :, lanes] = grads[k * CP : (k + 1) * CP].astype(BF)
        normed, grads = normed.astype(BF), grads.astype(BF)
        for t in range(HID // HT):
            rows = slice(t * HT, (t + 1) * HT)
            pre = jnp.dot(win_t[rows, :], normed, preferred_element_type=F32) + bias_in[rows, :]
            gact = jnp.dot(wout[rows, :], grads, preferred_element_type=F32)
            sq = pre * pre
            tangent = jnp.tanh(pre * (root_coef + (root_coef * cubic_coef) * sq))
            side = 0.5 + 0.5 * tangent
            value = pre * side
            slope = side + value * (1.0 - side) * (
                2.0 * root_coef + (6.0 * root_coef * cubic_coef) * sq
            )
            hidden[0, rows, lanes] = (gact * slope).astype(BF)
            hidden[1, rows, lanes] = value.astype(BF)
        x_grad = jnp.dot(win[...], hidden[0, :, lanes], preferred_element_type=F32) * gain
        centred = (values - mean_val) * inv_std
        first = jnp.sum(x_grad, axis=0, keepdims=True) / C
        second = jnp.sum(x_grad * centred, axis=0, keepdims=True) / C
        x_grad = inv_std * (x_grad - first - centred * second)
        branch = jnp.dot(wout_t[...], hidden[1, :, lanes], preferred_element_type=F32)
        branch = branch + vec[:, 2:3]
        for k in range(4):
            for r in range(SUB):
                here = slice(r * LANES, (r + 1) * LANES)
                grad_out[k][j * SUB + r] = x_grad[k * CP : (k + 1) * CP, here].astype(BF)
                branch_out[k][j * SUB + r] = branch[k * CP : (k + 1) * CP, here].astype(BF)
        return 0

    lax.fori_loop(0, 2, part, 0)


def mlp(half, me, xs, gs, weights, vec, bias_in, after=()):
    vmem = pl.BlockSpec(memory_space=pltpu.VMEM)
    piece = jax.ShapeDtypeStruct((HR, CP, LANES), BF)
    outs = pl.pallas_call(
        functools.partial(mlp_kernel, half),
        out_shape=[piece] * 8
        + [
            jax.ShapeDtypeStruct((2, HID, 2 * CELLS), BF),
            jax.ShapeDtypeStruct((2, 4, CP, 2 * CELLS), BF),
        ],
        in_specs=[pl.BlockSpec(memory_space=pltpu.SMEM)]
        + [vmem] * 14
        + [pl.BlockSpec(memory_space=pl.ANY)] * len(after),
        out_specs=[vmem] * 10,
        compiler_params=pltpu.CompilerParams(vmem_limit_bytes=24 << 20),
        cost_estimate=cost(12),
        name="mlp_b" if half else "mlp_a",
    )(me, *xs, *gs, *weights, vec, bias_in, *after)
    return outs[:4], outs[4:8], outs[8], outs[9].reshape(2, 4 * CP, 2 * CELLS)


def weight_kernel(which_ref, hid_a, hid_b, cells_a, cells_b, *refs):
    out, held = refs[-2:]
    which = which_ref[0]
    held[...] = dotg(hid_a[which], cells_a[which], 1, 1) + dotg(
        hid_b[which], cells_b[which], 1, 1
    )
    for t in range(3):
        out[t * HID : (t + 1) * HID, :] = held[:, t * LANES : (t + 1) * LANES].astype(BF)
    rest = [held[q * 400 : (q + 1) * 400, 3 * LANES :] for q in range(4)]
    out[3 * HID : 3 * HID + 400, :] = jnp.concatenate(rest, axis=1).astype(BF)
    out[3 * HID + 400 :, :] = jnp.zeros((WIRE - 3 * HID - 400, LANES), BF)


def weight_sums(which, hids, cells, after=()):
    vmem = pl.BlockSpec(memory_space=pltpu.VMEM)
    return pl.pallas_call(
        weight_kernel,
        out_shape=jax.ShapeDtypeStruct((WIRE, LANES), BF),
        in_specs=[pl.BlockSpec(memory_space=pltpu.SMEM)]
        + [vmem] * 4
        + [pl.BlockSpec(memory_space=pl.ANY)] * len(after),
        out_specs=vmem,
        scratch_shapes=[pltpu.VMEM((HID, 4 * CP), F32)],
        compiler_params=pltpu.CompilerParams(vmem_limit_bytes=16 << 20),
        cost_estimate=cost(4),
        name="weight_sums",
    )(which, *hids, *cells, *after)


def update_kernel(me_ref, *refs):
    k = pl.program_id(0)
    state_ref, mask_ref, scale_ref, out_ref = refs[8:]

    def write(early, late):
        branch = jnp.concatenate([early[...], late[...]], axis=0).astype(F32)
        branch = jnp.swapaxes(branch * scale_ref[...][None], 0, 1)[:LC]
        mask = mask_ref[...].astype(F32)
        out_ref[...] = (mask[None] * (state_ref[...].astype(F32) + branch)).astype(BF)

    for i in range(4):
        pl.when(k == i)(lambda i=i: write(refs[i], refs[4 + i]))


def update(me, pieces, state, sea_mask, scale):
    whole = pl.BlockSpec((HR, CP, LANES), lambda i, me: (0, 0, 0), pipeline_mode=pl.Buffered(1))
    return pl.pallas_call(
        update_kernel,
        out_shape=jax.ShapeDtypeStruct((LC, ROWS, LANES), BF),
        grid_spec=pltpu.PrefetchScalarGridSpec(
            num_scalar_prefetch=1,
            grid=(4,),
            in_specs=[whole] * 8
            + [
                pl.BlockSpec((LC, QR, LANES), lambda i, me: (0, me[0] ^ i, 0)),
                pl.BlockSpec((QR, LANES), lambda i, me: (me[0] ^ i, 0)),
                pl.BlockSpec((CP, 1), lambda i, me: (0, 0)),
            ],
            out_specs=pl.BlockSpec((LC, QR, LANES), lambda i, me: (0, me[0] ^ i, 0)),
        ),
        compiler_params=pltpu.CompilerParams(vmem_limit_bytes=32 << 20),
        cost_estimate=cost(4.4),
        name="update",
    )(me, *pieces, state, sea_mask, scale)


def weights_kernel(one, two, pad, one_out, one_t, two_out, two_t):
    for source, out, turned in ((one, one_out, one_t), (two, two_out, two_t)):
        padded = dotg(pad[...], source[...], 0, 0)
        out[...] = padded.astype(BF)
        turned[...] = padded.T.astype(BF)


def padded_weights(one, two, pad):
    vmem = pl.BlockSpec(memory_space=pltpu.VMEM)
    flat = jax.ShapeDtypeStruct((4 * CP, HID), BF)
    turned = jax.ShapeDtypeStruct((HID, 4 * CP), BF)
    return pl.pallas_call(
        weights_kernel,
        out_shape=[flat, turned, flat, turned],
        in_specs=[vmem] * 3,
        out_specs=[vmem] * 4,
        compiler_params=pltpu.CompilerParams(vmem_limit_bytes=48 << 20),
        cost_estimate=cost(5),
        name="padded_weights",
    )(one, two, pad)


def tap_patterns(kernel):
    lane = jnp.arange(4 * LANES)
    tile, pos = lane // LANES, lane % LANES
    away = jnp.where(pos % ROWS < ROWS // 2, pos % ROWS, pos % ROWS - ROWS)
    side = ((pos - away) // ROWS) % 2
    col = 2 * tile + side
    tap = jnp.where((jnp.abs(away) <= RIM) & (col < KW), (away + RIM) * KW + col, -1)
    pick = (jnp.arange(KW * KW)[:, None] == tap[None, :]).astype(BF)
    return jnp.dot(kernel.astype(BF), pick, preferred_element_type=F32).reshape(LC, 4, LANES)


def edge_picks():
    row = jnp.arange(8)[:, None]
    lane = jnp.arange(LANES)[None, :]
    head = ((row < RIM) & (lane == row)).astype(BF)
    tail = ((row < RIM) & (lane == LANES - RIM + row)).astype(BF)
    return head, tail


def edge_kernel(cells, pick, *refs):
    refs[-1][...] = dotg(pick[...], cells[...], 1, 1).astype(BF)


def edge(cells2d, pick, after=()):
    vmem = pl.BlockSpec(memory_space=pltpu.VMEM)
    return pl.pallas_call(
        edge_kernel,
        out_shape=jax.ShapeDtypeStruct((8, cells2d.shape[0]), BF),
        in_specs=[vmem, vmem] + [pl.BlockSpec(memory_space=pl.ANY)] * len(after),
        out_specs=vmem,
        compiler_params=pltpu.CompilerParams(vmem_limit_bytes=32 << 20),
        cost_estimate=cost(1),
        name="edge",
    )(cells2d, pick, *after)


def piece_edges_kernel(pick, *refs):
    first, last = refs[8:]
    for i in range(8):
        cells = refs[i][...].reshape(HR * CP, LANES)
        both = dotg(pick[...], cells, 1, 1).astype(BF)
        first[i] = both[:8]
        last[i] = both[8:]


def piece_edges(picks, pieces):
    vmem = pl.BlockSpec(memory_space=pltpu.VMEM)
    half = pl.BlockSpec((QR // 2, CP, LANES), lambda i: (0, 0, 0))
    whole = pl.BlockSpec((8, 8, HR * CP), lambda i: (0, 0, 0))
    out = jax.ShapeDtypeStruct((8, 8, HR * CP), BF)
    return pl.pallas_call(
        piece_edges_kernel,
        out_shape=[out, out],
        grid=(1,),
        in_specs=[pl.BlockSpec((16, LANES), lambda i: (0, 0))] + [half] * 8,
        out_specs=[whole] * 2,
        compiler_params=pltpu.CompilerParams(vmem_limit_bytes=24 << 20),
        cost_estimate=cost(2),
        name="piece_edges",
    )(picks, *pieces)


def piece_rims_kernel(pick, first, last, out):
    for i in range(8):
        both = jnp.concatenate([first[i], last[i]], axis=0)
        out[i] = dotg(both, pick[...], 0, 0).astype(BF).reshape(HR, CP, LANES)


def piece_rims(picks, first, last):
    vmem = pl.BlockSpec(memory_space=pltpu.VMEM)
    return pl.pallas_call(
        piece_rims_kernel,
        out_shape=jax.ShapeDtypeStruct((8, HR, CP, LANES), BF),
        in_specs=[vmem] * 3,
        out_specs=vmem,
        compiler_params=pltpu.CompilerParams(vmem_limit_bytes=24 << 20),
        cost_estimate=cost(2),
        name="piece_rims",
    )(picks, lon_shift(first, -1), lon_shift(last, 1))


def rims(first, last):
    both = jnp.concatenate([lon_shift(first, -1), lon_shift(last, 1)], 0)
    return dotg(both, jnp.concatenate(edge_picks(), 0), 0, 0).astype(BF)


PLANES = [[16 * half + i for i in range(16)] for half in range(2)]


def plane_exchange(pieces):
    return lax.all_to_all(pieces, "lon", 0, 0, axis_index_groups=PLANES)


def total_kernel(*refs):
    total = refs[0][0].astype(F32)
    for i in range(1, 16):
        total = total + refs[0][i].astype(F32)
    refs[-1][...] = total.astype(BF)


def plane_total(pieces, after):
    vmem = pl.BlockSpec(memory_space=pltpu.VMEM)
    return pl.pallas_call(
        total_kernel,
        out_shape=jax.ShapeDtypeStruct((PIECE, LANES), BF),
        in_specs=[vmem] + [pl.BlockSpec(memory_space=pl.ANY)] * len(after),
        out_specs=vmem,
        cost_estimate=cost(1.2),
        name="plane_total",
    )(pieces, *after)


def core_kernel(keep, other, *refs):
    refs[-1][...] = (keep[...].astype(F32) + other[...].astype(F32)).astype(BF)


def core_total(keep, other, after):
    step = WIRE // 4
    block = pl.BlockSpec((step, LANES), lambda i: (i, 0))
    return pl.pallas_call(
        core_kernel,
        out_shape=jax.ShapeDtypeStruct((WIRE, LANES), BF),
        grid=(4,),
        in_specs=[block, block] + [pl.BlockSpec(memory_space=pl.ANY)] * len(after),
        out_specs=block,
        cost_estimate=cost(2),
        name="core_total",
    )(keep, other, *after)


def copies_kernel(part, out):
    for i in range(16):
        out[i] = part[...]


def plane_copies(part):
    vmem = pl.BlockSpec(memory_space=pltpu.VMEM)
    return pl.pallas_call(
        copies_kernel,
        out_shape=jax.ShapeDtypeStruct((16, PIECE, LANES), BF),
        in_specs=[vmem],
        out_specs=vmem,
        cost_estimate=cost(1),
        name="plane_copies",
    )(part)


def reduce_gradients(keep, send, early, late):
    mine = core_total(keep, ch_swap(send, 1), early)
    mine = plane_exchange(mine.reshape(16, PIECE, LANES))
    wire = plane_total(mine, late)
    part = (
        (wire.astype(F32) + lon_swap(wire, 16).astype(F32))
        + (ch_swap(wire, 2).astype(F32) + both_swap(wire).astype(F32))
    ).astype(BF)
    return plane_exchange(plane_copies(part)).reshape(WIRE, LANES)


def finish_kernel(core_ref, own, other, pad, grad_in, grad_out, held):
    core = core_ref[0]
    for wire, slot in ((own, core), (other, 1 - core)):
        for t in range(3):
            held[slot, :, t * LANES : (t + 1) * LANES] = wire[t * HID : (t + 1) * HID, :]
        rest = wire[3 * HID : 3 * HID + 400, :]
        for q in range(4):
            held[slot, q * 400 : (q + 1) * 400, 3 * LANES :] = rest[:, q * 32 : (q + 1) * 32]
    factor = 1.0 / math.sqrt(ROWS * LANES * 32)
    grad_in[...] = dotg(pad[...], held[0], 1, 1) * factor
    grad_out[...] = dotg(pad[...], held[1], 1, 1) * factor


def finish(core, own, other, pad):
    vmem = pl.BlockSpec(memory_space=pltpu.VMEM)
    return pl.pallas_call(
        finish_kernel,
        out_shape=[
            jax.ShapeDtypeStruct((C, HID), F32),
            jax.ShapeDtypeStruct((C, HID), F32),
        ],
        in_specs=[pl.BlockSpec(memory_space=pltpu.SMEM)] + [vmem] * 3,
        out_specs=[vmem] * 2,
        scratch_shapes=[pltpu.VMEM((2, HID, 4 * CP), BF)],
        compiler_params=pltpu.CompilerParams(vmem_limit_bytes=32 << 20),
        cost_estimate=cost(6),
        name="finish",
    )(core, own, other, pad)


def both_swap(x):
    return lax.ppermute(x, ("lon", "ch"), [(i, i ^ (16 * 4 + 2)) for i in range(128)])


def body(
    ocean_state,
    sea_mask,
    kernel,
    conv_bias,
    norm_gain,
    norm_bias,
    weight_in,
    bias_in,
    weight_out,
    bias_out,
    layer_scale,
    cotangent,
):
    ch = lax.axis_index("ch")
    me = ch.reshape(1)
    core = (ch & 1).reshape(1)
    scale = jnp.pad(layer_scale, (0, CP - LC)).reshape(CP, 1)

    head, tail = edge_picks()
    state2d = ocean_state.reshape(LC * ROWS, LANES)
    sent = {}
    first = edge(state2d, head)
    sent[2] = branch_share(me, cotangent, sea_mask, scale, 2, (first,))
    last = edge(state2d, tail, (sent[2],))
    sent[3] = branch_share(me, cotangent, sea_mask, scale, 3, (last,))
    sent[1] = branch_share(me, cotangent, sea_mask, scale, 1, (sent[3],))
    sent[0] = branch_share(me, cotangent, sea_mask, scale, 0, (sent[1],))
    gs = [sent[0]] + [ch_swap(sent[k], k) for k in (1, 2, 3)]

    chan = jnp.arange(C)
    padded = jnp.arange(4 * CP)
    pad = ((chan // LC * CP + chan % LC)[:, None] == padded[None, :]).astype(BF)
    pad_own = (((chan // LC ^ ch) * CP + chan % LC)[:, None] == padded[None, :]).astype(BF)
    win, win_t, wout_t, wout = padded_weights(weight_in, weight_out.T, pad_own)
    vec = jnp.stack([norm_gain, norm_bias, bias_out], 1).reshape(4, LC, 3)
    vec = jnp.pad(vec, ((0, 0), (0, CP - LC), (0, 0)))
    vec = jnp.concatenate([lax.dynamic_index_in_dim(vec, ch ^ k, 0, False) for k in range(4)], 0)

    state_rim = rims(first, last).reshape(LC, ROWS, LANES)
    bias = jnp.broadcast_to(conv_bias[:, None, None], (LC, 1, LANES))
    conv = conv_forward(me, ocean_state, state_rim, tap_patterns(kernel), bias)
    xs = [
        [conv[4 * half]] + [ch_swap(conv[4 * half + k], k) for k in (1, 2, 3)] for half in (0, 1)
    ]

    weights = (win_t, win, wout, wout_t)
    bias_rows = bias_in.reshape(HID, 1)
    grad_a, branch_a, hid_a, cells_a = mlp(0, me, xs[0], gs, weights, vec, bias_rows)
    grad_a = [grad_a[0]] + [ch_swap(grad_a[k], k) for k in (1, 2, 3)]
    branch_a = [branch_a[0]] + [ch_swap(branch_a[k], k) for k in (1, 2, 3)]
    grad_b, branch_b, hid_b, cells_b = mlp(1, me, xs[1], gs, weights, vec, bias_rows, grad_a[:1])
    grad_b = [grad_b[0]] + [ch_swap(grad_b[k], k) for k in (1, 2, 3)]
    branch_b = [branch_b[0]] + [ch_swap(branch_b[k], k) for k in (1, 2, 3)]
    grads, branches = grad_a + grad_b, branch_a + branch_b
    send = weight_sums(1 - core, (hid_a, hid_b), (cells_a, cells_b), grad_a[1:])
    keep = weight_sums(core, (hid_a, hid_b), (cells_a, cells_b))

    picks = jnp.concatenate([head, tail], 0)
    grad_rims = piece_rims(picks, *piece_edges(picks, grads))
    own = reduce_gradients(keep, send, (), branch_a[1:] + grad_b[1:] + branch_b[1:])

    grad_state = conv_backward(
        me,
        grads,
        grad_rims,
        tap_patterns(kernel[:, ::-1]),
        cotangent,
        sea_mask,
    )
    updated = update(me, branches, ocean_state, sea_mask, scale)
    own, grad_state, updated = lax.optimization_barrier((own, grad_state, updated))
    grad_in, grad_out = finish(core, own, ch_swap(own, 1), pad)
    return updated, grad_state, grad_in, grad_out.T


def solution(mesh):
    return jax.shard_map(
        body,
        mesh=mesh,
        in_specs=(
            P("ch", None, "lon"),
            P(None, "lon"),
            P("ch", None),
            P("ch"),
            P(),
            P(),
            P(),
            P(),
            P(),
            P(),
            P("ch"),
            P("ch", None, "lon"),
        ),
        out_specs=(P("ch", None, "lon"), P("ch", None, "lon"), P(), P()),
        check_vma=False,
    )
```

```python
import functools
import math

import jax
import jax.numpy as jnp
from jax import lax
from jax.experimental import pallas as pl
from jax.experimental.pallas import tpu as pltpu
from jax.sharding import PartitionSpec as P

KW = 7
RIM = KW // 2
C = 400
HID = 1600
ROWS = 64
LANES = 128
LC = 100
CP = 104
QR = 16
HR = 8
GROUP = 8
VMEM = 63 << 20
BF = jnp.bfloat16
F32 = jnp.float32

root_coef = math.sqrt(2.0 / math.pi)
cubic_coef = 0.044715
norm_eps = 1e-06


def dotg(a, b, ca, cb):
    return lax.dot_general(a, b, (((ca,), (cb,)), ((), ())), preferred_element_type=F32)


def cost(micros):
    return pl.CostEstimate(flops=0, bytes_accessed=int(micros * 3.3e6), transcendentals=0)


def full(shape):
    return pl.BlockSpec(shape, lambda *i: (0,) * len(shape), pipeline_mode=pl.Buffered(1))


def ch_swap(x, k):
    return lax.ppermute(x, "ch", [(i, i ^ k) for i in range(4)])


def lon_shift(x, d):
    return lax.ppermute(x, "lon", [(i, (i + d) % 32) for i in range(32)])


def lon_swap(x, k):
    return lax.ppermute(x, "lon", [(i, i ^ k) for i in range(32)])


def share_kernel(me_ref, cot_ref, mask_ref, scale_ref, *refs):
    out_ref = refs[-1]
    cells = cot_ref[...].astype(F32)
    cells = jnp.concatenate([cells, jnp.zeros((CP - LC, QR, LANES), F32)], axis=0)
    cells = jnp.swapaxes(cells, 0, 1)
    mask = mask_ref[...].astype(F32)
    out_ref[...] = ((cells * mask[:, None, :]) * scale_ref[...][None]).astype(BF)


def branch_share(me, cotangent, sea_mask, scale, k, after):
    return pl.pallas_call(
        share_kernel,
        out_shape=jax.ShapeDtypeStruct((QR, CP, LANES), BF),
        grid_spec=pltpu.PrefetchScalarGridSpec(
            num_scalar_prefetch=1,
            grid=(1,),
            in_specs=[
                pl.BlockSpec((LC, QR, LANES), lambda i, me: (0, me[0] ^ k, 0)),
                pl.BlockSpec((QR, LANES), lambda i, me: (me[0] ^ k, 0)),
                pl.BlockSpec((CP, 1), lambda i, me: (0, 0)),
            ]
            + [pl.BlockSpec(memory_space=pl.ANY)] * len(after),
            out_specs=pl.BlockSpec((QR, CP, LANES), lambda i, me: (0, 0, 0)),
        ),
        compiler_params=pltpu.CompilerParams(vmem_limit_bytes=VMEM),
        cost_estimate=cost(1.2),
        name="branch_share",
    )(me, cotangent, sea_mask, scale, *after)


def conv_channel(cells, rim, pattern, lane, band):
    moved = []
    for off in range(-RIM, RIM + 1):
        if off == 0:
            moved.append(cells.astype(BF))
        else:
            edge = lane < off if off > 0 else lane >= LANES + off
            moved.append(pltpu.roll(jnp.where(edge, rim, cells), (-off) % LANES, 1).astype(BF))
    stacked = jnp.concatenate(moved, axis=0)
    tiles = []
    for t in range(4):
        row = jnp.broadcast_to(pattern[t : t + 1, :], (ROWS, LANES))
        row = pltpu.roll(row, 0, 1, stride=1, stride_axis=0)
        tiles.append(jnp.where(band, row, 0.0).astype(BF))
    banded = jnp.concatenate(tiles, axis=1)[:, : KW * ROWS]
    return jnp.dot(banded, stacked, preferred_element_type=F32)


def masks():
    lane = lax.broadcasted_iota(jnp.int32, (ROWS, LANES), 1)
    row = lax.broadcasted_iota(jnp.int32, (ROWS, LANES), 0)
    away = (lane & (ROWS - 1)) - row
    return lane, (away >= -RIM) & (away <= RIM)


def forward_kernel(me_ref, state_ref, rim_ref, pat_ref, bias_ref, *refs):
    held = refs[-1]
    step = pl.program_id(0)
    lane, band = masks()
    outs = []
    for c in range(GROUP):
        total = conv_channel(
            state_ref[c].astype(F32), rim_ref[c].astype(F32), pat_ref[c], lane, band
        )
        total = total + bias_ref[c]
        outs.append(jnp.where(step * GROUP + c < LC, total, 0.0))
    held[...] = jnp.swapaxes(jnp.stack(outs, 0), 0, 1).reshape(4, QR, GROUP, LANES)
    me = me_ref[0]
    for k in range(4):
        share = held[me ^ k].astype(BF)
        refs[k][...] = share[:HR]
        refs[4 + k][...] = share[HR:]


def conv_forward(me, state, rim, pattern, bias):
    share = jax.ShapeDtypeStruct((HR, CP, LANES), BF)
    return pl.pallas_call(
        forward_kernel,
        out_shape=[share] * 8,
        grid_spec=pltpu.PrefetchScalarGridSpec(
            num_scalar_prefetch=1,
            grid=(CP // GROUP,),
            in_specs=[
                pl.BlockSpec((GROUP, ROWS, LANES), lambda i, me: (i, 0, 0)),
                pl.BlockSpec((GROUP, ROWS, LANES), lambda i, me: (i, 0, 0)),
                pl.BlockSpec((GROUP, 4, LANES), lambda i, me: (i, 0, 0)),
                pl.BlockSpec((GROUP, 1, LANES), lambda i, me: (i, 0, 0)),
            ],
            out_specs=[pl.BlockSpec((HR, GROUP, LANES), lambda i, me: (0, i, 0))] * 8,
            scratch_shapes=[pltpu.VMEM((4, QR, GROUP, LANES), F32)],
        ),
        compiler_params=pltpu.CompilerParams(vmem_limit_bytes=VMEM),
        cost_estimate=cost(9),
        name="conv_forward",
    )(me, state, rim, pattern, bias)


def backward_kernel(me_ref, *refs):
    pieces = refs[:8]
    rims_in, pat_ref, cot_ref, mask_ref, out_ref, held, held_rim = refs[8:]
    lane, band = masks()
    me = me_ref[0]
    for k in range(4):
        held[me ^ k, :HR] = pieces[k][...].astype(F32)
        held[me ^ k, HR:] = pieces[4 + k][...].astype(F32)
        held_rim[me ^ k, :HR] = rims_in[k].astype(F32)
        held_rim[me ^ k, HR:] = rims_in[4 + k].astype(F32)
    cells = jnp.swapaxes(held[...].reshape(ROWS, GROUP, LANES), 0, 1)
    rims = jnp.swapaxes(held_rim[...].reshape(ROWS, GROUP, LANES), 0, 1)
    mask = mask_ref[...].astype(F32)
    for c in range(GROUP):
        total = conv_channel(cells[c], rims[c], pat_ref[c], lane, band)
        out_ref[c] = (cot_ref[c].astype(F32) * mask + total).astype(BF)


def conv_backward(me, pieces, rims, pattern, cotangent, sea_mask):
    return pl.pallas_call(
        backward_kernel,
        out_shape=jax.ShapeDtypeStruct((LC, ROWS, LANES), BF),
        grid_spec=pltpu.PrefetchScalarGridSpec(
            num_scalar_prefetch=1,
            grid=(CP // GROUP,),
            in_specs=[pl.BlockSpec((HR, GROUP, LANES), lambda i, me: (0, i, 0))] * 8
            + [
                pl.BlockSpec((8, HR, GROUP, LANES), lambda i, me: (0, 0, i, 0)),
                pl.BlockSpec((GROUP, 4, LANES), lambda i, me: (i, 0, 0)),
                pl.BlockSpec((GROUP, ROWS, LANES), lambda i, me: (i, 0, 0)),
                pl.BlockSpec((ROWS, LANES), lambda i, me: (0, 0)),
            ],
            out_specs=pl.BlockSpec((GROUP, ROWS, LANES), lambda i, me: (i, 0, 0)),
            scratch_shapes=[pltpu.VMEM((4, QR, GROUP, LANES), F32)] * 2,
        ),
        compiler_params=pltpu.CompilerParams(vmem_limit_bytes=VMEM),
        cost_estimate=cost(10),
        name="conv_backward",
    )(me, *pieces, rims, pattern, cotangent, sea_mask)


SUB = 4
CELLS = SUB * LANES
HT = 400
PIECE = 328
WIRE = 16 * PIECE


def mlp_kernel(half, me_ref, core_ref, *refs):
    xs, gs = refs[:4], refs[4:8]
    win_t, win, wout, wout_t, vec, bias_in = refs[8:14]
    if half:
        hid_in, cells_in = refs[14:16]
        grad_out, branch_out, wires = refs[17:21], refs[21:25], refs[25:27]
        hidden, cells, hid_a, cells_a, held, sems = refs[27:]
        copies = (
            pltpu.make_async_copy(hid_in, hid_a, sems.at[0]),
            pltpu.make_async_copy(cells_in, cells_a, sems.at[1]),
        )
    else:
        grad_out, branch_out = refs[14:18], refs[18:22]
        hidden, cells = refs[22:]
    step = pl.program_id(0)
    me = me_ref[0]
    if half:

        @pl.when(step == 0)
        def _():
            for copy in copies:
                copy.start()

        lanes = pl.ds(pl.multiple_of(step * CELLS, CELLS), CELLS)
    else:
        lanes = slice(0, CELLS)

    def gather(pieces):
        return jnp.concatenate(
            [
                jnp.concatenate([p[r].astype(F32) for r in range(SUB)], axis=1)
                for p in pieces
            ],
            axis=0,
        )

    gain = vec[:, 0:1]
    values = gather(xs)
    mean_val = jnp.sum(values, axis=0, keepdims=True) / C
    square = jnp.sum(values * values, axis=0, keepdims=True) / C
    inv_std = lax.rsqrt(square - mean_val * mean_val + norm_eps)
    normed = (values - mean_val) * inv_std * gain + vec[:, 1:2]
    grads = gather(gs)
    for k in range(4):
        rows = slice(k * CP, (k + 1) * CP)
        cells[0, me ^ k, :, lanes] = normed[rows].astype(cells.dtype)
        cells[1, me ^ k, :, lanes] = grads[rows].astype(cells.dtype)
    normed, grads = normed.astype(BF), grads.astype(BF)
    for t in range(HID // HT):
        rows = slice(t * HT, (t + 1) * HT)
        pre = jnp.dot(win_t[rows, :], normed, preferred_element_type=F32) + bias_in[rows, :]
        gact = jnp.dot(wout[rows, :], grads, preferred_element_type=F32)
        sq = pre * pre
        tangent = jnp.tanh(pre * (root_coef + (root_coef * cubic_coef) * sq))
        side = 0.5 + 0.5 * tangent
        value = pre * side
        slope = side + value * (1.0 - side) * (
            2.0 * root_coef + (6.0 * root_coef * cubic_coef) * sq
        )
        hidden[0, rows, lanes] = (gact * slope).astype(BF)
        hidden[1, rows, lanes] = value.astype(BF)
    x_grad = jnp.dot(win[...], hidden[0, :, lanes], preferred_element_type=F32) * gain
    centred = (values - mean_val) * inv_std
    first = jnp.sum(x_grad, axis=0, keepdims=True) / C
    second = jnp.sum(x_grad * centred, axis=0, keepdims=True) / C
    x_grad = inv_std * (x_grad - first - centred * second)
    branch = jnp.dot(wout_t[...], hidden[1, :, lanes], preferred_element_type=F32)
    branch = branch + vec[:, 2:3]
    for k in range(4):
        for r in range(SUB):
            here = slice(r * LANES, (r + 1) * LANES)
            grad_out[k][r] = x_grad[k * CP : (k + 1) * CP, here].astype(BF)
            branch_out[k][r] = branch[k * CP : (k + 1) * CP, here].astype(BF)
    if not half:
        return

    @pl.when(step == 1)
    def _():
        for copy in copies:
            copy.wait()
        core = core_ref[0]
        for out, slot in ((wires[0], core), (wires[1], 1 - core)):
            cells_b = cells[slot].reshape(4 * CP, 2 * CELLS).astype(BF)
            held[...] = dotg(hid_a[slot], cells_a[slot], 1, 1) + dotg(hidden[slot], cells_b, 1, 1)
            for t in range(3):
                out[t * HID : (t + 1) * HID, :] = held[:, t * LANES : (t + 1) * LANES].astype(BF)
            rest = [held[q * 400 : (q + 1) * 400, 3 * LANES :] for q in range(4)]
            out[3 * HID : 3 * HID + 400, :] = jnp.concatenate(rest, axis=1).astype(BF)
            out[3 * HID + 400 :, :] = jnp.zeros((WIRE - 3 * HID - 400, LANES), BF)


def mlp(half, me, core, xs, gs, weights, vec, bias_in, saved=(), after=()):
    any_space = pl.BlockSpec(memory_space=pl.ANY)

    def whole(shape):
        return pl.BlockSpec(
            shape, lambda i, me, core: (0,) * len(shape), pipeline_mode=pl.Buffered(1)
        )

    piece = pl.BlockSpec((SUB, CP, LANES), lambda i, me, core: (i, 0, 0))
    later = pl.BlockSpec((SUB, CP, LANES), lambda i, me, core: (2 * half + i, 0, 0))
    if half:
        shapes = [jax.ShapeDtypeStruct((WIRE, LANES), BF)] * 2
        specs = [whole((WIRE, LANES))] * 2
        scratch = [
            pltpu.VMEM((2, HID, 2 * CELLS), BF),
            pltpu.VMEM((2, 4, CP, 2 * CELLS), F32),
            pltpu.VMEM((2, HID, 2 * CELLS), BF),
            pltpu.VMEM((2, 4 * CP, 2 * CELLS), BF),
            pltpu.VMEM((HID, 4 * CP), F32),
            pltpu.SemaphoreType.DMA((2,)),
        ]
    else:
        shapes = [
            jax.ShapeDtypeStruct((2, HID, 2 * CELLS), BF),
            jax.ShapeDtypeStruct((2, 4, CP, 2 * CELLS), BF),
        ]
        specs = [
            pl.BlockSpec((2, HID, CELLS), lambda i, me, core: (0, 0, i)),
            pl.BlockSpec((2, 4, CP, CELLS), lambda i, me, core: (0, 0, 0, i)),
        ]
        scratch = []
    outs = pl.pallas_call(
        functools.partial(mlp_kernel, half),
        out_shape=[jax.ShapeDtypeStruct((HR, CP, LANES), BF)] * 8 + shapes,
        grid_spec=pltpu.PrefetchScalarGridSpec(
            num_scalar_prefetch=2,
            grid=(2,),
            in_specs=[piece] * 4
            + [later] * 4
            + [
                whole((HID, 4 * CP)),
                whole((4 * CP, HID)),
                whole((HID, 4 * CP)),
                whole((4 * CP, HID)),
                whole((4 * CP, 3)),
                whole((HID, 1)),
            ]
            + [any_space] * (len(saved) + len(after)),
            out_specs=[piece] * 8 + specs,
            scratch_shapes=scratch,
        ),
        compiler_params=pltpu.CompilerParams(vmem_limit_bytes=VMEM),
        cost_estimate=cost(22 if half else 14),
        name="mlp_b" if half else "mlp_a",
    )(me, core, *xs, *gs, *weights, vec, bias_in, *saved, *after)
    return outs[:4], outs[4:8], outs[8:]


def update_kernel(me_ref, *refs):
    k = pl.program_id(0)
    state_ref, mask_ref, scale_ref, out_ref, held = refs[8:]

    def take(early, late):
        held[:HR] = early[...]
        held[HR:] = late[...]

    for i in range(4):
        pl.when(k == i)(lambda i=i: take(refs[i], refs[4 + i]))
    branch = jnp.swapaxes(held[...].astype(F32) * scale_ref[...][None], 0, 1)[:LC]
    mask = mask_ref[...].astype(F32)
    out_ref[...] = (mask[None] * (state_ref[...].astype(F32) + branch)).astype(BF)


def update(me, pieces, state, sea_mask, scale):
    whole = pl.BlockSpec((HR, CP, LANES), lambda i, me: (0, 0, 0), pipeline_mode=pl.Buffered(1))
    return pl.pallas_call(
        update_kernel,
        out_shape=jax.ShapeDtypeStruct((LC, ROWS, LANES), BF),
        grid_spec=pltpu.PrefetchScalarGridSpec(
            num_scalar_prefetch=1,
            grid=(4,),
            in_specs=[whole] * 8
            + [
                pl.BlockSpec((LC, QR, LANES), lambda i, me: (0, me[0] ^ i, 0)),
                pl.BlockSpec((QR, LANES), lambda i, me: (me[0] ^ i, 0)),
                pl.BlockSpec((CP, 1), lambda i, me: (0, 0)),
            ],
            out_specs=pl.BlockSpec((LC, QR, LANES), lambda i, me: (0, me[0] ^ i, 0)),
            scratch_shapes=[pltpu.VMEM((QR, CP, LANES), BF)],
        ),
        compiler_params=pltpu.CompilerParams(vmem_limit_bytes=VMEM),
        cost_estimate=cost(4.4),
        name="update",
    )(me, *pieces, state, sea_mask, scale)


def weights_kernel(one, two, pad, one_out, one_t, two_out, two_t):
    for source, out, turned in ((one, one_out, one_t), (two, two_out, two_t)):
        padded = dotg(pad[...], source[...], 0, 0)
        out[...] = padded.astype(BF)
        turned[...] = padded.T.astype(BF)


def padded_weights(one, two, pad):
    flat = jax.ShapeDtypeStruct((4 * CP, HID), BF)
    turned = jax.ShapeDtypeStruct((HID, 4 * CP), BF)
    return pl.pallas_call(
        weights_kernel,
        out_shape=[flat, turned, flat, turned],
        grid=(1,),
        in_specs=[full((C, HID)), full((C, HID)), full((C, 4 * CP))],
        out_specs=[full(x.shape) for x in (flat, turned, flat, turned)],
        compiler_params=pltpu.CompilerParams(vmem_limit_bytes=VMEM),
        cost_estimate=cost(5),
        name="padded_weights",
    )(one, two, pad)


def tap_patterns(kernel):
    lane = jnp.arange(4 * LANES)
    tile, pos = lane // LANES, lane % LANES
    away = jnp.where(pos % ROWS < ROWS // 2, pos % ROWS, pos % ROWS - ROWS)
    side = ((pos - away) // ROWS) % 2
    col = 2 * tile + side
    tap = jnp.where((jnp.abs(away) <= RIM) & (col < KW), (away + RIM) * KW + col, -1)
    pick = (jnp.arange(KW * KW)[:, None] == tap[None, :]).astype(BF)
    return jnp.dot(kernel.astype(BF), pick, preferred_element_type=F32).reshape(LC, 4, LANES)


def edge_picks():
    row = jnp.arange(8)[:, None]
    lane = jnp.arange(LANES)[None, :]
    head = ((row < RIM) & (lane == row)).astype(BF)
    tail = ((row < RIM) & (lane == LANES - RIM + row)).astype(BF)
    return head, tail


def edge_kernel(cells, pick, *refs):
    refs[-1][...] = dotg(pick[...], cells[...], 1, 1).astype(BF)


def edge(cells2d, pick, after=()):
    return pl.pallas_call(
        edge_kernel,
        out_shape=jax.ShapeDtypeStruct((8, cells2d.shape[0]), BF),
        grid=(1,),
        in_specs=[full(cells2d.shape), full(pick.shape)]
        + [pl.BlockSpec(memory_space=pl.ANY)] * len(after),
        out_specs=full((8, cells2d.shape[0])),
        compiler_params=pltpu.CompilerParams(vmem_limit_bytes=VMEM),
        cost_estimate=cost(1),
        name="edge",
    )(cells2d, pick, *after)


def piece_edges_kernel(pick, *refs):
    first, last = refs[8:]
    for i in range(8):
        cells = refs[i][...].reshape(HR * CP, LANES)
        both = dotg(pick[...], cells, 1, 1).astype(BF)
        first[i] = both[:8]
        last[i] = both[8:]


def piece_edges(picks, pieces):
    half = pl.BlockSpec((QR // 2, CP, LANES), lambda i: (0, 0, 0))
    whole = pl.BlockSpec((8, 8, HR * CP), lambda i: (0, 0, 0))
    out = jax.ShapeDtypeStruct((8, 8, HR * CP), BF)
    return pl.pallas_call(
        piece_edges_kernel,
        out_shape=[out, out],
        grid=(1,),
        in_specs=[pl.BlockSpec((16, LANES), lambda i: (0, 0))] + [half] * 8,
        out_specs=[whole] * 2,
        compiler_params=pltpu.CompilerParams(vmem_limit_bytes=VMEM),
        cost_estimate=cost(2),
        name="piece_edges",
    )(picks, *pieces)


def piece_rims_kernel(pick, first, last, out):
    for i in range(8):
        both = jnp.concatenate([first[i], last[i]], axis=0)
        out[i] = dotg(both, pick[...], 0, 0).astype(BF).reshape(HR, CP, LANES)


def piece_rims(picks, first, last):
    return pl.pallas_call(
        piece_rims_kernel,
        out_shape=jax.ShapeDtypeStruct((8, HR, CP, LANES), BF),
        grid=(1,),
        in_specs=[full((16, LANES)), full((8, 8, HR * CP)), full((8, 8, HR * CP))],
        out_specs=full((8, HR, CP, LANES)),
        compiler_params=pltpu.CompilerParams(vmem_limit_bytes=VMEM),
        cost_estimate=cost(2),
        name="piece_rims",
    )(picks, lon_shift(first, -1), lon_shift(last, 1))


def rims(first, last):
    both = jnp.concatenate([lon_shift(first, -1), lon_shift(last, 1)], 0)
    return dotg(both, jnp.concatenate(edge_picks(), 0), 0, 0).astype(BF)


PLANES = [[16 * half + i for i in range(16)] for half in range(2)]


def plane_exchange(pieces):
    return lax.all_to_all(pieces, "lon", 0, 0, axis_index_groups=PLANES)


def total_kernel(*refs):
    total = refs[0][0].astype(F32)
    for i in range(1, 16):
        total = total + refs[0][i].astype(F32)
    refs[-1][...] = total.astype(BF)


def plane_total(pieces, after):
    return pl.pallas_call(
        total_kernel,
        out_shape=jax.ShapeDtypeStruct((PIECE, LANES), BF),
        grid=(1,),
        in_specs=[full((16, PIECE, LANES))] + [pl.BlockSpec(memory_space=pl.ANY)] * len(after),
        out_specs=full((PIECE, LANES)),
        compiler_params=pltpu.CompilerParams(vmem_limit_bytes=VMEM),
        cost_estimate=cost(1.2),
        name="plane_total",
    )(pieces, *after)


def copies_kernel(part, out):
    for i in range(16):
        out[i] = part[...]


def plane_copies(part):
    return pl.pallas_call(
        copies_kernel,
        out_shape=jax.ShapeDtypeStruct((16, PIECE, LANES), BF),
        grid=(1,),
        in_specs=[full((PIECE, LANES))],
        out_specs=full((16, PIECE, LANES)),
        compiler_params=pltpu.CompilerParams(vmem_limit_bytes=VMEM),
        cost_estimate=cost(1),
        name="plane_copies",
    )(part)


def reduce_gradients(keep, send, late):
    mine = (keep.astype(F32) + ch_swap(send, 1).astype(F32)).astype(BF)
    mine = plane_exchange(mine.reshape(16, PIECE, LANES))
    wire = plane_total(mine, late)
    part = (
        (wire.astype(F32) + lon_swap(wire, 16).astype(F32))
        + (ch_swap(wire, 2).astype(F32) + both_swap(wire).astype(F32))
    ).astype(BF)
    return plane_exchange(plane_copies(part)).reshape(WIRE, LANES)


def finish_kernel(core_ref, own, other, pad, grad_in, grad_out, held):
    core = core_ref[0]
    for wire, slot in ((own, core), (other, 1 - core)):
        for t in range(3):
            held[slot, :, t * LANES : (t + 1) * LANES] = wire[t * HID : (t + 1) * HID, :]
        rest = wire[3 * HID : 3 * HID + 400, :]
        for q in range(4):
            held[slot, q * 400 : (q + 1) * 400, 3 * LANES :] = rest[:, q * 32 : (q + 1) * 32]
    factor = 1.0 / math.sqrt(ROWS * LANES * 32)
    grad_in[...] = dotg(pad[...], held[0], 1, 1) * factor
    grad_out[...] = dotg(pad[...], held[1], 1, 1) * factor


def finish(core, own, other, pad):
    return pl.pallas_call(
        finish_kernel,
        out_shape=[
            jax.ShapeDtypeStruct((C, HID), F32),
            jax.ShapeDtypeStruct((C, HID), F32),
        ],
        grid=(1,),
        in_specs=[
            pl.BlockSpec(memory_space=pltpu.SMEM),
            full((WIRE, LANES)),
            full((WIRE, LANES)),
            full((C, 4 * CP)),
        ],
        out_specs=[full((C, HID))] * 2,
        scratch_shapes=[pltpu.VMEM((2, HID, 4 * CP), BF)],
        compiler_params=pltpu.CompilerParams(vmem_limit_bytes=VMEM),
        cost_estimate=cost(6),
        name="finish",
    )(core, own, other, pad)


def both_swap(x):
    return lax.ppermute(x, ("lon", "ch"), [(i, i ^ (16 * 4 + 2)) for i in range(128)])


def body(
    ocean_state,
    sea_mask,
    kernel,
    conv_bias,
    norm_gain,
    norm_bias,
    weight_in,
    bias_in,
    weight_out,
    bias_out,
    layer_scale,
    cotangent,
):
    ch = lax.axis_index("ch")
    me = ch.reshape(1)
    core = (ch & 1).reshape(1)
    scale = jnp.pad(layer_scale, (0, CP - LC)).reshape(CP, 1)

    head, tail = edge_picks()
    state2d = ocean_state.reshape(LC * ROWS, LANES)
    sent = {}
    first = edge(state2d, head)
    sent[2] = branch_share(me, cotangent, sea_mask, scale, 2, (first,))
    last = edge(state2d, tail, (sent[2],))
    sent[3] = branch_share(me, cotangent, sea_mask, scale, 3, (last,))
    sent[1] = branch_share(me, cotangent, sea_mask, scale, 1, (sent[3],))
    sent[0] = branch_share(me, cotangent, sea_mask, scale, 0, (sent[1],))
    gs = [sent[0]] + [ch_swap(sent[k], k) for k in (1, 2, 3)]

    chan = jnp.arange(C)
    padded = jnp.arange(4 * CP)
    pad = ((chan // LC * CP + chan % LC)[:, None] == padded[None, :]).astype(BF)
    pad_own = (((chan // LC ^ ch) * CP + chan % LC)[:, None] == padded[None, :]).astype(BF)
    win, win_t, wout_t, wout = padded_weights(weight_in, weight_out.T, pad_own)
    vec = jnp.stack([norm_gain, norm_bias, bias_out], 1).reshape(4, LC, 3)
    vec = jnp.pad(vec, ((0, 0), (0, CP - LC), (0, 0)))
    vec = jnp.concatenate([lax.dynamic_index_in_dim(vec, ch ^ k, 0, False) for k in range(4)], 0)

    state_rim = rims(first, last).reshape(LC, ROWS, LANES)
    bias = jnp.broadcast_to(conv_bias[:, None, None], (LC, 1, LANES))
    conv = conv_forward(me, ocean_state, state_rim, tap_patterns(kernel), bias)
    xs = [
        [conv[4 * half]] + [ch_swap(conv[4 * half + k], k) for k in (1, 2, 3)] for half in (0, 1)
    ]

    weights = (win_t, win, wout, wout_t)
    bias_rows = bias_in.reshape(HID, 1)
    grad_a, branch_a, (hid_a, cells_a) = mlp(0, me, core, xs[0], gs, weights, vec, bias_rows)
    saved = (hid_a, cells_a.reshape(2, 4 * CP, 2 * CELLS))
    grad_b, branch_b, (keep, send) = mlp(
        1, me, core, xs[1], gs, weights, vec, bias_rows, saved, grad_a[:1]
    )
    grad_a = [grad_a[0]] + [ch_swap(grad_a[k], k) for k in (1, 2, 3)]
    branch_a = [branch_a[0]] + [ch_swap(branch_a[k], k) for k in (1, 2, 3)]
    keep, send, grad_a, branch_a = lax.optimization_barrier((keep, send, grad_a, branch_a))
    grad_b = [grad_b[0]] + [ch_swap(grad_b[k], k) for k in (1, 2, 3)]
    branch_b = [branch_b[0]] + [ch_swap(branch_b[k], k) for k in (1, 2, 3)]
    grads, branches = grad_a + grad_b, branch_a + branch_b

    picks = jnp.concatenate([head, tail], 0)
    grad_rims = piece_rims(picks, *piece_edges(picks, grads))
    own = reduce_gradients(keep, send, grads[5:] + branches[5:])

    grad_state = conv_backward(
        me,
        grads,
        grad_rims,
        tap_patterns(kernel[:, ::-1]),
        cotangent,
        sea_mask,
    )
    updated = update(me, branches, ocean_state, sea_mask, scale)
    own, grad_state, updated = lax.optimization_barrier((own, grad_state, updated))
    grad_in, grad_out = finish(core, own, ch_swap(own, 1), pad)
    return updated, grad_state, grad_in, grad_out.T


def solution(mesh):
    return jax.shard_map(
        body,
        mesh=mesh,
        in_specs=(
            P("ch", None, "lon"),
            P(None, "lon"),
            P("ch", None),
            P("ch"),
            P(),
            P(),
            P(),
            P(),
            P(),
            P(),
            P("ch"),
            P("ch", None, "lon"),
        ),
        out_specs=(P("ch", None, "lon"), P("ch", None, "lon"), P(), P()),
        check_vma=False,
    )
```

```python
import functools
import math

import jax
import jax.numpy as jnp
from jax import lax
from jax.experimental import pallas as pl
from jax.experimental.pallas import tpu as pltpu
from jax.sharding import PartitionSpec as P

KW = 7
RIM = KW // 2
C = 400
HID = 1600
ROWS = 64
LANES = 128
LC = 100
CP = 104
QR = 16
HR = 8
GROUP = 8
VMEM = 63 << 20
BF = jnp.bfloat16
F32 = jnp.float32

root_coef = math.sqrt(2.0 / math.pi)
cubic_coef = 0.044715
norm_eps = 1e-06


def dotg(a, b, ca, cb):
    return lax.dot_general(a, b, (((ca,), (cb,)), ((), ())), preferred_element_type=F32)


def cost(micros):
    return pl.CostEstimate(flops=0, bytes_accessed=int(micros * 3.3e6), transcendentals=0)


def full(shape):
    return pl.BlockSpec(shape, lambda *i: (0,) * len(shape), pipeline_mode=pl.Buffered(1))


def ch_swap(x, k):
    return lax.ppermute(x, "ch", [(i, i ^ k) for i in range(4)])


def lon_shift(x, d):
    return lax.ppermute(x, "lon", [(i, (i + d) % 32) for i in range(32)])


def lon_swap(x, k):
    return lax.ppermute(x, "lon", [(i, i ^ k) for i in range(32)])


def share_kernel(me_ref, cot_ref, mask_ref, scale_ref, *refs):
    out_ref = refs[-1]
    cells = cot_ref[...].astype(F32)
    cells = jnp.concatenate([cells, jnp.zeros((CP - LC, QR, LANES), F32)], axis=0)
    cells = jnp.swapaxes(cells, 0, 1)
    mask = mask_ref[...].astype(F32)
    out_ref[...] = ((cells * mask[:, None, :]) * scale_ref[...][None]).astype(BF)


def branch_share(me, cotangent, sea_mask, scale, k, after):
    return pl.pallas_call(
        share_kernel,
        out_shape=jax.ShapeDtypeStruct((QR, CP, LANES), BF),
        grid_spec=pltpu.PrefetchScalarGridSpec(
            num_scalar_prefetch=1,
            grid=(1,),
            in_specs=[
                pl.BlockSpec((LC, QR, LANES), lambda i, me: (0, me[0] ^ k, 0)),
                pl.BlockSpec((QR, LANES), lambda i, me: (me[0] ^ k, 0)),
                pl.BlockSpec((CP, 1), lambda i, me: (0, 0)),
            ]
            + [pl.BlockSpec(memory_space=pl.ANY)] * len(after),
            out_specs=pl.BlockSpec((QR, CP, LANES), lambda i, me: (0, 0, 0)),
        ),
        compiler_params=pltpu.CompilerParams(vmem_limit_bytes=32 << 20),
        cost_estimate=cost(1.2),
        name="branch_share",
    )(me, cotangent, sea_mask, scale, *after)


def conv_channel(cells, rim, pattern, lane, band):
    moved = []
    for off in range(-RIM, RIM + 1):
        if off == 0:
            moved.append(cells.astype(BF))
        else:
            edge = lane < off if off > 0 else lane >= LANES + off
            moved.append(pltpu.roll(jnp.where(edge, rim, cells), (-off) % LANES, 1).astype(BF))
    stacked = jnp.concatenate(moved, axis=0)
    tiles = []
    for t in range(4):
        row = jnp.broadcast_to(pattern[t : t + 1, :], (ROWS, LANES))
        row = pltpu.roll(row, 0, 1, stride=1, stride_axis=0)
        tiles.append(jnp.where(band, row, 0.0).astype(BF))
    banded = jnp.concatenate(tiles, axis=1)[:, : KW * ROWS]
    return jnp.dot(banded, stacked, preferred_element_type=F32)


def masks():
    lane = lax.broadcasted_iota(jnp.int32, (ROWS, LANES), 1)
    row = lax.broadcasted_iota(jnp.int32, (ROWS, LANES), 0)
    away = (lane & (ROWS - 1)) - row
    return lane, (away >= -RIM) & (away <= RIM)


def forward_kernel(me_ref, state_ref, rim_ref, pat_ref, bias_ref, *refs):
    held = refs[-1]
    step = pl.program_id(0)
    lane, band = masks()
    outs = []
    for c in range(GROUP):
        total = conv_channel(
            state_ref[c].astype(F32), rim_ref[c].astype(F32), pat_ref[c], lane, band
        )
        total = total + bias_ref[c]
        outs.append(jnp.where(step * GROUP + c < LC, total, 0.0))
    held[...] = jnp.swapaxes(jnp.stack(outs, 0), 0, 1).reshape(4, QR, GROUP, LANES)
    me = me_ref[0]
    for k in range(4):
        share = held[me ^ k].astype(BF)
        refs[k][...] = share[:HR]
        refs[4 + k][...] = share[HR:]


def conv_forward(me, state, rim, pattern, bias):
    share = jax.ShapeDtypeStruct((HR, CP, LANES), BF)
    return pl.pallas_call(
        forward_kernel,
        out_shape=[share] * 8,
        grid_spec=pltpu.PrefetchScalarGridSpec(
            num_scalar_prefetch=1,
            grid=(CP // GROUP,),
            in_specs=[
                pl.BlockSpec((GROUP, ROWS, LANES), lambda i, me: (i, 0, 0)),
                pl.BlockSpec((GROUP, ROWS, LANES), lambda i, me: (i, 0, 0)),
                pl.BlockSpec((GROUP, 4, LANES), lambda i, me: (i, 0, 0)),
                pl.BlockSpec((GROUP, 1, LANES), lambda i, me: (i, 0, 0)),
            ],
            out_specs=[pl.BlockSpec((HR, GROUP, LANES), lambda i, me: (0, i, 0))] * 8,
            scratch_shapes=[pltpu.VMEM((4, QR, GROUP, LANES), F32)],
        ),
        compiler_params=pltpu.CompilerParams(vmem_limit_bytes=32 << 20),
        cost_estimate=cost(9),
        name="conv_forward",
    )(me, state, rim, pattern, bias)


def backward_kernel(me_ref, *refs):
    pieces = refs[:8]
    rims_in, pat_ref, cot_ref, mask_ref, out_ref, held, held_rim = refs[8:]
    lane, band = masks()
    me = me_ref[0]
    for k in range(4):
        held[me ^ k, :HR] = pieces[k][...].astype(F32)
        held[me ^ k, HR:] = pieces[4 + k][...].astype(F32)
        held_rim[me ^ k, :HR] = rims_in[k].astype(F32)
        held_rim[me ^ k, HR:] = rims_in[4 + k].astype(F32)
    cells = jnp.swapaxes(held[...].reshape(ROWS, GROUP, LANES), 0, 1)
    rims = jnp.swapaxes(held_rim[...].reshape(ROWS, GROUP, LANES), 0, 1)
    mask = mask_ref[...].astype(F32)
    for c in range(GROUP):
        total = conv_channel(cells[c], rims[c], pat_ref[c], lane, band)
        out_ref[c] = (cot_ref[c].astype(F32) * mask + total).astype(BF)


def conv_backward(me, pieces, rims, pattern, cotangent, sea_mask):
    return pl.pallas_call(
        backward_kernel,
        out_shape=jax.ShapeDtypeStruct((LC, ROWS, LANES), BF),
        grid_spec=pltpu.PrefetchScalarGridSpec(
            num_scalar_prefetch=1,
            grid=(CP // GROUP,),
            in_specs=[pl.BlockSpec((HR, GROUP, LANES), lambda i, me: (0, i, 0))] * 8
            + [
                pl.BlockSpec((8, HR, GROUP, LANES), lambda i, me: (0, 0, i, 0)),
                pl.BlockSpec((GROUP, 4, LANES), lambda i, me: (i, 0, 0)),
                pl.BlockSpec((GROUP, ROWS, LANES), lambda i, me: (i, 0, 0)),
                pl.BlockSpec((ROWS, LANES), lambda i, me: (0, 0)),
            ],
            out_specs=pl.BlockSpec((GROUP, ROWS, LANES), lambda i, me: (i, 0, 0)),
            scratch_shapes=[pltpu.VMEM((4, QR, GROUP, LANES), F32)] * 2,
        ),
        compiler_params=pltpu.CompilerParams(vmem_limit_bytes=32 << 20),
        cost_estimate=cost(10),
        name="conv_backward",
    )(me, *pieces, rims, pattern, cotangent, sea_mask)


SUB = 4
CELLS = SUB * LANES
HT = 400
PIECE = 328
WIRE = 16 * PIECE


def mlp_kernel(half, me_ref, core_ref, *refs):
    xs, gs = refs[:4], refs[4:8]
    win_t, win, wout, wout_t, vec, bias_in = refs[8:14]
    if half:
        hid_in, cells_in = refs[14:16]
        grad_out, branch_out, wires = refs[17:21], refs[21:25], refs[25:27]
        hidden, cells, hid_a, cells_a, held, sems = refs[27:]
        copies = (
            pltpu.make_async_copy(hid_in, hid_a, sems.at[0]),
            pltpu.make_async_copy(cells_in, cells_a, sems.at[1]),
        )
    else:
        grad_out, branch_out = refs[14:18], refs[18:22]
        hidden, cells = refs[22:]
    step = pl.program_id(0)
    me = me_ref[0]
    if half:

        @pl.when(step == 0)
        def _():
            for copy in copies:
                copy.start()

        lanes = pl.ds(pl.multiple_of(step * CELLS, CELLS), CELLS)
    else:
        lanes = slice(0, CELLS)

    def gather(pieces):
        return jnp.concatenate(
            [
                jnp.concatenate([p[r].astype(F32) for r in range(SUB)], axis=1)
                for p in pieces
            ],
            axis=0,
        )

    gain = vec[:, 0:1]
    values = gather(xs)
    mean_val = jnp.sum(values, axis=0, keepdims=True) / C
    square = jnp.sum(values * values, axis=0, keepdims=True) / C
    inv_std = lax.rsqrt(square - mean_val * mean_val + norm_eps)
    normed = (values - mean_val) * inv_std * gain + vec[:, 1:2]
    grads = gather(gs)
    for k in range(4):
        rows = slice(k * CP, (k + 1) * CP)
        cells[0, me ^ k, :, lanes] = normed[rows].astype(cells.dtype)
        cells[1, me ^ k, :, lanes] = grads[rows].astype(cells.dtype)
    normed, grads = normed.astype(BF), grads.astype(BF)
    for t in range(HID // HT):
        rows = slice(t * HT, (t + 1) * HT)
        pre = jnp.dot(win_t[rows, :], normed, preferred_element_type=F32) + bias_in[rows, :]
        gact = jnp.dot(wout[rows, :], grads, preferred_element_type=F32)
        sq = pre * pre
        tangent = jnp.tanh(pre * (root_coef + (root_coef * cubic_coef) * sq))
        side = 0.5 + 0.5 * tangent
        value = pre * side
        slope = side + value * (1.0 - side) * (
            2.0 * root_coef + (6.0 * root_coef * cubic_coef) * sq
        )
        hidden[0, rows, lanes] = (gact * slope).astype(BF)
        hidden[1, rows, lanes] = value.astype(BF)
    x_grad = jnp.dot(win[...], hidden[0, :, lanes], preferred_element_type=F32) * gain
    centred = (values - mean_val) * inv_std
    first = jnp.sum(x_grad, axis=0, keepdims=True) / C
    second = jnp.sum(x_grad * centred, axis=0, keepdims=True) / C
    x_grad = inv_std * (x_grad - first - centred * second)
    branch = jnp.dot(wout_t[...], hidden[1, :, lanes], preferred_element_type=F32)
    branch = branch + vec[:, 2:3]
    for k in range(4):
        for r in range(SUB):
            here = slice(r * LANES, (r + 1) * LANES)
            grad_out[k][r] = x_grad[k * CP : (k + 1) * CP, here].astype(BF)
            branch_out[k][r] = branch[k * CP : (k + 1) * CP, here].astype(BF)
    if not half:
        return

    @pl.when(step == 1)
    def _():
        for copy in copies:
            copy.wait()
        core = core_ref[0]
        for out, slot in ((wires[0], core), (wires[1], 1 - core)):
            cells_b = cells[slot].reshape(4 * CP, 2 * CELLS).astype(BF)
            held[...] = dotg(hid_a[slot], cells_a[slot], 1, 1) + dotg(hidden[slot], cells_b, 1, 1)
            for t in range(3):
                out[t * HID : (t + 1) * HID, :] = held[:, t * LANES : (t + 1) * LANES].astype(BF)
            rest = [held[q * 400 : (q + 1) * 400, 3 * LANES :] for q in range(4)]
            out[3 * HID : 3 * HID + 400, :] = jnp.concatenate(rest, axis=1).astype(BF)
            out[3 * HID + 400 :, :] = jnp.zeros((WIRE - 3 * HID - 400, LANES), BF)


def mlp(half, me, core, xs, gs, weights, vec, bias_in, saved=(), after=()):
    any_space = pl.BlockSpec(memory_space=pl.ANY)

    def whole(shape):
        return pl.BlockSpec(
            shape, lambda i, me, core: (0,) * len(shape), pipeline_mode=pl.Buffered(1)
        )

    piece = pl.BlockSpec((SUB, CP, LANES), lambda i, me, core: (i, 0, 0))
    later = pl.BlockSpec((SUB, CP, LANES), lambda i, me, core: (2 * half + i, 0, 0))
    if half:
        shapes = [jax.ShapeDtypeStruct((WIRE, LANES), BF)] * 2
        specs = [whole((WIRE, LANES))] * 2
        scratch = [
            pltpu.VMEM((2, HID, 2 * CELLS), BF),
            pltpu.VMEM((2, 4, CP, 2 * CELLS), F32),
            pltpu.VMEM((2, HID, 2 * CELLS), BF),
            pltpu.VMEM((2, 4 * CP, 2 * CELLS), BF),
            pltpu.VMEM((HID, 4 * CP), F32),
            pltpu.SemaphoreType.DMA((2,)),
        ]
    else:
        shapes = [
            jax.ShapeDtypeStruct((2, HID, 2 * CELLS), BF),
            jax.ShapeDtypeStruct((2, 4, CP, 2 * CELLS), BF),
        ]
        specs = [
            pl.BlockSpec((2, HID, CELLS), lambda i, me, core: (0, 0, i)),
            pl.BlockSpec((2, 4, CP, CELLS), lambda i, me, core: (0, 0, 0, i)),
        ]
        scratch = []
    outs = pl.pallas_call(
        functools.partial(mlp_kernel, half),
        out_shape=[jax.ShapeDtypeStruct((HR, CP, LANES), BF)] * 8 + shapes,
        grid_spec=pltpu.PrefetchScalarGridSpec(
            num_scalar_prefetch=2,
            grid=(2,),
            in_specs=[piece] * 4
            + [later] * 4
            + [
                whole((HID, 4 * CP)),
                whole((4 * CP, HID)),
                whole((HID, 4 * CP)),
                whole((4 * CP, HID)),
                whole((4 * CP, 3)),
                whole((HID, 1)),
            ]
            + [any_space] * (len(saved) + len(after)),
            out_specs=[piece] * 8 + specs,
            scratch_shapes=scratch,
        ),
        compiler_params=pltpu.CompilerParams(vmem_limit_bytes=VMEM),
        cost_estimate=cost(22 if half else 14),
        name="mlp_b" if half else "mlp_a",
    )(me, core, *xs, *gs, *weights, vec, bias_in, *saved, *after)
    return outs[:4], outs[4:8], outs[8:]


def update_kernel(me_ref, *refs):
    k = pl.program_id(0)
    state_ref, mask_ref, scale_ref, out_ref, held = refs[8:]

    def take(early, late):
        held[:HR] = early[...]
        held[HR:] = late[...]

    for i in range(4):
        pl.when(k == i)(lambda i=i: take(refs[i], refs[4 + i]))
    branch = jnp.swapaxes(held[...].astype(F32) * scale_ref[...][None], 0, 1)[:LC]
    mask = mask_ref[...].astype(F32)
    out_ref[...] = (mask[None] * (state_ref[...].astype(F32) + branch)).astype(BF)


def update(me, pieces, state, sea_mask, scale):
    whole = pl.BlockSpec((HR, CP, LANES), lambda i, me: (0, 0, 0), pipeline_mode=pl.Buffered(1))
    return pl.pallas_call(
        update_kernel,
        out_shape=jax.ShapeDtypeStruct((LC, ROWS, LANES), BF),
        grid_spec=pltpu.PrefetchScalarGridSpec(
            num_scalar_prefetch=1,
            grid=(4,),
            in_specs=[whole] * 8
            + [
                pl.BlockSpec((LC, QR, LANES), lambda i, me: (0, me[0] ^ i, 0)),
                pl.BlockSpec((QR, LANES), lambda i, me: (me[0] ^ i, 0)),
                pl.BlockSpec((CP, 1), lambda i, me: (0, 0)),
            ],
            out_specs=pl.BlockSpec((LC, QR, LANES), lambda i, me: (0, me[0] ^ i, 0)),
            scratch_shapes=[pltpu.VMEM((QR, CP, LANES), BF)],
        ),
        compiler_params=pltpu.CompilerParams(vmem_limit_bytes=32 << 20),
        cost_estimate=cost(4.4),
        name="update",
    )(me, *pieces, state, sea_mask, scale)


def weights_kernel(one, two, pad, one_out, one_t, two_out, two_t):
    for source, out, turned in ((one, one_out, one_t), (two, two_out, two_t)):
        padded = dotg(pad[...], source[...], 0, 0)
        out[...] = padded.astype(BF)
        turned[...] = padded.T.astype(BF)


def padded_weights(one, two, pad):
    flat = jax.ShapeDtypeStruct((4 * CP, HID), BF)
    turned = jax.ShapeDtypeStruct((HID, 4 * CP), BF)
    return pl.pallas_call(
        weights_kernel,
        out_shape=[flat, turned, flat, turned],
        grid=(1,),
        in_specs=[full((C, HID)), full((C, HID)), full((C, 4 * CP))],
        out_specs=[full(x.shape) for x in (flat, turned, flat, turned)],
        compiler_params=pltpu.CompilerParams(vmem_limit_bytes=32 << 20),
        cost_estimate=cost(5),
        name="padded_weights",
    )(one, two, pad)


def tap_patterns(kernel):
    lane = jnp.arange(4 * LANES)
    tile, pos = lane // LANES, lane % LANES
    away = jnp.where(pos % ROWS < ROWS // 2, pos % ROWS, pos % ROWS - ROWS)
    side = ((pos - away) // ROWS) % 2
    col = 2 * tile + side
    tap = jnp.where((jnp.abs(away) <= RIM) & (col < KW), (away + RIM) * KW + col, -1)
    pick = (jnp.arange(KW * KW)[:, None] == tap[None, :]).astype(BF)
    return jnp.dot(kernel.astype(BF), pick, preferred_element_type=F32).reshape(LC, 4, LANES)


def edge_picks():
    row = jnp.arange(8)[:, None]
    lane = jnp.arange(LANES)[None, :]
    head = ((row < RIM) & (lane == row)).astype(BF)
    tail = ((row < RIM) & (lane == LANES - RIM + row)).astype(BF)
    return head, tail


def edge_kernel(cells, pick, *refs):
    refs[-1][...] = dotg(pick[...], cells[...], 1, 1).astype(BF)


def edge(cells2d, pick, after=()):
    return pl.pallas_call(
        edge_kernel,
        out_shape=jax.ShapeDtypeStruct((8, cells2d.shape[0]), BF),
        grid=(1,),
        in_specs=[full(cells2d.shape), full(pick.shape)]
        + [pl.BlockSpec(memory_space=pl.ANY)] * len(after),
        out_specs=full((8, cells2d.shape[0])),
        compiler_params=pltpu.CompilerParams(vmem_limit_bytes=32 << 20),
        cost_estimate=cost(1),
        name="edge",
    )(cells2d, pick, *after)


def piece_edges_kernel(pick, *refs):
    first, last = refs[8:]
    for i in range(8):
        cells = refs[i][...].reshape(HR * CP, LANES)
        both = dotg(pick[...], cells, 1, 1).astype(BF)
        first[i] = both[:8]
        last[i] = both[8:]


def piece_edges(picks, pieces):
    half = pl.BlockSpec((QR // 2, CP, LANES), lambda i: (0, 0, 0))
    whole = pl.BlockSpec((8, 8, HR * CP), lambda i: (0, 0, 0))
    out = jax.ShapeDtypeStruct((8, 8, HR * CP), BF)
    return pl.pallas_call(
        piece_edges_kernel,
        out_shape=[out, out],
        grid=(1,),
        in_specs=[pl.BlockSpec((16, LANES), lambda i: (0, 0))] + [half] * 8,
        out_specs=[whole] * 2,
        compiler_params=pltpu.CompilerParams(vmem_limit_bytes=32 << 20),
        cost_estimate=cost(2),
        name="piece_edges",
    )(picks, *pieces)


def piece_rims_kernel(pick, first, last, out):
    for i in range(8):
        both = jnp.concatenate([first[i], last[i]], axis=0)
        out[i] = dotg(both, pick[...], 0, 0).astype(BF).reshape(HR, CP, LANES)


def piece_rims(picks, first, last):
    return pl.pallas_call(
        piece_rims_kernel,
        out_shape=jax.ShapeDtypeStruct((8, HR, CP, LANES), BF),
        grid=(1,),
        in_specs=[full((16, LANES)), full((8, 8, HR * CP)), full((8, 8, HR * CP))],
        out_specs=full((8, HR, CP, LANES)),
        compiler_params=pltpu.CompilerParams(vmem_limit_bytes=32 << 20),
        cost_estimate=cost(2),
        name="piece_rims",
    )(picks, first, last)


def rims(first, last):
    both = jnp.concatenate([lon_shift(first, -1), lon_shift(last, 1)], 0)
    return dotg(both, jnp.concatenate(edge_picks(), 0), 0, 0).astype(BF)


PLANES = [[16 * half + i for i in range(16)] for half in range(2)]


def plane_exchange(pieces):
    return lax.all_to_all(pieces, "lon", 0, 0, axis_index_groups=PLANES)


def total_kernel(*refs):
    total = refs[0][0].astype(F32)
    for i in range(1, 16):
        total = total + refs[0][i].astype(F32)
    refs[-1][...] = total.astype(BF)


def plane_total(pieces, after):
    return pl.pallas_call(
        total_kernel,
        out_shape=jax.ShapeDtypeStruct((PIECE, LANES), BF),
        grid=(1,),
        in_specs=[full((16, PIECE, LANES))] + [pl.BlockSpec(memory_space=pl.ANY)] * len(after),
        out_specs=full((PIECE, LANES)),
        compiler_params=pltpu.CompilerParams(vmem_limit_bytes=32 << 20),
        cost_estimate=cost(1.2),
        name="plane_total",
    )(pieces, *after)


def copies_kernel(part, out):
    for i in range(16):
        out[i] = part[...]


def plane_copies(part):
    return pl.pallas_call(
        copies_kernel,
        out_shape=jax.ShapeDtypeStruct((16, PIECE, LANES), BF),
        grid=(1,),
        in_specs=[full((PIECE, LANES))],
        out_specs=full((16, PIECE, LANES)),
        compiler_params=pltpu.CompilerParams(vmem_limit_bytes=32 << 20),
        cost_estimate=cost(1),
        name="plane_copies",
    )(part)


def reduce_gradients(keep, send, late):
    mine = (keep.astype(F32) + ch_swap(send, 1).astype(F32)).astype(BF)
    mine = plane_exchange(mine.reshape(16, PIECE, LANES))
    wire = plane_total(mine, late)
    part = (
        (wire.astype(F32) + lon_swap(wire, 16).astype(F32))
        + (ch_swap(wire, 2).astype(F32) + both_swap(wire).astype(F32))
    ).astype(BF)
    return plane_exchange(plane_copies(part)).reshape(WIRE, LANES)


def finish_kernel(core_ref, own, other, pad, grad_in, grad_out, held):
    core = core_ref[0]
    for wire, slot in ((own, core), (other, 1 - core)):
        for t in range(3):
            held[slot, :, t * LANES : (t + 1) * LANES] = wire[t * HID : (t + 1) * HID, :]
        rest = wire[3 * HID : 3 * HID + 400, :]
        for q in range(4):
            held[slot, q * 400 : (q + 1) * 400, 3 * LANES :] = rest[:, q * 32 : (q + 1) * 32]
    factor = 1.0 / math.sqrt(ROWS * LANES * 32)
    grad_in[...] = dotg(pad[...], held[0], 1, 1) * factor
    grad_out[...] = dotg(pad[...], held[1], 1, 1) * factor


def finish(core, own, other, pad):
    return pl.pallas_call(
        finish_kernel,
        out_shape=[
            jax.ShapeDtypeStruct((C, HID), F32),
            jax.ShapeDtypeStruct((C, HID), F32),
        ],
        grid=(1,),
        in_specs=[
            pl.BlockSpec(memory_space=pltpu.SMEM),
            full((WIRE, LANES)),
            full((WIRE, LANES)),
            full((C, 4 * CP)),
        ],
        out_specs=[full((C, HID))] * 2,
        scratch_shapes=[pltpu.VMEM((2, HID, 4 * CP), BF)],
        compiler_params=pltpu.CompilerParams(vmem_limit_bytes=32 << 20),
        cost_estimate=cost(6),
        name="finish",
    )(core, own, other, pad)


def both_swap(x):
    return lax.ppermute(x, ("lon", "ch"), [(i, i ^ (16 * 4 + 2)) for i in range(128)])


def body(
    ocean_state,
    sea_mask,
    kernel,
    conv_bias,
    norm_gain,
    norm_bias,
    weight_in,
    bias_in,
    weight_out,
    bias_out,
    layer_scale,
    cotangent,
):
    ch = lax.axis_index("ch")
    me = ch.reshape(1)
    core = (ch & 1).reshape(1)
    scale = jnp.pad(layer_scale, (0, CP - LC)).reshape(CP, 1)

    head, tail = edge_picks()
    state2d = ocean_state.reshape(LC * ROWS, LANES)
    sent = {}
    first = edge(state2d, head)
    sent[2] = branch_share(me, cotangent, sea_mask, scale, 2, (first,))
    last = edge(state2d, tail, (sent[2],))
    sent[3] = branch_share(me, cotangent, sea_mask, scale, 3, (last,))
    sent[1] = branch_share(me, cotangent, sea_mask, scale, 1, (sent[3],))
    sent[0] = branch_share(me, cotangent, sea_mask, scale, 0, (sent[1],))
    gs = [sent[0]] + [ch_swap(sent[k], k) for k in (1, 2, 3)]

    chan = jnp.arange(C)
    padded = jnp.arange(4 * CP)
    pad = ((chan // LC * CP + chan % LC)[:, None] == padded[None, :]).astype(BF)
    pad_own = (((chan // LC ^ ch) * CP + chan % LC)[:, None] == padded[None, :]).astype(BF)
    win, win_t, wout_t, wout = padded_weights(weight_in, weight_out.T, pad_own)
    vec = jnp.stack([norm_gain, norm_bias, bias_out], 1).reshape(4, LC, 3)
    vec = jnp.pad(vec, ((0, 0), (0, CP - LC), (0, 0)))
    vec = jnp.concatenate([lax.dynamic_index_in_dim(vec, ch ^ k, 0, False) for k in range(4)], 0)

    state_rim = rims(first, last).reshape(LC, ROWS, LANES)
    bias = jnp.broadcast_to(conv_bias[:, None, None], (LC, 1, LANES))
    conv = conv_forward(me, ocean_state, state_rim, tap_patterns(kernel), bias)
    xs = [
        [conv[4 * half]] + [ch_swap(conv[4 * half + k], k) for k in (1, 2, 3)] for half in (0, 1)
    ]

    weights = (win_t, win, wout, wout_t)
    bias_rows = bias_in.reshape(HID, 1)
    grad_a, branch_a, (hid_a, cells_a) = mlp(0, me, core, xs[0], gs, weights, vec, bias_rows)
    saved = (hid_a, cells_a.reshape(2, 4 * CP, 2 * CELLS))
    grad_b, branch_b, (keep, send) = mlp(
        1, me, core, xs[1], gs, weights, vec, bias_rows, saved, grad_a[:1]
    )
    grad_a = [grad_a[0]] + [ch_swap(grad_a[k], k) for k in (1, 2, 3)]
    branch_a = [branch_a[0]] + [ch_swap(branch_a[k], k) for k in (1, 2, 3)]
    keep, send, grad_a, branch_a = lax.optimization_barrier((keep, send, grad_a, branch_a))
    grad_b = [grad_b[0]] + [ch_swap(grad_b[k], k) for k in (1, 2, 3)]
    grads = grad_a + grad_b
    picks = jnp.concatenate([head, tail], 0)
    first, last = piece_edges(picks, grads)
    first, last, branch_b = lax.optimization_barrier((first, last, branch_b))
    branch_b = [branch_b[0]] + [ch_swap(branch_b[k], k) for k in (1, 2, 3)]
    branches = branch_a + branch_b
    from_right, from_left = lon_shift(first, -1), lon_shift(last, 1)
    own = reduce_gradients(keep, send, [from_right, from_left] + branch_b[1:])
    grad_rims = piece_rims(picks, from_right, from_left)

    grad_state = conv_backward(
        me,
        grads,
        grad_rims,
        tap_patterns(kernel[:, ::-1]),
        cotangent,
        sea_mask,
    )
    updated = update(me, branches, ocean_state, sea_mask, scale)
    own, grad_state, updated = lax.optimization_barrier((own, grad_state, updated))
    grad_in, grad_out = finish(core, own, ch_swap(own, 1), pad)
    return updated, grad_state, grad_in, grad_out.T


def solution(mesh):
    return jax.shard_map(
        body,
        mesh=mesh,
        in_specs=(
            P("ch", None, "lon"),
            P(None, "lon"),
            P("ch", None),
            P("ch"),
            P(),
            P(),
            P(),
            P(),
            P(),
            P(),
            P("ch"),
            P("ch", None, "lon"),
        ),
        out_specs=(P("ch", None, "lon"), P("ch", None, "lon"), P(), P()),
        check_vma=False,
    )
```

```python
import functools
import math

import jax
import jax.numpy as jnp
from jax import lax
from jax.experimental import pallas as pl
from jax.experimental.pallas import tpu as pltpu
from jax.sharding import PartitionSpec as P

KW = 7
RIM = KW // 2
C = 400
HID = 1600
ROWS = 64
LANES = 128
LC = 100
CP = 104
QR = 16
HR = 8
GROUP = 8
VMEM = 63 << 20
BF = jnp.bfloat16
F32 = jnp.float32

root_coef = math.sqrt(2.0 / math.pi)
cubic_coef = 0.044715
norm_eps = 1e-06


def dotg(a, b, ca, cb):
    return lax.dot_general(a, b, (((ca,), (cb,)), ((), ())), preferred_element_type=F32)


def cost(micros):
    return pl.CostEstimate(flops=0, bytes_accessed=int(micros * 3.3e6), transcendentals=0)


def full(shape):
    return pl.BlockSpec(shape, lambda *i: (0,) * len(shape), pipeline_mode=pl.Buffered(1))


def ch_swap(x, k):
    return lax.ppermute(x, "ch", [(i, i ^ k) for i in range(4)])


def lon_shift(x, d):
    return lax.ppermute(x, "lon", [(i, (i + d) % 32) for i in range(32)])


def lon_swap(x, k):
    return lax.ppermute(x, "lon", [(i, i ^ k) for i in range(32)])


def share_kernel(me_ref, cot_ref, mask_ref, scale_ref, *refs):
    out_ref = refs[-1]
    cells = cot_ref[...].astype(F32)
    cells = jnp.concatenate([cells, jnp.zeros((CP - LC, QR, LANES), F32)], axis=0)
    cells = jnp.swapaxes(cells, 0, 1)
    mask = mask_ref[...].astype(F32)
    out_ref[...] = ((cells * mask[:, None, :]) * scale_ref[...][None]).astype(BF)


def branch_share(me, cotangent, sea_mask, scale, k, after):
    return pl.pallas_call(
        share_kernel,
        out_shape=jax.ShapeDtypeStruct((QR, CP, LANES), BF),
        grid_spec=pltpu.PrefetchScalarGridSpec(
            num_scalar_prefetch=1,
            grid=(1,),
            in_specs=[
                pl.BlockSpec((LC, QR, LANES), lambda i, me: (0, me[0] ^ k, 0)),
                pl.BlockSpec((QR, LANES), lambda i, me: (me[0] ^ k, 0)),
                pl.BlockSpec((CP, 1), lambda i, me: (0, 0)),
            ]
            + [pl.BlockSpec(memory_space=pl.ANY)] * len(after),
            out_specs=pl.BlockSpec((QR, CP, LANES), lambda i, me: (0, 0, 0)),
        ),
        compiler_params=pltpu.CompilerParams(vmem_limit_bytes=32 << 20),
        cost_estimate=cost(1.2),
        name="branch_share",
    )(me, cotangent, sea_mask, scale, *after)


def conv_channel(cells, rim, pattern, lane, band):
    moved = []
    for off in range(-RIM, RIM + 1):
        if off == 0:
            moved.append(cells.astype(BF))
        else:
            edge = lane < off if off > 0 else lane >= LANES + off
            moved.append(pltpu.roll(jnp.where(edge, rim, cells), (-off) % LANES, 1).astype(BF))
    stacked = jnp.concatenate(moved, axis=0)
    tiles = []
    for t in range(4):
        row = jnp.broadcast_to(pattern[t : t + 1, :], (ROWS, LANES))
        row = pltpu.roll(row, 0, 1, stride=1, stride_axis=0)
        tiles.append(jnp.where(band, row, 0.0).astype(BF))
    banded = jnp.concatenate(tiles, axis=1)[:, : KW * ROWS]
    return jnp.dot(banded, stacked, preferred_element_type=F32)


def masks():
    lane = lax.broadcasted_iota(jnp.int32, (ROWS, LANES), 1)
    row = lax.broadcasted_iota(jnp.int32, (ROWS, LANES), 0)
    away = (lane & (ROWS - 1)) - row
    return lane, (away >= -RIM) & (away <= RIM)


def forward_kernel(me_ref, state_ref, rim_ref, pat_ref, bias_ref, *refs):
    held = refs[-1]
    step = pl.program_id(0)
    lane, band = masks()
    outs = []
    for c in range(GROUP):
        total = conv_channel(
            state_ref[c].astype(F32), rim_ref[c].astype(F32), pat_ref[c], lane, band
        )
        total = total + bias_ref[c]
        outs.append(jnp.where(step * GROUP + c < LC, total, 0.0))
    held[...] = jnp.swapaxes(jnp.stack(outs, 0), 0, 1).reshape(4, QR, GROUP, LANES)
    me = me_ref[0]
    for k in range(4):
        share = held[me ^ k].astype(BF)
        refs[k][...] = share[:HR]
        refs[4 + k][...] = share[HR:]


def conv_forward(me, state, rim, pattern, bias):
    share = pltpu.HBM((HR, CP, LANES), BF)
    return pl.pallas_call(
        forward_kernel,
        out_shape=[share] * 8,
        grid_spec=pltpu.PrefetchScalarGridSpec(
            num_scalar_prefetch=1,
            grid=(CP // GROUP,),
            in_specs=[
                pl.BlockSpec((GROUP, ROWS, LANES), lambda i, me: (i, 0, 0)),
                pl.BlockSpec((GROUP, ROWS, LANES), lambda i, me: (i, 0, 0)),
                pl.BlockSpec((GROUP, 4, LANES), lambda i, me: (i, 0, 0)),
                pl.BlockSpec((GROUP, 1, LANES), lambda i, me: (i, 0, 0)),
            ],
            out_specs=[pl.BlockSpec((HR, GROUP, LANES), lambda i, me: (0, i, 0))] * 8,
            scratch_shapes=[pltpu.VMEM((4, QR, GROUP, LANES), F32)],
        ),
        compiler_params=pltpu.CompilerParams(vmem_limit_bytes=32 << 20),
        cost_estimate=cost(9),
        name="conv_forward",
    )(me, state, rim, pattern, bias)


def backward_kernel(me_ref, *refs):
    pieces = refs[:8]
    rims_in, pat_ref, cot_ref, mask_ref, out_ref, held, held_rim = refs[8:]
    lane, band = masks()
    me = me_ref[0]
    for k in range(4):
        held[me ^ k, :HR] = pieces[k][...].astype(F32)
        held[me ^ k, HR:] = pieces[4 + k][...].astype(F32)
        held_rim[me ^ k, :HR] = rims_in[k].astype(F32)
        held_rim[me ^ k, HR:] = rims_in[4 + k].astype(F32)
    cells = jnp.swapaxes(held[...].reshape(ROWS, GROUP, LANES), 0, 1)
    rims = jnp.swapaxes(held_rim[...].reshape(ROWS, GROUP, LANES), 0, 1)
    mask = mask_ref[...].astype(F32)
    for c in range(GROUP):
        total = conv_channel(cells[c], rims[c], pat_ref[c], lane, band)
        out_ref[c] = (cot_ref[c].astype(F32) * mask + total).astype(BF)


def conv_backward(me, early, late, rims, pattern, cotangent, sea_mask):
    return pl.pallas_call(
        backward_kernel,
        out_shape=jax.ShapeDtypeStruct((LC, ROWS, LANES), BF),
        grid_spec=pltpu.PrefetchScalarGridSpec(
            num_scalar_prefetch=1,
            grid=(CP // GROUP,),
            in_specs=[pl.BlockSpec((None, HR, GROUP, LANES), lambda i, me: (0, 0, i, 0))] * 4
            + [pl.BlockSpec((HR, GROUP, LANES), lambda i, me: (0, i, 0))] * 4
            + [
                pl.BlockSpec((8, HR, GROUP, LANES), lambda i, me: (0, 0, i, 0)),
                pl.BlockSpec((GROUP, 4, LANES), lambda i, me: (i, 0, 0)),
                pl.BlockSpec((GROUP, ROWS, LANES), lambda i, me: (i, 0, 0)),
                pl.BlockSpec((ROWS, LANES), lambda i, me: (0, 0)),
            ],
            out_specs=pl.BlockSpec((GROUP, ROWS, LANES), lambda i, me: (i, 0, 0)),
            scratch_shapes=[pltpu.VMEM((4, QR, GROUP, LANES), F32)] * 2,
        ),
        compiler_params=pltpu.CompilerParams(vmem_limit_bytes=32 << 20),
        cost_estimate=cost(10),
        name="conv_backward",
    )(me, *early, *late, rims, pattern, cotangent, sea_mask)


SUB = 4
CELLS = SUB * LANES
HT = 400
PIECE = 328
WIRE = 16 * PIECE


def mlp_kernel(half, me_ref, core_ref, *refs):
    xs, gs = refs[:4], refs[4:8]
    win_t, win, wout, wout_t, vec, bias_in = refs[8:14]
    if half:
        hid_in, cells_in = refs[14:16]
        grad_out, branch_out, wires = refs[17:21], refs[21:25], refs[25:27]
        hidden, cells, hid_a, cells_a, held, sems = refs[27:]
        copies = (
            pltpu.make_async_copy(hid_in, hid_a, sems.at[0]),
            pltpu.make_async_copy(cells_in, cells_a, sems.at[1]),
        )
    else:
        both_out = refs[14:18]
        hidden, cells = refs[18:]
    step = pl.program_id(0)
    me = me_ref[0]
    if half:

        @pl.when(step == 0)
        def _():
            for copy in copies:
                copy.start()

        lanes = pl.ds(pl.multiple_of(step * CELLS, CELLS), CELLS)
    else:
        lanes = slice(0, CELLS)

    def gather(pieces):
        return jnp.concatenate(
            [
                jnp.concatenate([p[r].astype(F32) for r in range(SUB)], axis=1)
                for p in pieces
            ],
            axis=0,
        )

    gain = vec[:, 0:1]
    values = gather(xs)
    mean_val = jnp.sum(values, axis=0, keepdims=True) / C
    square = jnp.sum(values * values, axis=0, keepdims=True) / C
    inv_std = lax.rsqrt(square - mean_val * mean_val + norm_eps)
    normed = (values - mean_val) * inv_std * gain + vec[:, 1:2]
    grads = gather(gs)
    for k in range(4):
        rows = slice(k * CP, (k + 1) * CP)
        cells[0, me ^ k, :, lanes] = normed[rows].astype(cells.dtype)
        cells[1, me ^ k, :, lanes] = grads[rows].astype(cells.dtype)
    normed, grads = normed.astype(BF), grads.astype(BF)
    for t in range(HID // HT):
        rows = slice(t * HT, (t + 1) * HT)
        pre = jnp.dot(win_t[rows, :], normed, preferred_element_type=F32) + bias_in[rows, :]
        gact = jnp.dot(wout[rows, :], grads, preferred_element_type=F32)
        sq = pre * pre
        tangent = jnp.tanh(pre * (root_coef + (root_coef * cubic_coef) * sq))
        side = 0.5 + 0.5 * tangent
        value = pre * side
        slope = side + value * (1.0 - side) * (
            2.0 * root_coef + (6.0 * root_coef * cubic_coef) * sq
        )
        hidden[0, rows, lanes] = (gact * slope).astype(BF)
        hidden[1, rows, lanes] = value.astype(BF)
    x_grad = jnp.dot(win[...], hidden[0, :, lanes], preferred_element_type=F32) * gain
    centred = (values - mean_val) * inv_std
    first = jnp.sum(x_grad, axis=0, keepdims=True) / C
    second = jnp.sum(x_grad * centred, axis=0, keepdims=True) / C
    x_grad = inv_std * (x_grad - first - centred * second)
    branch = jnp.dot(wout_t[...], hidden[1, :, lanes], preferred_element_type=F32)
    branch = branch + vec[:, 2:3]
    for k in range(4):
        for r in range(SUB):
            here = slice(r * LANES, (r + 1) * LANES)
            grad_piece = x_grad[k * CP : (k + 1) * CP, here].astype(BF)
            branch_piece = branch[k * CP : (k + 1) * CP, here].astype(BF)
            if half:
                grad_out[k][r] = grad_piece
                branch_out[k][r] = branch_piece
            else:
                both_out[k][0, r] = grad_piece
                both_out[k][1, r] = branch_piece
    if not half:
        return

    @pl.when(step == 1)
    def _():
        for copy in copies:
            copy.wait()
        core = core_ref[0]
        for out, slot in ((wires[0], core), (wires[1], 1 - core)):
            cells_b = cells[slot].reshape(4 * CP, 2 * CELLS).astype(BF)
            held[...] = dotg(hid_a[slot], cells_a[slot], 1, 1) + dotg(hidden[slot], cells_b, 1, 1)
            for t in range(3):
                out[t * HID : (t + 1) * HID, :] = held[:, t * LANES : (t + 1) * LANES].astype(BF)
            rest = [held[q * 400 : (q + 1) * 400, 3 * LANES :] for q in range(4)]
            out[3 * HID : 3 * HID + 400, :] = jnp.concatenate(rest, axis=1).astype(BF)
            out[3 * HID + 400 :, :] = jnp.zeros((WIRE - 3 * HID - 400, LANES), BF)


def mlp(half, me, core, xs, gs, weights, vec, bias_in, saved=(), after=()):
    any_space = pl.BlockSpec(memory_space=pl.ANY)

    def whole(shape):
        return pl.BlockSpec(
            shape, lambda i, me, core: (0,) * len(shape), pipeline_mode=pl.Buffered(1)
        )

    piece = pl.BlockSpec((SUB, CP, LANES), lambda i, me, core: (i, 0, 0))
    later = pl.BlockSpec((SUB, CP, LANES), lambda i, me, core: (2 * half + i, 0, 0))
    if half:
        shapes = [jax.ShapeDtypeStruct((WIRE, LANES), BF)] * 2
        specs = [whole((WIRE, LANES))] * 2
        scratch = [
            pltpu.VMEM((2, HID, 2 * CELLS), BF),
            pltpu.VMEM((2, 4, CP, 2 * CELLS), F32),
            pltpu.VMEM((2, HID, 2 * CELLS), BF),
            pltpu.VMEM((2, 4 * CP, 2 * CELLS), BF),
            pltpu.VMEM((HID, 4 * CP), F32),
            pltpu.SemaphoreType.DMA((2,)),
        ]
    else:
        shapes = [
            jax.ShapeDtypeStruct((2, HID, 2 * CELLS), BF),
            jax.ShapeDtypeStruct((2, 4, CP, 2 * CELLS), BF),
        ]
        specs = [
            pl.BlockSpec((2, HID, CELLS), lambda i, me, core: (0, 0, i)),
            pl.BlockSpec((2, 4, CP, CELLS), lambda i, me, core: (0, 0, 0, i)),
        ]
        scratch = []
    count = 8 if half else 4
    result = (HR, CP, LANES) if half else (2, HR, CP, LANES)
    place = piece
    if not half:
        place = pl.BlockSpec((2, SUB, CP, LANES), lambda i, me, core: (0, i, 0, 0))
    outs = pl.pallas_call(
        functools.partial(mlp_kernel, half),
        out_shape=[jax.ShapeDtypeStruct(result, BF)] * count + shapes,
        grid_spec=pltpu.PrefetchScalarGridSpec(
            num_scalar_prefetch=2,
            grid=(2,),
            in_specs=[piece] * 4
            + [later] * 4
            + [
                whole((HID, 4 * CP)),
                whole((4 * CP, HID)),
                whole((HID, 4 * CP)),
                whole((4 * CP, HID)),
                whole((4 * CP, 3)),
                whole((HID, 1)),
            ]
            + [any_space] * (len(saved) + len(after)),
            out_specs=[place] * count + specs,
            scratch_shapes=scratch,
        ),
        compiler_params=pltpu.CompilerParams(vmem_limit_bytes=VMEM),
        cost_estimate=cost(22 if half else 14),
        name="mlp_b" if half else "mlp_a",
    )(me, core, *xs, *gs, *weights, vec, bias_in, *saved, *after)
    return outs[:4], outs[4:count], outs[count:]


def update_kernel(me_ref, *refs):
    k = pl.program_id(0)
    state_ref, mask_ref, scale_ref, out_ref, held = refs[8:]

    def take(early, late):
        held[:HR] = early[...]
        held[HR:] = late[...]

    for i in range(4):
        pl.when(k == i)(lambda i=i: take(refs[i], refs[4 + i]))
    branch = jnp.swapaxes(held[...].astype(F32) * scale_ref[...][None], 0, 1)[:LC]
    mask = mask_ref[...].astype(F32)
    out_ref[...] = (mask[None] * (state_ref[...].astype(F32) + branch)).astype(BF)


def update(me, early, late, state, sea_mask, scale):
    whole = pl.BlockSpec((HR, CP, LANES), lambda i, me: (0, 0, 0), pipeline_mode=pl.Buffered(1))
    return pl.pallas_call(
        update_kernel,
        out_shape=jax.ShapeDtypeStruct((LC, ROWS, LANES), BF),
        grid_spec=pltpu.PrefetchScalarGridSpec(
            num_scalar_prefetch=1,
            grid=(4,),
            in_specs=[
                pl.BlockSpec(
                    (None, HR, CP, LANES),
                    lambda i, me: (1, 0, 0, 0),
                    pipeline_mode=pl.Buffered(1),
                )
            ]
            * 4
            + [whole] * 4
            + [
                pl.BlockSpec((LC, QR, LANES), lambda i, me: (0, me[0] ^ i, 0)),
                pl.BlockSpec((QR, LANES), lambda i, me: (me[0] ^ i, 0)),
                pl.BlockSpec((CP, 1), lambda i, me: (0, 0)),
            ],
            out_specs=pl.BlockSpec((LC, QR, LANES), lambda i, me: (0, me[0] ^ i, 0)),
            scratch_shapes=[pltpu.VMEM((QR, CP, LANES), BF)],
        ),
        compiler_params=pltpu.CompilerParams(vmem_limit_bytes=VMEM),
        cost_estimate=cost(4.4),
        name="update",
    )(me, *early, *late, state, sea_mask, scale)


def weights_kernel(one, two, pad, one_out, one_t, two_out, two_t):
    for source, out, turned in ((one, one_out, one_t), (two, two_out, two_t)):
        padded = dotg(pad[...], source[...], 0, 0)
        out[...] = padded.astype(BF)
        turned[...] = padded.T.astype(BF)


def padded_weights(one, two, pad):
    flat = pltpu.HBM((4 * CP, HID), BF)
    turned = pltpu.HBM((HID, 4 * CP), BF)
    return pl.pallas_call(
        weights_kernel,
        out_shape=[flat, turned, flat, turned],
        grid=(1,),
        in_specs=[full((C, HID)), full((C, HID)), full((C, 4 * CP))],
        out_specs=[full(x.shape) for x in (flat, turned, flat, turned)],
        compiler_params=pltpu.CompilerParams(vmem_limit_bytes=32 << 20),
        cost_estimate=cost(5),
        name="padded_weights",
    )(one, two, pad)


def tap_patterns(kernel):
    lane = jnp.arange(4 * LANES)
    tile, pos = lane // LANES, lane % LANES
    away = jnp.where(pos % ROWS < ROWS // 2, pos % ROWS, pos % ROWS - ROWS)
    side = ((pos - away) // ROWS) % 2
    col = 2 * tile + side
    tap = jnp.where((jnp.abs(away) <= RIM) & (col < KW), (away + RIM) * KW + col, -1)
    pick = (jnp.arange(KW * KW)[:, None] == tap[None, :]).astype(BF)
    return jnp.dot(kernel.astype(BF), pick, preferred_element_type=F32).reshape(LC, 4, LANES)


def edge_picks():
    row = jnp.arange(8)[:, None]
    lane = jnp.arange(LANES)[None, :]
    head = ((row < RIM) & (lane == row)).astype(BF)
    tail = ((row < RIM) & (lane == LANES - RIM + row)).astype(BF)
    return head, tail


def edge_kernel(cells, pick, *refs):
    refs[-1][...] = dotg(pick[...], cells[...], 1, 1).astype(BF)


def edge(cells2d, pick, after=()):
    return pl.pallas_call(
        edge_kernel,
        out_shape=jax.ShapeDtypeStruct((8, cells2d.shape[0]), BF),
        grid=(1,),
        in_specs=[full(cells2d.shape), full(pick.shape)]
        + [pl.BlockSpec(memory_space=pl.ANY)] * len(after),
        out_specs=full((8, cells2d.shape[0])),
        compiler_params=pltpu.CompilerParams(vmem_limit_bytes=32 << 20),
        cost_estimate=cost(1),
        name="edge",
    )(cells2d, pick, *after)


def piece_edges_kernel(pick, *refs):
    first, last = refs[8:]
    for i in range(8):
        cells = refs[i][...].reshape(HR * CP, LANES)
        both = dotg(pick[...], cells, 1, 1).astype(BF)
        first[i] = both[:8]
        last[i] = both[8:]


def piece_edges(picks, early, late):
    half = pl.BlockSpec((QR // 2, CP, LANES), lambda i: (0, 0, 0))
    whole = pl.BlockSpec((8, 8, HR * CP), lambda i: (0, 0, 0))
    out = jax.ShapeDtypeStruct((8, 8, HR * CP), BF)
    return pl.pallas_call(
        piece_edges_kernel,
        out_shape=[out, out],
        grid=(1,),
        in_specs=[pl.BlockSpec((16, LANES), lambda i: (0, 0))]
        + [pl.BlockSpec((None, HR, CP, LANES), lambda i: (0, 0, 0, 0))] * 4
        + [half] * 4,
        out_specs=[whole] * 2,
        compiler_params=pltpu.CompilerParams(vmem_limit_bytes=32 << 20),
        cost_estimate=cost(2),
        name="piece_edges",
    )(picks, *early, *late)


def piece_rims_kernel(pick, first, last, out):
    for i in range(8):
        both = jnp.concatenate([first[i], last[i]], axis=0)
        out[i] = dotg(both, pick[...], 0, 0).astype(BF).reshape(HR, CP, LANES)


def piece_rims(picks, first, last):
    return pl.pallas_call(
        piece_rims_kernel,
        out_shape=jax.ShapeDtypeStruct((8, HR, CP, LANES), BF),
        grid=(1,),
        in_specs=[full((16, LANES)), full((8, 8, HR * CP)), full((8, 8, HR * CP))],
        out_specs=full((8, HR, CP, LANES)),
        compiler_params=pltpu.CompilerParams(vmem_limit_bytes=32 << 20),
        cost_estimate=cost(2),
        name="piece_rims",
    )(picks, first, last)


def rims(first, last):
    both = jnp.concatenate([lon_shift(first, -1), lon_shift(last, 1)], 0)
    return dotg(both, jnp.concatenate(edge_picks(), 0), 0, 0).astype(BF)


PLANES = [[16 * half + i for i in range(16)] for half in range(2)]


def plane_exchange(pieces):
    return lax.all_to_all(pieces, "lon", 0, 0, axis_index_groups=PLANES)


def total_kernel(*refs):
    total = refs[0][0].astype(F32)
    for i in range(1, 16):
        total = total + refs[0][i].astype(F32)
    refs[-1][...] = total.astype(BF)


def plane_total(pieces, after):
    return pl.pallas_call(
        total_kernel,
        out_shape=jax.ShapeDtypeStruct((PIECE, LANES), BF),
        grid=(1,),
        in_specs=[full((16, PIECE, LANES))] + [pl.BlockSpec(memory_space=pl.ANY)] * len(after),
        out_specs=full((PIECE, LANES)),
        compiler_params=pltpu.CompilerParams(vmem_limit_bytes=32 << 20),
        cost_estimate=cost(1.2),
        name="plane_total",
    )(pieces, *after)


def copies_kernel(part, *refs):
    out = refs[-1]
    for i in range(16):
        out[i] = part[...]


def plane_copies(part, after):
    return pl.pallas_call(
        copies_kernel,
        out_shape=jax.ShapeDtypeStruct((16, PIECE, LANES), BF),
        grid=(1,),
        in_specs=[full((PIECE, LANES))] + [pl.BlockSpec(memory_space=pl.ANY)] * len(after),
        out_specs=full((16, PIECE, LANES)),
        compiler_params=pltpu.CompilerParams(vmem_limit_bytes=32 << 20),
        cost_estimate=cost(1),
        name="plane_copies",
    )(part, *after)


def reduce_gradients(keep, send, late, last):
    mine = (keep.astype(F32) + ch_swap(send, 1).astype(F32)).astype(BF)
    mine = plane_exchange(mine.reshape(16, PIECE, LANES))
    wire = plane_total(mine, late)
    part = (
        (wire.astype(F32) + lon_swap(wire, 16).astype(F32))
        + (ch_swap(wire, 2).astype(F32) + both_swap(wire).astype(F32))
    ).astype(BF)
    return plane_exchange(plane_copies(part, last)).reshape(WIRE, LANES)


def finish_kernel(core_ref, own, other, pad, grad_in, grad_out, held):
    core = core_ref[0]
    for wire, slot in ((own, core), (other, 1 - core)):
        for t in range(3):
            held[slot, :, t * LANES : (t + 1) * LANES] = wire[t * HID : (t + 1) * HID, :]
        rest = wire[3 * HID : 3 * HID + 400, :]
        for q in range(4):
            held[slot, q * 400 : (q + 1) * 400, 3 * LANES :] = rest[:, q * 32 : (q + 1) * 32]
    factor = 1.0 / math.sqrt(ROWS * LANES * 32)
    grad_in[...] = dotg(pad[...], held[0], 1, 1) * factor
    grad_out[...] = dotg(pad[...], held[1], 1, 1) * factor


def finish(core, own, other, pad):
    return pl.pallas_call(
        finish_kernel,
        out_shape=[
            jax.ShapeDtypeStruct((C, HID), F32),
            jax.ShapeDtypeStruct((C, HID), F32),
        ],
        grid=(1,),
        in_specs=[
            pl.BlockSpec(memory_space=pltpu.SMEM),
            full((WIRE, LANES)),
            full((WIRE, LANES)),
            full((C, 4 * CP)),
        ],
        out_specs=[full((C, HID))] * 2,
        scratch_shapes=[pltpu.VMEM((2, HID, 4 * CP), BF)],
        compiler_params=pltpu.CompilerParams(vmem_limit_bytes=32 << 20),
        cost_estimate=cost(6),
        name="finish",
    )(core, own, other, pad)


def both_swap(x):
    return lax.ppermute(x, ("lon", "ch"), [(i, i ^ (16 * 4 + 2)) for i in range(128)])


def body(
    ocean_state,
    sea_mask,
    kernel,
    conv_bias,
    norm_gain,
    norm_bias,
    weight_in,
    bias_in,
    weight_out,
    bias_out,
    layer_scale,
    cotangent,
):
    ch = lax.axis_index("ch")
    me = ch.reshape(1)
    core = (ch & 1).reshape(1)
    scale = jnp.pad(layer_scale, (0, CP - LC)).reshape(CP, 1)

    head, tail = edge_picks()
    state2d = ocean_state.reshape(LC * ROWS, LANES)
    sent = {}
    first = edge(state2d, head)
    sent[2] = branch_share(me, cotangent, sea_mask, scale, 2, (first,))
    last = edge(state2d, tail, (sent[2],))
    sent[3] = branch_share(me, cotangent, sea_mask, scale, 3, (last,))
    sent[1] = branch_share(me, cotangent, sea_mask, scale, 1, (sent[3],))
    sent[0] = branch_share(me, cotangent, sea_mask, scale, 0, (sent[1],))
    gs = [sent[0]] + [ch_swap(sent[k], k) for k in (1, 2, 3)]

    chan = jnp.arange(C)
    padded = jnp.arange(4 * CP)
    pad = ((chan // LC * CP + chan % LC)[:, None] == padded[None, :]).astype(BF)
    pad_own = (((chan // LC ^ ch) * CP + chan % LC)[:, None] == padded[None, :]).astype(BF)
    win, win_t, wout_t, wout = padded_weights(weight_in, weight_out.T, pad_own)
    vec = jnp.stack([norm_gain, norm_bias, bias_out], 1).reshape(4, LC, 3)
    vec = jnp.pad(vec, ((0, 0), (0, CP - LC), (0, 0)))
    vec = jnp.concatenate([lax.dynamic_index_in_dim(vec, ch ^ k, 0, False) for k in range(4)], 0)

    state_rim = rims(first, last).reshape(LC, ROWS, LANES)
    bias = jnp.broadcast_to(conv_bias[:, None, None], (LC, 1, LANES))
    conv = conv_forward(me, ocean_state, state_rim, tap_patterns(kernel), bias)
    weights, gs, second = lax.optimization_barrier(((win_t, win, wout, wout_t), gs, conv[4:]))
    xs = [
        [half[0]] + [ch_swap(half[k], k) for k in (1, 2, 3)] for half in (conv[:4], second)
    ]

    bias_rows = bias_in.reshape(HID, 1)
    early, _, (hid_a, cells_a) = mlp(0, me, core, xs[0], gs, weights, vec, bias_rows)
    early, second = lax.optimization_barrier((early, xs[1]))
    saved = (hid_a, cells_a.reshape(2, 4 * CP, 2 * CELLS))
    grad_b, branch_b, (keep, send) = mlp(
        1, me, core, second, gs, weights, vec, bias_rows, saved, early[:1]
    )
    early = [early[0]] + [ch_swap(early[k], k) for k in (1, 2, 3)]
    keep, send, early = lax.optimization_barrier((keep, send, early))
    grad_b = [grad_b[0]] + [ch_swap(grad_b[k], k) for k in (1, 2, 3)]
    branch_b = [branch_b[0]] + [ch_swap(branch_b[k], k) for k in (1, 2, 3)]
    grad_b, branch_b = lax.optimization_barrier((grad_b, branch_b))
    updated = update(me, early, branch_b, ocean_state, sea_mask, scale)
    picks = jnp.concatenate([head, tail], 0)
    first, last = piece_edges(picks, early, grad_b)
    from_right, from_left = lon_shift(first, -1), lon_shift(last, 1)
    own = reduce_gradients(keep, send, branch_b[1:], (updated,))
    grad_rims = piece_rims(picks, from_right, from_left)

    grad_state = conv_backward(
        me,
        early,
        grad_b,
        grad_rims,
        tap_patterns(kernel[:, ::-1]),
        cotangent,
        sea_mask,
    )
    own, grad_state = lax.optimization_barrier((own, grad_state))
    grad_in, grad_out = finish(core, own, ch_swap(own, 1), pad)
    return updated, grad_state, grad_in, grad_out.T


def solution(mesh):
    return jax.shard_map(
        body,
        mesh=mesh,
        in_specs=(
            P("ch", None, "lon"),
            P(None, "lon"),
            P("ch", None),
            P("ch"),
            P(),
            P(),
            P(),
            P(),
            P(),
            P(),
            P("ch"),
            P("ch", None, "lon"),
        ),
        out_specs=(P("ch", None, "lon"), P("ch", None, "lon"), P(), P()),
        check_vma=False,
    )
```

```python
import functools
import math

import jax
import jax.numpy as jnp
from jax import lax
from jax.experimental import pallas as pl
from jax.experimental.pallas import tpu as pltpu
from jax.sharding import PartitionSpec as P

KW = 7
RIM = KW // 2
C = 400
HID = 1600
ROWS = 64
LANES = 128
LC = 100
CP = 104
QR = 16
HR = 8
GROUP = 8
VMEM = 63 << 20
BF = jnp.bfloat16
F32 = jnp.float32

root_coef = math.sqrt(2.0 / math.pi)
cubic_coef = 0.044715
norm_eps = 1e-06


def dotg(a, b, ca, cb):
    return lax.dot_general(a, b, (((ca,), (cb,)), ((), ())), preferred_element_type=F32)


def cost(micros):
    return pl.CostEstimate(flops=0, bytes_accessed=int(micros * 3.3e6), transcendentals=0)


def full(shape):
    return pl.BlockSpec(shape, lambda *i: (0,) * len(shape), pipeline_mode=pl.Buffered(1))


def ch_swap(x, k):
    return lax.ppermute(x, "ch", [(i, i ^ k) for i in range(4)])


def lon_shift(x, d):
    return lax.ppermute(x, "lon", [(i, (i + d) % 32) for i in range(32)])


def lon_swap(x, k):
    return lax.ppermute(x, "lon", [(i, i ^ k) for i in range(32)])


def share_kernel(me_ref, cot_ref, mask_ref, scale_ref, *refs):
    out_ref = refs[-1]
    cells = cot_ref[...].astype(F32)
    cells = jnp.concatenate([cells, jnp.zeros((CP - LC, QR, LANES), F32)], axis=0)
    cells = jnp.swapaxes(cells, 0, 1)
    mask = mask_ref[...].astype(F32)
    out_ref[...] = ((cells * mask[:, None, :]) * scale_ref[...][None]).astype(BF)


def branch_share(me, cotangent, sea_mask, scale, k, after):
    return pl.pallas_call(
        share_kernel,
        out_shape=jax.ShapeDtypeStruct((QR, CP, LANES), BF),
        grid_spec=pltpu.PrefetchScalarGridSpec(
            num_scalar_prefetch=1,
            grid=(1,),
            in_specs=[
                pl.BlockSpec((LC, QR, LANES), lambda i, me: (0, me[0] ^ k, 0)),
                pl.BlockSpec((QR, LANES), lambda i, me: (me[0] ^ k, 0)),
                pl.BlockSpec((CP, 1), lambda i, me: (0, 0)),
            ]
            + [pl.BlockSpec(memory_space=pl.ANY)] * len(after),
            out_specs=pl.BlockSpec((QR, CP, LANES), lambda i, me: (0, 0, 0)),
        ),
        compiler_params=pltpu.CompilerParams(vmem_limit_bytes=32 << 20),
        cost_estimate=cost(1.2),
        name="branch_share",
    )(me, cotangent, sea_mask, scale, *after)


def conv_channel(cells, rim, pattern, lane, band):
    moved = []
    for off in range(-RIM, RIM + 1):
        if off == 0:
            moved.append(cells.astype(BF))
        else:
            edge = lane < off if off > 0 else lane >= LANES + off
            moved.append(pltpu.roll(jnp.where(edge, rim, cells), (-off) % LANES, 1).astype(BF))
    stacked = jnp.concatenate(moved, axis=0)
    tiles = []
    for t in range(4):
        row = jnp.broadcast_to(pattern[t : t + 1, :], (ROWS, LANES))
        row = pltpu.roll(row, 0, 1, stride=1, stride_axis=0)
        tiles.append(jnp.where(band, row, 0.0).astype(BF))
    banded = jnp.concatenate(tiles, axis=1)[:, : KW * ROWS]
    return jnp.dot(banded, stacked, preferred_element_type=F32)


def masks():
    lane = lax.broadcasted_iota(jnp.int32, (ROWS, LANES), 1)
    row = lax.broadcasted_iota(jnp.int32, (ROWS, LANES), 0)
    away = (lane & (ROWS - 1)) - row
    return lane, (away >= -RIM) & (away <= RIM)


def forward_kernel(me_ref, state_ref, rim_ref, pat_ref, bias_ref, *refs):
    held = refs[-1]
    step = pl.program_id(0)
    lane, band = masks()
    outs = []
    for c in range(GROUP):
        total = conv_channel(
            state_ref[c].astype(F32), rim_ref[c].astype(F32), pat_ref[c], lane, band
        )
        total = total + bias_ref[c]
        outs.append(jnp.where(step * GROUP + c < LC, total, 0.0))
    held[...] = jnp.swapaxes(jnp.stack(outs, 0), 0, 1).reshape(4, QR, GROUP, LANES)
    me = me_ref[0]
    for k in range(4):
        share = held[me ^ k].astype(BF)
        refs[k][...] = share[:HR]
        refs[4 + k][...] = share[HR:]


def conv_forward(me, state, rim, pattern, bias):
    share = pltpu.HBM((HR, CP, LANES), BF)
    return pl.pallas_call(
        forward_kernel,
        out_shape=[share] * 8,
        grid_spec=pltpu.PrefetchScalarGridSpec(
            num_scalar_prefetch=1,
            grid=(CP // GROUP,),
            in_specs=[
                pl.BlockSpec((GROUP, ROWS, LANES), lambda i, me: (i, 0, 0)),
                pl.BlockSpec((GROUP, ROWS, LANES), lambda i, me: (i, 0, 0)),
                pl.BlockSpec((GROUP, 4, LANES), lambda i, me: (i, 0, 0)),
                pl.BlockSpec((GROUP, 1, LANES), lambda i, me: (i, 0, 0)),
            ],
            out_specs=[pl.BlockSpec((HR, GROUP, LANES), lambda i, me: (0, i, 0))] * 8,
            scratch_shapes=[pltpu.VMEM((4, QR, GROUP, LANES), F32)],
        ),
        compiler_params=pltpu.CompilerParams(vmem_limit_bytes=32 << 20),
        cost_estimate=cost(9),
        name="conv_forward",
    )(me, state, rim, pattern, bias)


def backward_kernel(me_ref, *refs):
    pieces = refs[:8]
    rims_in, pat_ref, cot_ref, mask_ref, out_ref, held, held_rim = refs[8:]
    lane, band = masks()
    me = me_ref[0]
    for k in range(4):
        held[me ^ k, :HR] = pieces[k][...].astype(F32)
        held[me ^ k, HR:] = pieces[4 + k][...].astype(F32)
        held_rim[me ^ k, :HR] = rims_in[k].astype(F32)
        held_rim[me ^ k, HR:] = rims_in[4 + k].astype(F32)
    cells = jnp.swapaxes(held[...].reshape(ROWS, GROUP, LANES), 0, 1)
    rims = jnp.swapaxes(held_rim[...].reshape(ROWS, GROUP, LANES), 0, 1)
    mask = mask_ref[...].astype(F32)
    for c in range(GROUP):
        total = conv_channel(cells[c], rims[c], pat_ref[c], lane, band)
        out_ref[c] = (cot_ref[c].astype(F32) * mask + total).astype(BF)


def conv_backward(me, early, late, rims, pattern, cotangent, sea_mask):
    return pl.pallas_call(
        backward_kernel,
        out_shape=jax.ShapeDtypeStruct((LC, ROWS, LANES), BF),
        grid_spec=pltpu.PrefetchScalarGridSpec(
            num_scalar_prefetch=1,
            grid=(CP // GROUP,),
            in_specs=[pl.BlockSpec((None, HR, GROUP, LANES), lambda i, me: (0, 0, i, 0))] * 4
            + [pl.BlockSpec((HR, GROUP, LANES), lambda i, me: (0, i, 0))] * 4
            + [
                pl.BlockSpec((8, HR, GROUP, LANES), lambda i, me: (0, 0, i, 0)),
                pl.BlockSpec((GROUP, 4, LANES), lambda i, me: (i, 0, 0)),
                pl.BlockSpec((GROUP, ROWS, LANES), lambda i, me: (i, 0, 0)),
                pl.BlockSpec((ROWS, LANES), lambda i, me: (0, 0)),
            ],
            out_specs=pl.BlockSpec((GROUP, ROWS, LANES), lambda i, me: (i, 0, 0)),
            scratch_shapes=[pltpu.VMEM((4, QR, GROUP, LANES), F32)] * 2,
        ),
        compiler_params=pltpu.CompilerParams(vmem_limit_bytes=VMEM),
        cost_estimate=cost(10),
        name="conv_backward",
    )(me, *early, *late, rims, pattern, cotangent, sea_mask)


SUB = 4
CELLS = SUB * LANES
HT = 400
PIECE = 328
WIRE = 16 * PIECE


def mlp_kernel(half, me_ref, core_ref, *refs):
    xs, gs = refs[:4], refs[4:8]
    win_t, win, wout, wout_t, vec, bias_in = refs[8:14]
    if half:
        hid_in, cells_in = refs[14:16]
        grad_out, branch_out, wires = refs[17:21], refs[21:25], refs[25:27]
        hidden, cells, hid_a, cells_a, held, sems = refs[27:]
        copies = (
            pltpu.make_async_copy(hid_in, hid_a, sems.at[0]),
            pltpu.make_async_copy(cells_in, cells_a, sems.at[1]),
        )
    else:
        both_out = refs[14:18]
        hidden, cells = refs[18:]
    step = pl.program_id(0)
    me = me_ref[0]
    if half:

        @pl.when(step == 0)
        def _():
            for copy in copies:
                copy.start()

        lanes = pl.ds(pl.multiple_of(step * CELLS, CELLS), CELLS)
    else:
        lanes = slice(0, CELLS)

    def gather(pieces):
        return jnp.concatenate(
            [
                jnp.concatenate([p[r].astype(F32) for r in range(SUB)], axis=1)
                for p in pieces
            ],
            axis=0,
        )

    gain = vec[:, 0:1]
    values = gather(xs)
    mean_val = jnp.sum(values, axis=0, keepdims=True) / C
    square = jnp.sum(values * values, axis=0, keepdims=True) / C
    inv_std = lax.rsqrt(square - mean_val * mean_val + norm_eps)
    normed = (values - mean_val) * inv_std * gain + vec[:, 1:2]
    grads = gather(gs)
    for k in range(4):
        rows = slice(k * CP, (k + 1) * CP)
        cells[0, me ^ k, :, lanes] = normed[rows].astype(cells.dtype)
        cells[1, me ^ k, :, lanes] = grads[rows].astype(cells.dtype)
    normed, grads = normed.astype(BF), grads.astype(BF)
    for t in range(HID // HT):
        rows = slice(t * HT, (t + 1) * HT)
        pre = jnp.dot(win_t[rows, :], normed, preferred_element_type=F32) + bias_in[rows, :]
        gact = jnp.dot(wout[rows, :], grads, preferred_element_type=F32)
        sq = pre * pre
        tangent = jnp.tanh(pre * (root_coef + (root_coef * cubic_coef) * sq))
        side = 0.5 + 0.5 * tangent
        value = pre * side
        slope = side + value * (1.0 - side) * (
            2.0 * root_coef + (6.0 * root_coef * cubic_coef) * sq
        )
        hidden[0, rows, lanes] = (gact * slope).astype(BF)
        hidden[1, rows, lanes] = value.astype(BF)
    x_grad = jnp.dot(win[...], hidden[0, :, lanes], preferred_element_type=F32) * gain
    centred = (values - mean_val) * inv_std
    first = jnp.sum(x_grad, axis=0, keepdims=True) / C
    second = jnp.sum(x_grad * centred, axis=0, keepdims=True) / C
    x_grad = inv_std * (x_grad - first - centred * second)
    branch = jnp.dot(wout_t[...], hidden[1, :, lanes], preferred_element_type=F32)
    branch = branch + vec[:, 2:3]
    for k in range(4):
        for r in range(SUB):
            here = slice(r * LANES, (r + 1) * LANES)
            grad_piece = x_grad[k * CP : (k + 1) * CP, here].astype(BF)
            branch_piece = branch[k * CP : (k + 1) * CP, here].astype(BF)
            if half:
                grad_out[k][r] = grad_piece
                branch_out[k][r] = branch_piece
            else:
                both_out[k][0, r] = grad_piece
                both_out[k][1, r] = branch_piece
    if not half:
        return

    @pl.when(step == 1)
    def _():
        for copy in copies:
            copy.wait()
        core = core_ref[0]
        for out, slot in ((wires[0], core), (wires[1], 1 - core)):
            cells_b = cells[slot].reshape(4 * CP, 2 * CELLS).astype(BF)
            held[...] = dotg(hid_a[slot], cells_a[slot], 1, 1) + dotg(hidden[slot], cells_b, 1, 1)
            for t in range(3):
                out[t * HID : (t + 1) * HID, :] = held[:, t * LANES : (t + 1) * LANES].astype(BF)
            rest = [held[q * 400 : (q + 1) * 400, 3 * LANES :] for q in range(4)]
            out[3 * HID : 3 * HID + 400, :] = jnp.concatenate(rest, axis=1).astype(BF)
            out[3 * HID + 400 :, :] = jnp.zeros((WIRE - 3 * HID - 400, LANES), BF)


def mlp(half, me, core, xs, gs, weights, vec, bias_in, saved=(), after=()):
    any_space = pl.BlockSpec(memory_space=pl.ANY)

    def whole(shape):
        return pl.BlockSpec(
            shape, lambda i, me, core: (0,) * len(shape), pipeline_mode=pl.Buffered(1)
        )

    piece = pl.BlockSpec((SUB, CP, LANES), lambda i, me, core: (i, 0, 0))
    later = pl.BlockSpec((SUB, CP, LANES), lambda i, me, core: (2 * half + i, 0, 0))
    if half:
        shapes = [jax.ShapeDtypeStruct((WIRE, LANES), BF)] * 2
        specs = [whole((WIRE, LANES))] * 2
        scratch = [
            pltpu.VMEM((2, HID, 2 * CELLS), BF),
            pltpu.VMEM((2, 4, CP, 2 * CELLS), F32),
            pltpu.VMEM((2, HID, 2 * CELLS), BF),
            pltpu.VMEM((2, 4 * CP, 2 * CELLS), BF),
            pltpu.VMEM((HID, 4 * CP), F32),
            pltpu.SemaphoreType.DMA((2,)),
        ]
    else:
        shapes = [
            jax.ShapeDtypeStruct((2, HID, 2 * CELLS), BF),
            jax.ShapeDtypeStruct((2, 4, CP, 2 * CELLS), BF),
        ]
        specs = [
            pl.BlockSpec((2, HID, CELLS), lambda i, me, core: (0, 0, i)),
            pl.BlockSpec((2, 4, CP, CELLS), lambda i, me, core: (0, 0, 0, i)),
        ]
        scratch = []
    count = 8 if half else 4
    result = (HR, CP, LANES) if half else (2, HR, CP, LANES)
    place = piece
    if not half:
        place = pl.BlockSpec((2, SUB, CP, LANES), lambda i, me, core: (0, i, 0, 0))
    outs = pl.pallas_call(
        functools.partial(mlp_kernel, half),
        out_shape=[jax.ShapeDtypeStruct(result, BF)] * count + shapes,
        grid_spec=pltpu.PrefetchScalarGridSpec(
            num_scalar_prefetch=2,
            grid=(2,),
            in_specs=[piece] * 4
            + [later] * 4
            + [
                whole((HID, 4 * CP)),
                whole((4 * CP, HID)),
                whole((HID, 4 * CP)),
                whole((4 * CP, HID)),
                whole((4 * CP, 3)),
                whole((HID, 1)),
            ]
            + [any_space] * (len(saved) + len(after)),
            out_specs=[place] * count + specs,
            scratch_shapes=scratch,
        ),
        compiler_params=pltpu.CompilerParams(vmem_limit_bytes=VMEM),
        cost_estimate=cost(22 if half else 14),
        name="mlp_b" if half else "mlp_a",
    )(me, core, *xs, *gs, *weights, vec, bias_in, *saved, *after)
    return outs[:4], outs[4:count], outs[count:]


def update_kernel(me_ref, *refs):
    k = pl.program_id(0)
    state_ref, mask_ref, scale_ref, out_ref, held = refs[8:]

    def take(early, late):
        held[:HR] = early[...]
        held[HR:] = late[...]

    for i in range(4):
        pl.when(k == i)(lambda i=i: take(refs[i], refs[4 + i]))
    branch = jnp.swapaxes(held[...].astype(F32) * scale_ref[...][None], 0, 1)[:LC]
    mask = mask_ref[...].astype(F32)
    out_ref[...] = (mask[None] * (state_ref[...].astype(F32) + branch)).astype(BF)


def update(me, early, late, state, sea_mask, scale):
    whole = pl.BlockSpec((HR, CP, LANES), lambda i, me: (0, 0, 0), pipeline_mode=pl.Buffered(1))
    return pl.pallas_call(
        update_kernel,
        out_shape=jax.ShapeDtypeStruct((LC, ROWS, LANES), BF),
        grid_spec=pltpu.PrefetchScalarGridSpec(
            num_scalar_prefetch=1,
            grid=(4,),
            in_specs=[
                pl.BlockSpec(
                    (None, HR, CP, LANES),
                    lambda i, me: (1, 0, 0, 0),
                    pipeline_mode=pl.Buffered(1),
                )
            ]
            * 4
            + [whole] * 4
            + [
                pl.BlockSpec((LC, QR, LANES), lambda i, me: (0, me[0] ^ i, 0)),
                pl.BlockSpec((QR, LANES), lambda i, me: (me[0] ^ i, 0)),
                pl.BlockSpec((CP, 1), lambda i, me: (0, 0)),
            ],
            out_specs=pl.BlockSpec((LC, QR, LANES), lambda i, me: (0, me[0] ^ i, 0)),
            scratch_shapes=[pltpu.VMEM((QR, CP, LANES), BF)],
        ),
        compiler_params=pltpu.CompilerParams(vmem_limit_bytes=VMEM),
        cost_estimate=cost(4.4),
        name="update",
    )(me, *early, *late, state, sea_mask, scale)


def weights_kernel(one, two, pad, *refs):
    one_out, one_t, two_out, two_t = refs[-4:]
    for source, out, turned in ((one, one_out, one_t), (two, two_out, two_t)):
        padded = dotg(pad[...], source[...], 0, 0)
        out[...] = padded.astype(BF)
        turned[...] = padded.T.astype(BF)


def padded_weights(one, two, pad, after):
    flat = pltpu.HBM((4 * CP, HID), BF)
    turned = pltpu.HBM((HID, 4 * CP), BF)
    return pl.pallas_call(
        weights_kernel,
        out_shape=[flat, turned, flat, turned],
        grid=(1,),
        in_specs=[full((C, HID)), full((C, HID)), full((C, 4 * CP))]
        + [pl.BlockSpec(memory_space=pl.ANY)] * len(after),
        out_specs=[full(x.shape) for x in (flat, turned, flat, turned)],
        compiler_params=pltpu.CompilerParams(vmem_limit_bytes=32 << 20),
        cost_estimate=cost(5),
        name="padded_weights",
    )(one, two, pad, *after)


def tap_patterns(kernel):
    lane = jnp.arange(4 * LANES)
    tile, pos = lane // LANES, lane % LANES
    away = jnp.where(pos % ROWS < ROWS // 2, pos % ROWS, pos % ROWS - ROWS)
    side = ((pos - away) // ROWS) % 2
    col = 2 * tile + side
    tap = jnp.where((jnp.abs(away) <= RIM) & (col < KW), (away + RIM) * KW + col, -1)
    pick = (jnp.arange(KW * KW)[:, None] == tap[None, :]).astype(BF)
    return jnp.dot(kernel.astype(BF), pick, preferred_element_type=F32).reshape(LC, 4, LANES)


def edge_picks():
    row = jnp.arange(8)[:, None]
    lane = jnp.arange(LANES)[None, :]
    head = ((row < RIM) & (lane == row)).astype(BF)
    tail = ((row < RIM) & (lane == LANES - RIM + row)).astype(BF)
    return head, tail


def edge_kernel(cells, pick, *refs):
    refs[-1][...] = dotg(pick[...], cells[...], 1, 1).astype(BF)


def edge(cells2d, pick, after=()):
    return pl.pallas_call(
        edge_kernel,
        out_shape=jax.ShapeDtypeStruct((8, cells2d.shape[0]), BF),
        grid=(1,),
        in_specs=[full(cells2d.shape), full(pick.shape)]
        + [pl.BlockSpec(memory_space=pl.ANY)] * len(after),
        out_specs=full((8, cells2d.shape[0])),
        compiler_params=pltpu.CompilerParams(vmem_limit_bytes=32 << 20),
        cost_estimate=cost(1),
        name="edge",
    )(cells2d, pick, *after)


def piece_edges_kernel(pick, *refs):
    first, last = refs[8:]
    for i in range(8):
        cells = refs[i][...].reshape(HR * CP, LANES)
        both = dotg(pick[...], cells, 1, 1).astype(BF)
        first[i] = both[:8]
        last[i] = both[8:]


def piece_edges(picks, early, late):
    half = pl.BlockSpec((QR // 2, CP, LANES), lambda i: (0, 0, 0))
    whole = pl.BlockSpec((8, 8, HR * CP), lambda i: (0, 0, 0))
    out = pltpu.HBM((8, 8, HR * CP), BF)
    return pl.pallas_call(
        piece_edges_kernel,
        out_shape=[out, out],
        grid=(1,),
        in_specs=[pl.BlockSpec((16, LANES), lambda i: (0, 0))]
        + [pl.BlockSpec((None, HR, CP, LANES), lambda i: (0, 0, 0, 0))] * 4
        + [half] * 4,
        out_specs=[whole] * 2,
        compiler_params=pltpu.CompilerParams(vmem_limit_bytes=32 << 20),
        cost_estimate=cost(2),
        name="piece_edges",
    )(picks, *early, *late)


def piece_rims_kernel(pick, first, last, out):
    for i in range(8):
        both = jnp.concatenate([first[i], last[i]], axis=0)
        out[i] = dotg(both, pick[...], 0, 0).astype(BF).reshape(HR, CP, LANES)


def piece_rims(picks, first, last):
    return pl.pallas_call(
        piece_rims_kernel,
        out_shape=jax.ShapeDtypeStruct((8, HR, CP, LANES), BF),
        grid=(1,),
        in_specs=[full((16, LANES)), full((8, 8, HR * CP)), full((8, 8, HR * CP))],
        out_specs=full((8, HR, CP, LANES)),
        compiler_params=pltpu.CompilerParams(vmem_limit_bytes=32 << 20),
        cost_estimate=cost(2),
        name="piece_rims",
    )(picks, first, last)


def rims(first, last):
    both = jnp.concatenate([lon_shift(first, -1), lon_shift(last, 1)], 0)
    return dotg(both, jnp.concatenate(edge_picks(), 0), 0, 0).astype(BF)


PLANES = [[16 * half + i for i in range(16)] for half in range(2)]


def plane_exchange(pieces):
    return lax.all_to_all(pieces, "lon", 0, 0, axis_index_groups=PLANES)


def total_kernel(*refs):
    total = refs[0][0].astype(F32)
    for i in range(1, 16):
        total = total + refs[0][i].astype(F32)
    refs[-1][...] = total.astype(BF)


def plane_total(pieces, after):
    return pl.pallas_call(
        total_kernel,
        out_shape=jax.ShapeDtypeStruct((PIECE, LANES), BF),
        grid=(1,),
        in_specs=[full((16, PIECE, LANES))] + [pl.BlockSpec(memory_space=pl.ANY)] * len(after),
        out_specs=full((PIECE, LANES)),
        compiler_params=pltpu.CompilerParams(vmem_limit_bytes=32 << 20),
        cost_estimate=cost(1.2),
        name="plane_total",
    )(pieces, *after)


def copies_kernel(part, *refs):
    out = refs[-1]
    for i in range(16):
        out[i] = part[...]


def plane_copies(part, after):
    return pl.pallas_call(
        copies_kernel,
        out_shape=jax.ShapeDtypeStruct((16, PIECE, LANES), BF),
        grid=(1,),
        in_specs=[full((PIECE, LANES))] + [pl.BlockSpec(memory_space=pl.ANY)] * len(after),
        out_specs=full((16, PIECE, LANES)),
        compiler_params=pltpu.CompilerParams(vmem_limit_bytes=32 << 20),
        cost_estimate=cost(1),
        name="plane_copies",
    )(part, *after)


def reduce_gradients(keep, send, late, first, last):
    mine = (keep.astype(F32) + ch_swap(send, 1).astype(F32)).astype(BF)
    mine = plane_exchange(mine.reshape(16, PIECE, LANES))
    mine, first, last = lax.optimization_barrier((mine, first, last))
    from_right, from_left = lon_shift(first, -1), lon_shift(last, 1)
    wire = plane_total(mine, late)
    part = (
        (wire.astype(F32) + lon_swap(wire, 16).astype(F32))
        + (ch_swap(wire, 2).astype(F32) + both_swap(wire).astype(F32))
    ).astype(BF)
    copies = plane_copies(part, (from_right, from_left))
    return plane_exchange(copies).reshape(WIRE, LANES), from_right, from_left


def finish_kernel(core_ref, own, other, pad, grad_in, grad_out, held):
    core = core_ref[0]
    for wire, slot in ((own, core), (other, 1 - core)):
        for t in range(3):
            held[slot, :, t * LANES : (t + 1) * LANES] = wire[t * HID : (t + 1) * HID, :]
        rest = wire[3 * HID : 3 * HID + 400, :]
        for q in range(4):
            held[slot, q * 400 : (q + 1) * 400, 3 * LANES :] = rest[:, q * 32 : (q + 1) * 32]
    factor = 1.0 / math.sqrt(ROWS * LANES * 32)
    grad_in[...] = dotg(pad[...], held[0], 1, 1) * factor
    grad_out[...] = dotg(pad[...], held[1], 1, 1) * factor


def finish(core, own, other, pad):
    return pl.pallas_call(
        finish_kernel,
        out_shape=[
            jax.ShapeDtypeStruct((C, HID), F32),
            jax.ShapeDtypeStruct((C, HID), F32),
        ],
        grid=(1,),
        in_specs=[
            pl.BlockSpec(memory_space=pltpu.SMEM),
            full((WIRE, LANES)),
            full((WIRE, LANES)),
            full((C, 4 * CP)),
        ],
        out_specs=[full((C, HID))] * 2,
        scratch_shapes=[pltpu.VMEM((2, HID, 4 * CP), BF)],
        compiler_params=pltpu.CompilerParams(vmem_limit_bytes=32 << 20),
        cost_estimate=cost(6),
        name="finish",
    )(core, own, other, pad)


def both_swap(x):
    return lax.ppermute(x, ("lon", "ch"), [(i, i ^ (16 * 4 + 2)) for i in range(128)])


def body(
    ocean_state,
    sea_mask,
    kernel,
    conv_bias,
    norm_gain,
    norm_bias,
    weight_in,
    bias_in,
    weight_out,
    bias_out,
    layer_scale,
    cotangent,
):
    ch = lax.axis_index("ch")
    me = ch.reshape(1)
    core = (ch & 1).reshape(1)
    scale = jnp.pad(layer_scale, (0, CP - LC)).reshape(CP, 1)

    head, tail = edge_picks()
    state2d = ocean_state.reshape(LC * ROWS, LANES)
    sent = {}
    first = edge(state2d, head)
    sent[2] = branch_share(me, cotangent, sea_mask, scale, 2, (first,))
    last = edge(state2d, tail, (sent[2],))
    sent[3] = branch_share(me, cotangent, sea_mask, scale, 3, (last,))
    sent[1] = branch_share(me, cotangent, sea_mask, scale, 1, (sent[3],))
    sent[0] = branch_share(me, cotangent, sea_mask, scale, 0, (sent[1],))
    gs = [sent[0]] + [ch_swap(sent[k], k) for k in (1, 2, 3)]

    chan = jnp.arange(C)
    padded = jnp.arange(4 * CP)
    pad = ((chan // LC * CP + chan % LC)[:, None] == padded[None, :]).astype(BF)
    pad_own = (((chan // LC ^ ch) * CP + chan % LC)[:, None] == padded[None, :]).astype(BF)
    vec = jnp.stack([norm_gain, norm_bias, bias_out], 1).reshape(4, LC, 3)
    vec = jnp.pad(vec, ((0, 0), (0, CP - LC), (0, 0)))
    vec = jnp.concatenate([lax.dynamic_index_in_dim(vec, ch ^ k, 0, False) for k in range(4)], 0)

    state_rim = rims(first, last).reshape(LC, ROWS, LANES)
    bias = jnp.broadcast_to(conv_bias[:, None, None], (LC, 1, LANES))
    conv = conv_forward(me, ocean_state, state_rim, tap_patterns(kernel), bias)
    win, win_t, wout_t, wout = padded_weights(weight_in, weight_out.T, pad_own, conv[:1])
    weights, gs, second = lax.optimization_barrier(((win_t, win, wout, wout_t), gs, conv[4:]))
    xs = [
        [half[0]] + [ch_swap(half[k], k) for k in (1, 2, 3)] for half in (conv[:4], second)
    ]

    bias_rows = bias_in.reshape(HID, 1)
    early, _, (hid_a, cells_a) = mlp(0, me, core, xs[0], gs, weights, vec, bias_rows)
    early, second = lax.optimization_barrier((early, xs[1]))
    saved = (hid_a, cells_a.reshape(2, 4 * CP, 2 * CELLS))
    grad_b, branch_b, (keep, send) = mlp(
        1, me, core, second, gs, weights, vec, bias_rows, saved, early[:1]
    )
    early = [early[0]] + [ch_swap(early[k], k) for k in (1, 2, 3)]
    keep, send, early = lax.optimization_barrier((keep, send, early))
    grad_b = [grad_b[0]] + [ch_swap(grad_b[k], k) for k in (1, 2, 3)]
    branch_b = [branch_b[0]] + [ch_swap(branch_b[k], k) for k in (1, 2, 3)]
    grad_b, branch_b = lax.optimization_barrier((grad_b, branch_b))
    updated = update(me, early, branch_b, ocean_state, sea_mask, scale)
    picks = jnp.concatenate([head, tail], 0)
    first, last = piece_edges(picks, early, grad_b)
    own, from_right, from_left = reduce_gradients(
        keep, send, branch_b[1:], first, last
    )
    grad_rims = piece_rims(picks, from_right, from_left)

    grad_state = conv_backward(
        me,
        early,
        grad_b,
        grad_rims,
        tap_patterns(kernel[:, ::-1]),
        cotangent,
        sea_mask,
    )
    own, grad_state, updated = lax.optimization_barrier((own, grad_state, updated))
    grad_in, grad_out = finish(core, own, ch_swap(own, 1), pad)
    return updated, grad_state, grad_in, grad_out.T


def solution(mesh):
    return jax.shard_map(
        body,
        mesh=mesh,
        in_specs=(
            P("ch", None, "lon"),
            P(None, "lon"),
            P("ch", None),
            P("ch"),
            P(),
            P(),
            P(),
            P(),
            P(),
            P(),
            P("ch"),
            P("ch", None, "lon"),
        ),
        out_specs=(P("ch", None, "lon"), P("ch", None, "lon"), P(), P()),
        check_vma=False,
    )
```

```python
import functools
import math

import jax
import jax.numpy as jnp
from jax import lax
from jax.experimental import pallas as pl
from jax.experimental.pallas import tpu as pltpu
from jax.sharding import PartitionSpec as P

KW = 7
RIM = KW // 2
C = 400
HID = 1600
ROWS = 64
LANES = 128
LC = 100
CP = 104
QR = 16
HR = 8
GROUP = 8
VMEM = 63 << 20
BF = jnp.bfloat16
F32 = jnp.float32

root_coef = math.sqrt(2.0 / math.pi)
cubic_coef = 0.044715
norm_eps = 1e-06


def dotg(a, b, ca, cb):
    return lax.dot_general(a, b, (((ca,), (cb,)), ((), ())), preferred_element_type=F32)


def cost(micros):
    return pl.CostEstimate(flops=0, bytes_accessed=int(micros * 3.3e6), transcendentals=0)


def full(shape):
    return pl.BlockSpec(shape, lambda *i: (0,) * len(shape), pipeline_mode=pl.Buffered(1))


def ch_swap(x, k):
    return lax.ppermute(x, "ch", [(i, i ^ k) for i in range(4)])


def lon_shift(x, d):
    return lax.ppermute(x, "lon", [(i, (i + d) % 32) for i in range(32)])


def lon_swap(x, k):
    return lax.ppermute(x, "lon", [(i, i ^ k) for i in range(32)])


def share_kernel(me_ref, cot_ref, mask_ref, scale_ref, *refs):
    out_ref = refs[-1]
    cells = cot_ref[...].astype(F32)
    cells = jnp.concatenate([cells, jnp.zeros((CP - LC, QR, LANES), F32)], axis=0)
    cells = jnp.swapaxes(cells, 0, 1)
    mask = mask_ref[...].astype(F32)
    out_ref[...] = ((cells * mask[:, None, :]) * scale_ref[...][None]).astype(BF)


def branch_share(me, cotangent, sea_mask, scale, k, after):
    return pl.pallas_call(
        share_kernel,
        out_shape=jax.ShapeDtypeStruct((QR, CP, LANES), BF),
        grid_spec=pltpu.PrefetchScalarGridSpec(
            num_scalar_prefetch=1,
            grid=(1,),
            in_specs=[
                pl.BlockSpec((LC, QR, LANES), lambda i, me: (0, me[0] ^ k, 0)),
                pl.BlockSpec((QR, LANES), lambda i, me: (me[0] ^ k, 0)),
                pl.BlockSpec((CP, 1), lambda i, me: (0, 0)),
            ]
            + [pl.BlockSpec(memory_space=pl.ANY)] * len(after),
            out_specs=pl.BlockSpec((QR, CP, LANES), lambda i, me: (0, 0, 0)),
        ),
        compiler_params=pltpu.CompilerParams(vmem_limit_bytes=32 << 20),
        cost_estimate=cost(1.2),
        name="branch_share",
    )(me, cotangent, sea_mask, scale, *after)


def conv_channel(cells, rim, pattern, lane, band):
    moved = []
    for off in range(-RIM, RIM + 1):
        if off == 0:
            moved.append(cells.astype(BF))
        else:
            edge = lane < off if off > 0 else lane >= LANES + off
            moved.append(pltpu.roll(jnp.where(edge, rim, cells), (-off) % LANES, 1).astype(BF))
    stacked = jnp.concatenate(moved, axis=0)
    tiles = []
    for t in range(4):
        row = jnp.broadcast_to(pattern[t : t + 1, :], (ROWS, LANES))
        row = pltpu.roll(row, 0, 1, stride=1, stride_axis=0)
        tiles.append(jnp.where(band, row, 0.0).astype(BF))
    banded = jnp.concatenate(tiles, axis=1)[:, : KW * ROWS]
    return jnp.dot(banded, stacked, preferred_element_type=F32)


def masks():
    lane = lax.broadcasted_iota(jnp.int32, (ROWS, LANES), 1)
    row = lax.broadcasted_iota(jnp.int32, (ROWS, LANES), 0)
    away = (lane & (ROWS - 1)) - row
    return lane, (away >= -RIM) & (away <= RIM)


def forward_kernel(me_ref, state_ref, rim_ref, pat_ref, bias_ref, *refs):
    held = refs[-1]
    step = pl.program_id(0)
    lane, band = masks()
    outs = []
    for c in range(GROUP):
        total = conv_channel(
            state_ref[c].astype(F32), rim_ref[c].astype(F32), pat_ref[c], lane, band
        )
        total = total + bias_ref[c]
        outs.append(jnp.where(step * GROUP + c < LC, total, 0.0))
    held[...] = jnp.swapaxes(jnp.stack(outs, 0), 0, 1).reshape(4, QR, GROUP, LANES)
    me = me_ref[0]
    for k in range(4):
        share = held[me ^ k].astype(BF)
        refs[k][...] = share[:HR]
        refs[4 + k][...] = share[HR:]


def conv_forward(me, state, rim, pattern, bias):
    share = pltpu.HBM((HR, CP, LANES), BF)
    return pl.pallas_call(
        forward_kernel,
        out_shape=[share] * 8,
        grid_spec=pltpu.PrefetchScalarGridSpec(
            num_scalar_prefetch=1,
            grid=(CP // GROUP,),
            in_specs=[
                pl.BlockSpec((GROUP, ROWS, LANES), lambda i, me: (i, 0, 0)),
                pl.BlockSpec((GROUP, ROWS, LANES), lambda i, me: (i, 0, 0)),
                pl.BlockSpec((GROUP, 4, LANES), lambda i, me: (i, 0, 0)),
                pl.BlockSpec((GROUP, 1, LANES), lambda i, me: (i, 0, 0)),
            ],
            out_specs=[pl.BlockSpec((HR, GROUP, LANES), lambda i, me: (0, i, 0))] * 8,
            scratch_shapes=[pltpu.VMEM((4, QR, GROUP, LANES), F32)],
        ),
        compiler_params=pltpu.CompilerParams(vmem_limit_bytes=32 << 20),
        cost_estimate=cost(9),
        name="conv_forward",
    )(me, state, rim, pattern, bias)


def backward_kernel(me_ref, *refs):
    pieces = refs[:8]
    rims_in, pat_ref, cot_ref, mask_ref, out_ref, held, held_rim = refs[8:]
    lane, band = masks()
    me = me_ref[0]
    for k in range(4):
        held[me ^ k, :HR] = pieces[k][...].astype(F32)
        held[me ^ k, HR:] = pieces[4 + k][...].astype(F32)
        held_rim[me ^ k, :HR] = rims_in[k].astype(F32)
        held_rim[me ^ k, HR:] = rims_in[4 + k].astype(F32)
    cells = jnp.swapaxes(held[...].reshape(ROWS, GROUP, LANES), 0, 1)
    rims = jnp.swapaxes(held_rim[...].reshape(ROWS, GROUP, LANES), 0, 1)
    mask = mask_ref[...].astype(F32)
    for c in range(GROUP):
        total = conv_channel(cells[c], rims[c], pat_ref[c], lane, band)
        out_ref[c] = (cot_ref[c].astype(F32) * mask + total).astype(BF)


def conv_backward(me, early, late, rims, pattern, cotangent, sea_mask):
    return pl.pallas_call(
        backward_kernel,
        out_shape=jax.ShapeDtypeStruct((LC, ROWS, LANES), BF),
        grid_spec=pltpu.PrefetchScalarGridSpec(
            num_scalar_prefetch=1,
            grid=(CP // GROUP,),
            in_specs=[pl.BlockSpec((None, HR, GROUP, LANES), lambda i, me: (0, 0, i, 0))] * 4
            + [pl.BlockSpec((HR, GROUP, LANES), lambda i, me: (0, i, 0))] * 4
            + [
                pl.BlockSpec((8, HR, GROUP, LANES), lambda i, me: (0, 0, i, 0)),
                pl.BlockSpec((GROUP, 4, LANES), lambda i, me: (i, 0, 0)),
                pl.BlockSpec((GROUP, ROWS, LANES), lambda i, me: (i, 0, 0)),
                pl.BlockSpec((ROWS, LANES), lambda i, me: (0, 0)),
            ],
            out_specs=pl.BlockSpec((GROUP, ROWS, LANES), lambda i, me: (i, 0, 0)),
            scratch_shapes=[pltpu.VMEM((4, QR, GROUP, LANES), F32)] * 2,
        ),
        compiler_params=pltpu.CompilerParams(vmem_limit_bytes=VMEM),
        cost_estimate=cost(10),
        name="conv_backward",
    )(me, *early, *late, rims, pattern, cotangent, sea_mask)


SUB = 4
CELLS = SUB * LANES
HT = 400
PIECE = 328
WIRE = 16 * PIECE


def mlp_kernel(half, me_ref, core_ref, *refs):
    xs, gs = refs[:4], refs[4:8]
    win_t, win, wout, wout_t, vec, bias_in = refs[8:14]
    if half:
        hid_in, cells_in = refs[14:16]
        grad_out, branch_out, wires = refs[17:21], refs[21:25], refs[25:27]
        hidden, cells, hid_a, cells_a, held, sems = refs[27:]
        copies = (
            pltpu.make_async_copy(hid_in, hid_a, sems.at[0]),
            pltpu.make_async_copy(cells_in, cells_a, sems.at[1]),
        )
    else:
        both_out = refs[14:18]
        hidden, cells = refs[18:]
    step = pl.program_id(0)
    me = me_ref[0]
    if half:

        @pl.when(step == 0)
        def _():
            for copy in copies:
                copy.start()

        lanes = pl.ds(pl.multiple_of(step * CELLS, CELLS), CELLS)
    else:
        lanes = slice(0, CELLS)

    def gather(pieces):
        return jnp.concatenate(
            [
                jnp.concatenate([p[r].astype(F32) for r in range(SUB)], axis=1)
                for p in pieces
            ],
            axis=0,
        )

    gain = vec[:, 0:1]
    values = gather(xs)
    mean_val = jnp.sum(values, axis=0, keepdims=True) / C
    square = jnp.sum(values * values, axis=0, keepdims=True) / C
    inv_std = lax.rsqrt(square - mean_val * mean_val + norm_eps)
    normed = (values - mean_val) * inv_std * gain + vec[:, 1:2]
    grads = gather(gs)
    for k in range(4):
        rows = slice(k * CP, (k + 1) * CP)
        cells[0, me ^ k, :, lanes] = normed[rows].astype(cells.dtype)
        cells[1, me ^ k, :, lanes] = grads[rows].astype(cells.dtype)
    normed, grads = normed.astype(BF), grads.astype(BF)
    for t in range(HID // HT):
        rows = slice(t * HT, (t + 1) * HT)
        pre = jnp.dot(win_t[rows, :], normed, preferred_element_type=F32) + bias_in[rows, :]
        gact = jnp.dot(wout[rows, :], grads, preferred_element_type=F32)
        sq = pre * pre
        tangent = jnp.tanh(pre * (root_coef + (root_coef * cubic_coef) * sq))
        side = 0.5 + 0.5 * tangent
        value = pre * side
        slope = side + value * (1.0 - side) * (
            2.0 * root_coef + (6.0 * root_coef * cubic_coef) * sq
        )
        hidden[0, rows, lanes] = (gact * slope).astype(BF)
        hidden[1, rows, lanes] = value.astype(BF)
    x_grad = jnp.dot(win[...], hidden[0, :, lanes], preferred_element_type=F32) * gain
    centred = (values - mean_val) * inv_std
    first = jnp.sum(x_grad, axis=0, keepdims=True) / C
    second = jnp.sum(x_grad * centred, axis=0, keepdims=True) / C
    x_grad = inv_std * (x_grad - first - centred * second)
    branch = jnp.dot(wout_t[...], hidden[1, :, lanes], preferred_element_type=F32)
    branch = branch + vec[:, 2:3]
    for k in range(4):
        for r in range(SUB):
            here = slice(r * LANES, (r + 1) * LANES)
            grad_piece = x_grad[k * CP : (k + 1) * CP, here].astype(BF)
            branch_piece = branch[k * CP : (k + 1) * CP, here].astype(BF)
            if half:
                grad_out[k][r] = grad_piece
                branch_out[k][r] = branch_piece
            else:
                both_out[k][0, r] = grad_piece
                both_out[k][1, r] = branch_piece
    if not half:
        return

    @pl.when(step == 1)
    def _():
        for copy in copies:
            copy.wait()
        core = core_ref[0]
        for out, slot in ((wires[0], core), (wires[1], 1 - core)):
            cells_b = cells[slot].reshape(4 * CP, 2 * CELLS).astype(BF)
            held[...] = dotg(hid_a[slot], cells_a[slot], 1, 1) + dotg(hidden[slot], cells_b, 1, 1)
            for t in range(3):
                out[t * HID : (t + 1) * HID, :] = held[:, t * LANES : (t + 1) * LANES].astype(BF)
            rest = [held[q * 400 : (q + 1) * 400, 3 * LANES :] for q in range(4)]
            out[3 * HID : 3 * HID + 400, :] = jnp.concatenate(rest, axis=1).astype(BF)
            out[3 * HID + 400 :, :] = jnp.zeros((WIRE - 3 * HID - 400, LANES), BF)


def mlp(half, me, core, xs, gs, weights, vec, bias_in, saved=(), after=()):
    any_space = pl.BlockSpec(memory_space=pl.ANY)

    def whole(shape):
        return pl.BlockSpec(
            shape, lambda i, me, core: (0,) * len(shape), pipeline_mode=pl.Buffered(1)
        )

    piece = pl.BlockSpec((SUB, CP, LANES), lambda i, me, core: (i, 0, 0))
    later = pl.BlockSpec((SUB, CP, LANES), lambda i, me, core: (2 * half + i, 0, 0))
    if half:
        shapes = [jax.ShapeDtypeStruct((WIRE, LANES), BF)] * 2
        specs = [whole((WIRE, LANES))] * 2
        scratch = [
            pltpu.VMEM((2, HID, 2 * CELLS), BF),
            pltpu.VMEM((2, 4, CP, 2 * CELLS), F32),
            pltpu.VMEM((2, HID, 2 * CELLS), BF),
            pltpu.VMEM((2, 4 * CP, 2 * CELLS), BF),
            pltpu.VMEM((HID, 4 * CP), F32),
            pltpu.SemaphoreType.DMA((2,)),
        ]
    else:
        shapes = [
            jax.ShapeDtypeStruct((2, HID, 2 * CELLS), BF),
            jax.ShapeDtypeStruct((2, 4, CP, 2 * CELLS), BF),
        ]
        specs = [
            pl.BlockSpec((2, HID, CELLS), lambda i, me, core: (0, 0, i)),
            pl.BlockSpec((2, 4, CP, CELLS), lambda i, me, core: (0, 0, 0, i)),
        ]
        scratch = []
    count = 8 if half else 4
    result = (HR, CP, LANES) if half else (2, HR, CP, LANES)
    place = piece
    if not half:
        place = pl.BlockSpec((2, SUB, CP, LANES), lambda i, me, core: (0, i, 0, 0))
    outs = pl.pallas_call(
        functools.partial(mlp_kernel, half),
        out_shape=[jax.ShapeDtypeStruct(result, BF)] * count + shapes,
        grid_spec=pltpu.PrefetchScalarGridSpec(
            num_scalar_prefetch=2,
            grid=(2,),
            in_specs=[piece] * 4
            + [later] * 4
            + [
                whole((HID, 4 * CP)),
                whole((4 * CP, HID)),
                whole((HID, 4 * CP)),
                whole((4 * CP, HID)),
                whole((4 * CP, 3)),
                whole((HID, 1)),
            ]
            + [any_space] * (len(saved) + len(after)),
            out_specs=[place] * count + specs,
            scratch_shapes=scratch,
        ),
        compiler_params=pltpu.CompilerParams(vmem_limit_bytes=VMEM),
        cost_estimate=cost(22 if half else 14),
        name="mlp_b" if half else "mlp_a",
    )(me, core, *xs, *gs, *weights, vec, bias_in, *saved, *after)
    return outs[:4], outs[4:count], outs[count:]


def update_kernel(me_ref, *refs):
    k = pl.program_id(0)
    state_ref, mask_ref, scale_ref, out_ref, held = refs[8:]

    def take(early, late):
        held[:HR] = early[...]
        held[HR:] = late[...]

    for i in range(4):
        pl.when(k == i)(lambda i=i: take(refs[i], refs[4 + i]))
    branch = jnp.swapaxes(held[...].astype(F32) * scale_ref[...][None], 0, 1)[:LC]
    mask = mask_ref[...].astype(F32)
    out_ref[...] = (mask[None] * (state_ref[...].astype(F32) + branch)).astype(BF)


def update(me, early, late, state, sea_mask, scale):
    whole = pl.BlockSpec((HR, CP, LANES), lambda i, me: (0, 0, 0), pipeline_mode=pl.Buffered(1))
    return pl.pallas_call(
        update_kernel,
        out_shape=jax.ShapeDtypeStruct((LC, ROWS, LANES), BF),
        grid_spec=pltpu.PrefetchScalarGridSpec(
            num_scalar_prefetch=1,
            grid=(4,),
            in_specs=[
                pl.BlockSpec(
                    (None, HR, CP, LANES),
                    lambda i, me: (1, 0, 0, 0),
                    pipeline_mode=pl.Buffered(1),
                )
            ]
            * 4
            + [whole] * 4
            + [
                pl.BlockSpec((LC, QR, LANES), lambda i, me: (0, me[0] ^ i, 0)),
                pl.BlockSpec((QR, LANES), lambda i, me: (me[0] ^ i, 0)),
                pl.BlockSpec((CP, 1), lambda i, me: (0, 0)),
            ],
            out_specs=pl.BlockSpec((LC, QR, LANES), lambda i, me: (0, me[0] ^ i, 0)),
            scratch_shapes=[pltpu.VMEM((QR, CP, LANES), BF)],
        ),
        compiler_params=pltpu.CompilerParams(vmem_limit_bytes=VMEM),
        cost_estimate=cost(4.4),
        name="update",
    )(me, *early, *late, state, sea_mask, scale)


def weights_kernel(one, two, pad, *refs):
    one_out, one_t, two_out, two_t = refs[-4:]
    for source, out, turned in ((one, one_out, one_t), (two, two_out, two_t)):
        padded = dotg(pad[...], source[...], 0, 0)
        out[...] = padded.astype(BF)
        turned[...] = padded.T.astype(BF)


def padded_weights(one, two, pad, after):
    flat = pltpu.HBM((4 * CP, HID), BF)
    turned = pltpu.HBM((HID, 4 * CP), BF)
    return pl.pallas_call(
        weights_kernel,
        out_shape=[flat, turned, flat, turned],
        grid=(1,),
        in_specs=[full((C, HID)), full((C, HID)), full((C, 4 * CP))]
        + [pl.BlockSpec(memory_space=pl.ANY)] * len(after),
        out_specs=[full(x.shape) for x in (flat, turned, flat, turned)],
        compiler_params=pltpu.CompilerParams(vmem_limit_bytes=32 << 20),
        cost_estimate=cost(5),
        name="padded_weights",
    )(one, two, pad, *after)


def tap_patterns(kernel):
    lane = jnp.arange(4 * LANES)
    tile, pos = lane // LANES, lane % LANES
    away = jnp.where(pos % ROWS < ROWS // 2, pos % ROWS, pos % ROWS - ROWS)
    side = ((pos - away) // ROWS) % 2
    col = 2 * tile + side
    tap = jnp.where((jnp.abs(away) <= RIM) & (col < KW), (away + RIM) * KW + col, -1)
    pick = (jnp.arange(KW * KW)[:, None] == tap[None, :]).astype(BF)
    return jnp.dot(kernel.astype(BF), pick, preferred_element_type=F32).reshape(LC, 4, LANES)


def edge_picks():
    row = jnp.arange(8)[:, None]
    lane = jnp.arange(LANES)[None, :]
    head = ((row < RIM) & (lane == row)).astype(BF)
    tail = ((row < RIM) & (lane == LANES - RIM + row)).astype(BF)
    return head, tail


def edge_kernel(cells, pick, *refs):
    refs[-1][...] = dotg(pick[...], cells[...], 1, 1).astype(BF)


def edge(cells2d, pick, after=()):
    return pl.pallas_call(
        edge_kernel,
        out_shape=jax.ShapeDtypeStruct((8, cells2d.shape[0]), BF),
        grid=(1,),
        in_specs=[full(cells2d.shape), full(pick.shape)]
        + [pl.BlockSpec(memory_space=pl.ANY)] * len(after),
        out_specs=full((8, cells2d.shape[0])),
        compiler_params=pltpu.CompilerParams(vmem_limit_bytes=32 << 20),
        cost_estimate=cost(1),
        name="edge",
    )(cells2d, pick, *after)


def piece_edges_kernel(pick, *refs):
    first, last = refs[8:]
    for i in range(8):
        cells = refs[i][...].reshape(HR * CP, LANES)
        both = dotg(pick[...], cells, 1, 1).astype(BF)
        first[i] = both[:8]
        last[i] = both[8:]


def piece_edges(picks, early, late):
    half = pl.BlockSpec((QR // 2, CP, LANES), lambda i: (0, 0, 0))
    whole = pl.BlockSpec((8, 8, HR * CP), lambda i: (0, 0, 0))
    out = pltpu.HBM((8, 8, HR * CP), BF)
    return pl.pallas_call(
        piece_edges_kernel,
        out_shape=[out, out],
        grid=(1,),
        in_specs=[pl.BlockSpec((16, LANES), lambda i: (0, 0))]
        + [pl.BlockSpec((None, HR, CP, LANES), lambda i: (0, 0, 0, 0))] * 4
        + [half] * 4,
        out_specs=[whole] * 2,
        compiler_params=pltpu.CompilerParams(vmem_limit_bytes=32 << 20),
        cost_estimate=cost(2),
        name="piece_edges",
    )(picks, *early, *late)


def piece_rims_kernel(pick, first, last, out):
    for i in range(8):
        both = jnp.concatenate([first[i], last[i]], axis=0)
        out[i] = dotg(both, pick[...], 0, 0).astype(BF).reshape(HR, CP, LANES)


def piece_rims(picks, first, last):
    return pl.pallas_call(
        piece_rims_kernel,
        out_shape=jax.ShapeDtypeStruct((8, HR, CP, LANES), BF),
        grid=(1,),
        in_specs=[full((16, LANES)), full((8, 8, HR * CP)), full((8, 8, HR * CP))],
        out_specs=full((8, HR, CP, LANES)),
        compiler_params=pltpu.CompilerParams(vmem_limit_bytes=32 << 20),
        cost_estimate=cost(2),
        name="piece_rims",
    )(picks, first, last)


def rims(first, last):
    both = jnp.concatenate([lon_shift(first, -1), lon_shift(last, 1)], 0)
    return dotg(both, jnp.concatenate(edge_picks(), 0), 0, 0).astype(BF)


PLANES = [[16 * half + i for i in range(16)] for half in range(2)]


def plane_exchange(pieces):
    return lax.all_to_all(pieces, "lon", 0, 0, axis_index_groups=PLANES)


def total_kernel(*refs):
    total = refs[0][0].astype(F32)
    for i in range(1, 16):
        total = total + refs[0][i].astype(F32)
    refs[-1][...] = total.astype(BF)


def plane_total(pieces, after):
    return pl.pallas_call(
        total_kernel,
        out_shape=jax.ShapeDtypeStruct((PIECE, LANES), BF),
        grid=(1,),
        in_specs=[full((16, PIECE, LANES))] + [pl.BlockSpec(memory_space=pl.ANY)] * len(after),
        out_specs=full((PIECE, LANES)),
        compiler_params=pltpu.CompilerParams(vmem_limit_bytes=32 << 20),
        cost_estimate=cost(1.2),
        name="plane_total",
    )(pieces, *after)


def copies_kernel(part, *refs):
    out = refs[-1]
    for i in range(16):
        out[i] = part[...]


def plane_copies(part, after):
    return pl.pallas_call(
        copies_kernel,
        out_shape=jax.ShapeDtypeStruct((16, PIECE, LANES), BF),
        grid=(1,),
        in_specs=[full((PIECE, LANES))] + [pl.BlockSpec(memory_space=pl.ANY)] * len(after),
        out_specs=full((16, PIECE, LANES)),
        compiler_params=pltpu.CompilerParams(vmem_limit_bytes=32 << 20),
        cost_estimate=cost(1),
        name="plane_copies",
    )(part, *after)


def reduce_gradients(mine, late, from_right, from_left):
    mine = plane_exchange(mine.reshape(16, PIECE, LANES))
    mine, from_right, from_left = lax.optimization_barrier((mine, from_right, from_left))
    wire = plane_total(mine, late)
    part = (
        (wire.astype(F32) + lon_swap(wire, 16).astype(F32))
        + (ch_swap(wire, 2).astype(F32) + both_swap(wire).astype(F32))
    ).astype(BF)
    return plane_exchange(plane_copies(part, ())).reshape(WIRE, LANES), from_right, from_left


def finish_kernel(core_ref, own, other, pad, grad_in, grad_out, held):
    core = core_ref[0]
    for wire, slot in ((own, core), (other, 1 - core)):
        for t in range(3):
            held[slot, :, t * LANES : (t + 1) * LANES] = wire[t * HID : (t + 1) * HID, :]
        rest = wire[3 * HID : 3 * HID + 400, :]
        for q in range(4):
            held[slot, q * 400 : (q + 1) * 400, 3 * LANES :] = rest[:, q * 32 : (q + 1) * 32]
    factor = 1.0 / math.sqrt(ROWS * LANES * 32)
    grad_in[...] = dotg(pad[...], held[0], 1, 1) * factor
    grad_out[...] = dotg(pad[...], held[1], 1, 1) * factor


def finish(core, own, other, pad):
    return pl.pallas_call(
        finish_kernel,
        out_shape=[
            jax.ShapeDtypeStruct((C, HID), F32),
            jax.ShapeDtypeStruct((C, HID), F32),
        ],
        grid=(1,),
        in_specs=[
            pl.BlockSpec(memory_space=pltpu.SMEM),
            full((WIRE, LANES)),
            full((WIRE, LANES)),
            full((C, 4 * CP)),
        ],
        out_specs=[full((C, HID))] * 2,
        scratch_shapes=[pltpu.VMEM((2, HID, 4 * CP), BF)],
        compiler_params=pltpu.CompilerParams(vmem_limit_bytes=32 << 20),
        cost_estimate=cost(6),
        name="finish",
    )(core, own, other, pad)


def both_swap(x):
    return lax.ppermute(x, ("lon", "ch"), [(i, i ^ (16 * 4 + 2)) for i in range(128)])


def body(
    ocean_state,
    sea_mask,
    kernel,
    conv_bias,
    norm_gain,
    norm_bias,
    weight_in,
    bias_in,
    weight_out,
    bias_out,
    layer_scale,
    cotangent,
):
    ch = lax.axis_index("ch")
    me = ch.reshape(1)
    core = (ch & 1).reshape(1)
    scale = jnp.pad(layer_scale, (0, CP - LC)).reshape(CP, 1)

    head, tail = edge_picks()
    state2d = ocean_state.reshape(LC * ROWS, LANES)
    sent = {}
    first = edge(state2d, head)
    sent[2] = branch_share(me, cotangent, sea_mask, scale, 2, (first,))
    last = edge(state2d, tail, (sent[2],))
    sent[3] = branch_share(me, cotangent, sea_mask, scale, 3, (last,))
    sent[1] = branch_share(me, cotangent, sea_mask, scale, 1, (sent[3],))
    sent[0] = branch_share(me, cotangent, sea_mask, scale, 0, (sent[1],))
    gs = [sent[0]] + [ch_swap(sent[k], k) for k in (1, 2, 3)]

    chan = jnp.arange(C)
    padded = jnp.arange(4 * CP)
    pad = ((chan // LC * CP + chan % LC)[:, None] == padded[None, :]).astype(BF)
    pad_own = (((chan // LC ^ ch) * CP + chan % LC)[:, None] == padded[None, :]).astype(BF)
    vec = jnp.stack([norm_gain, norm_bias, bias_out], 1).reshape(4, LC, 3)
    vec = jnp.pad(vec, ((0, 0), (0, CP - LC), (0, 0)))
    vec = jnp.concatenate([lax.dynamic_index_in_dim(vec, ch ^ k, 0, False) for k in range(4)], 0)

    state_rim = rims(first, last).reshape(LC, ROWS, LANES)
    bias = jnp.broadcast_to(conv_bias[:, None, None], (LC, 1, LANES))
    conv = conv_forward(me, ocean_state, state_rim, tap_patterns(kernel), bias)
    win, win_t, wout_t, wout = padded_weights(weight_in, weight_out.T, pad_own, conv[:1])
    weights, gs, second = lax.optimization_barrier(((win_t, win, wout, wout_t), gs, conv[4:]))
    xs = [
        [half[0]] + [ch_swap(half[k], k) for k in (1, 2, 3)] for half in (conv[:4], second)
    ]

    bias_rows = bias_in.reshape(HID, 1)
    early, _, (hid_a, cells_a) = mlp(0, me, core, xs[0], gs, weights, vec, bias_rows)
    early, second = lax.optimization_barrier((early, xs[1]))
    saved = (hid_a, cells_a.reshape(2, 4 * CP, 2 * CELLS))
    grad_b, branch_b, (keep, send) = mlp(
        1, me, core, second, gs, weights, vec, bias_rows, saved, early[:1]
    )
    early = [early[0]] + [ch_swap(early[k], k) for k in (1, 2, 3)]
    keep, send, early = lax.optimization_barrier((keep, send, early))
    grad_b = [grad_b[0]] + [ch_swap(grad_b[k], k) for k in (1, 2, 3)]
    mine = (keep.astype(F32) + ch_swap(send, 1).astype(F32)).astype(BF)
    mine, grad_b, branch_b = lax.optimization_barrier((mine, grad_b, branch_b))
    branch_b = [branch_b[0]] + [ch_swap(branch_b[k], k) for k in (1, 2, 3)]
    updated = update(me, early, branch_b, ocean_state, sea_mask, scale)
    picks = jnp.concatenate([head, tail], 0)
    first, last = piece_edges(picks, early, grad_b)
    from_right, from_left = lon_shift(first, -1), lon_shift(last, 1)
    own, from_right, from_left = reduce_gradients(mine, branch_b[1:], from_right, from_left)
    grad_rims = piece_rims(picks, from_right, from_left)

    grad_state = conv_backward(
        me,
        early,
        grad_b,
        grad_rims,
        tap_patterns(kernel[:, ::-1]),
        cotangent,
        sea_mask,
    )
    own, grad_state, updated = lax.optimization_barrier((own, grad_state, updated))
    grad_in, grad_out = finish(core, own, ch_swap(own, 1), pad)
    return updated, grad_state, grad_in, grad_out.T


def solution(mesh):
    return jax.shard_map(
        body,
        mesh=mesh,
        in_specs=(
            P("ch", None, "lon"),
            P(None, "lon"),
            P("ch", None),
            P("ch"),
            P(),
            P(),
            P(),
            P(),
            P(),
            P(),
            P("ch"),
            P("ch", None, "lon"),
        ),
        out_specs=(P("ch", None, "lon"), P("ch", None, "lon"), P(), P()),
        check_vma=False,
    )
```

```python
import functools
import math

import jax
import jax.numpy as jnp
from jax import lax
from jax.experimental import pallas as pl
from jax.experimental.pallas import tpu as pltpu
from jax.sharding import PartitionSpec as P

KW = 7
RIM = KW // 2
C = 400
HID = 1600
ROWS = 64
LANES = 128
LC = 100
CP = 104
QR = 16
HR = 8
GROUP = 8
VMEM = 63 << 20
BF = jnp.bfloat16
F32 = jnp.float32

root_coef = math.sqrt(2.0 / math.pi)
cubic_coef = 0.044715
norm_eps = 1e-06


def dotg(a, b, ca, cb):
    return lax.dot_general(a, b, (((ca,), (cb,)), ((), ())), preferred_element_type=F32)


def cost(micros):
    return pl.CostEstimate(flops=0, bytes_accessed=int(micros * 3.3e6), transcendentals=0)


def full(shape):
    return pl.BlockSpec(shape, lambda *i: (0,) * len(shape), pipeline_mode=pl.Buffered(1))


def ch_swap(x, k):
    return lax.ppermute(x, "ch", [(i, i ^ k) for i in range(4)])


def lon_shift(x, d):
    return lax.ppermute(x, "lon", [(i, (i + d) % 32) for i in range(32)])


def lon_swap(x, k):
    return lax.ppermute(x, "lon", [(i, i ^ k) for i in range(32)])


def share_kernel(me_ref, cot_ref, mask_ref, scale_ref, *refs):
    out_ref = refs[-1]
    cells = cot_ref[...].astype(F32)
    cells = jnp.concatenate([cells, jnp.zeros((CP - LC, QR, LANES), F32)], axis=0)
    cells = jnp.swapaxes(cells, 0, 1)
    mask = mask_ref[...].astype(F32)
    out_ref[...] = ((cells * mask[:, None, :]) * scale_ref[...][None]).astype(BF)


def branch_share(me, cotangent, sea_mask, scale, k, after):
    return pl.pallas_call(
        share_kernel,
        out_shape=jax.ShapeDtypeStruct((QR, CP, LANES), BF),
        grid_spec=pltpu.PrefetchScalarGridSpec(
            num_scalar_prefetch=1,
            grid=(1,),
            in_specs=[
                pl.BlockSpec((LC, QR, LANES), lambda i, me: (0, me[0] ^ k, 0)),
                pl.BlockSpec((QR, LANES), lambda i, me: (me[0] ^ k, 0)),
                pl.BlockSpec((CP, 1), lambda i, me: (0, 0)),
            ]
            + [pl.BlockSpec(memory_space=pl.ANY)] * len(after),
            out_specs=pl.BlockSpec((QR, CP, LANES), lambda i, me: (0, 0, 0)),
        ),
        compiler_params=pltpu.CompilerParams(vmem_limit_bytes=32 << 20),
        cost_estimate=cost(1.2),
        name="branch_share",
    )(me, cotangent, sea_mask, scale, *after)


def conv_channel(cells, rim, pattern, lane, band):
    moved = []
    for off in range(-RIM, RIM + 1):
        if off == 0:
            moved.append(cells.astype(BF))
        else:
            edge = lane < off if off > 0 else lane >= LANES + off
            moved.append(pltpu.roll(jnp.where(edge, rim, cells), (-off) % LANES, 1).astype(BF))
    stacked = jnp.concatenate(moved, axis=0)
    tiles = []
    for t in range(4):
        row = jnp.broadcast_to(pattern[t : t + 1, :], (ROWS, LANES))
        row = pltpu.roll(row, 0, 1, stride=1, stride_axis=0)
        tiles.append(jnp.where(band, row, 0.0).astype(BF))
    banded = jnp.concatenate(tiles, axis=1)[:, : KW * ROWS]
    return jnp.dot(banded, stacked, preferred_element_type=F32)


def masks():
    lane = lax.broadcasted_iota(jnp.int32, (ROWS, LANES), 1)
    row = lax.broadcasted_iota(jnp.int32, (ROWS, LANES), 0)
    away = (lane & (ROWS - 1)) - row
    return lane, (away >= -RIM) & (away <= RIM)


def forward_kernel(me_ref, state_ref, rim_ref, pat_ref, bias_ref, *refs):
    held = refs[-1]
    step = pl.program_id(0)
    lane, band = masks()
    outs = []
    for c in range(GROUP):
        total = conv_channel(
            state_ref[c].astype(F32), rim_ref[c].astype(F32), pat_ref[c], lane, band
        )
        total = total + bias_ref[c]
        outs.append(jnp.where(step * GROUP + c < LC, total, 0.0))
    held[...] = jnp.swapaxes(jnp.stack(outs, 0), 0, 1).reshape(4, QR, GROUP, LANES)
    me = me_ref[0]
    for k in range(4):
        share = held[me ^ k].astype(BF)
        refs[k][...] = share[:HR]
        refs[4 + k][...] = share[HR:]


def conv_forward(me, state, rim, pattern, bias):
    share = pltpu.HBM((HR, CP, LANES), BF)
    return pl.pallas_call(
        forward_kernel,
        out_shape=[share] * 8,
        grid_spec=pltpu.PrefetchScalarGridSpec(
            num_scalar_prefetch=1,
            grid=(CP // GROUP,),
            in_specs=[
                pl.BlockSpec((GROUP, ROWS, LANES), lambda i, me: (i, 0, 0)),
                pl.BlockSpec((GROUP, ROWS, LANES), lambda i, me: (i, 0, 0)),
                pl.BlockSpec((GROUP, 4, LANES), lambda i, me: (i, 0, 0)),
                pl.BlockSpec((GROUP, 1, LANES), lambda i, me: (i, 0, 0)),
            ],
            out_specs=[pl.BlockSpec((HR, GROUP, LANES), lambda i, me: (0, i, 0))] * 8,
            scratch_shapes=[pltpu.VMEM((4, QR, GROUP, LANES), F32)],
        ),
        compiler_params=pltpu.CompilerParams(vmem_limit_bytes=VMEM),
        cost_estimate=cost(9),
        name="conv_forward",
    )(me, state, rim, pattern, bias)


def backward_kernel(me_ref, *refs):
    pieces = refs[:8]
    rims_in, pat_ref, cot_ref, mask_ref, out_ref, held, held_rim = refs[8:]
    lane, band = masks()
    me = me_ref[0]
    for k in range(4):
        held[me ^ k, :HR] = pieces[k][...].astype(F32)
        held[me ^ k, HR:] = pieces[4 + k][...].astype(F32)
        held_rim[me ^ k, :HR] = rims_in[k].astype(F32)
        held_rim[me ^ k, HR:] = rims_in[4 + k].astype(F32)
    cells = jnp.swapaxes(held[...].reshape(ROWS, GROUP, LANES), 0, 1)
    rims = jnp.swapaxes(held_rim[...].reshape(ROWS, GROUP, LANES), 0, 1)
    mask = mask_ref[...].astype(F32)
    for c in range(GROUP):
        total = conv_channel(cells[c], rims[c], pat_ref[c], lane, band)
        out_ref[c] = (cot_ref[c].astype(F32) * mask + total).astype(BF)


def conv_backward(me, early, late, rims, pattern, cotangent, sea_mask):
    return pl.pallas_call(
        backward_kernel,
        out_shape=jax.ShapeDtypeStruct((LC, ROWS, LANES), BF),
        grid_spec=pltpu.PrefetchScalarGridSpec(
            num_scalar_prefetch=1,
            grid=(CP // GROUP,),
            in_specs=[pl.BlockSpec((None, HR, GROUP, LANES), lambda i, me: (0, 0, i, 0))] * 4
            + [pl.BlockSpec((HR, GROUP, LANES), lambda i, me: (0, i, 0))] * 4
            + [
                pl.BlockSpec((8, HR, GROUP, LANES), lambda i, me: (0, 0, i, 0)),
                pl.BlockSpec((GROUP, 4, LANES), lambda i, me: (i, 0, 0)),
                pl.BlockSpec((GROUP, ROWS, LANES), lambda i, me: (i, 0, 0)),
                pl.BlockSpec((ROWS, LANES), lambda i, me: (0, 0)),
            ],
            out_specs=pl.BlockSpec((GROUP, ROWS, LANES), lambda i, me: (i, 0, 0)),
            scratch_shapes=[pltpu.VMEM((4, QR, GROUP, LANES), F32)] * 2,
        ),
        compiler_params=pltpu.CompilerParams(vmem_limit_bytes=VMEM),
        cost_estimate=cost(10),
        name="conv_backward",
    )(me, *early, *late, rims, pattern, cotangent, sea_mask)


SUB = 4
CELLS = SUB * LANES
HT = 400
PIECE = 328
WIRE = 16 * PIECE


def mlp_kernel(half, me_ref, core_ref, *refs):
    xs, gs = refs[:4], refs[4:8]
    win_t, win, wout, wout_t, vec, bias_in = refs[8:14]
    if half:
        hid_in, cells_in = refs[14:16]
        grad_out, branch_out, wires = refs[17:21], refs[21:25], refs[25:27]
        hidden, cells, hid_a, cells_a, held, sems = refs[27:]
        copies = (
            pltpu.make_async_copy(hid_in, hid_a, sems.at[0]),
            pltpu.make_async_copy(cells_in, cells_a, sems.at[1]),
        )
    else:
        both_out = refs[14:18]
        hidden, cells = refs[18:]
    step = pl.program_id(0)
    me = me_ref[0]
    if half:

        @pl.when(step == 0)
        def _():
            for copy in copies:
                copy.start()

        lanes = pl.ds(pl.multiple_of(step * CELLS, CELLS), CELLS)
    else:
        lanes = slice(0, CELLS)

    def gather(pieces):
        return jnp.concatenate(
            [
                jnp.concatenate([p[r].astype(F32) for r in range(SUB)], axis=1)
                for p in pieces
            ],
            axis=0,
        )

    gain = vec[:, 0:1]
    values = gather(xs)
    mean_val = jnp.sum(values, axis=0, keepdims=True) / C
    square = jnp.sum(values * values, axis=0, keepdims=True) / C
    inv_std = lax.rsqrt(square - mean_val * mean_val + norm_eps)
    normed = (values - mean_val) * inv_std * gain + vec[:, 1:2]
    grads = gather(gs)
    for k in range(4):
        rows = slice(k * CP, (k + 1) * CP)
        cells[0, me ^ k, :, lanes] = normed[rows].astype(cells.dtype)
        cells[1, me ^ k, :, lanes] = grads[rows].astype(cells.dtype)
    normed, grads = normed.astype(BF), grads.astype(BF)
    for t in range(HID // HT):
        rows = slice(t * HT, (t + 1) * HT)
        pre = jnp.dot(win_t[rows, :], normed, preferred_element_type=F32) + bias_in[rows, :]
        gact = jnp.dot(wout[rows, :], grads, preferred_element_type=F32)
        sq = pre * pre
        tangent = jnp.tanh(pre * (root_coef + (root_coef * cubic_coef) * sq))
        side = 0.5 + 0.5 * tangent
        value = pre * side
        slope = side + value * (1.0 - side) * (
            2.0 * root_coef + (6.0 * root_coef * cubic_coef) * sq
        )
        hidden[0, rows, lanes] = (gact * slope).astype(BF)
        hidden[1, rows, lanes] = value.astype(BF)
    x_grad = jnp.dot(win[...], hidden[0, :, lanes], preferred_element_type=F32) * gain
    centred = (values - mean_val) * inv_std
    first = jnp.sum(x_grad, axis=0, keepdims=True) / C
    second = jnp.sum(x_grad * centred, axis=0, keepdims=True) / C
    x_grad = inv_std * (x_grad - first - centred * second)
    branch = jnp.dot(wout_t[...], hidden[1, :, lanes], preferred_element_type=F32)
    branch = branch + vec[:, 2:3]
    for k in range(4):
        for r in range(SUB):
            here = slice(r * LANES, (r + 1) * LANES)
            grad_piece = x_grad[k * CP : (k + 1) * CP, here].astype(BF)
            branch_piece = branch[k * CP : (k + 1) * CP, here].astype(BF)
            if half:
                grad_out[k][r] = grad_piece
                branch_out[k][r] = branch_piece
            else:
                both_out[k][0, r] = grad_piece
                both_out[k][1, r] = branch_piece
    if not half:
        return

    @pl.when(step == 1)
    def _():
        for copy in copies:
            copy.wait()
        core = core_ref[0]
        for out, slot in ((wires[0], core), (wires[1], 1 - core)):
            cells_b = cells[slot].reshape(4 * CP, 2 * CELLS).astype(BF)
            held[...] = dotg(hid_a[slot], cells_a[slot], 1, 1) + dotg(hidden[slot], cells_b, 1, 1)
            for t in range(3):
                out[t * HID : (t + 1) * HID, :] = held[:, t * LANES : (t + 1) * LANES].astype(BF)
            rest = [held[q * 400 : (q + 1) * 400, 3 * LANES :] for q in range(4)]
            out[3 * HID : 3 * HID + 400, :] = jnp.concatenate(rest, axis=1).astype(BF)
            out[3 * HID + 400 :, :] = jnp.zeros((WIRE - 3 * HID - 400, LANES), BF)


def mlp(half, me, core, xs, gs, weights, vec, bias_in, saved=(), after=()):
    any_space = pl.BlockSpec(memory_space=pl.ANY)

    def whole(shape):
        return pl.BlockSpec(
            shape, lambda i, me, core: (0,) * len(shape), pipeline_mode=pl.Buffered(1)
        )

    piece = pl.BlockSpec((SUB, CP, LANES), lambda i, me, core: (i, 0, 0))
    later = pl.BlockSpec((SUB, CP, LANES), lambda i, me, core: (2 * half + i, 0, 0))
    if half:
        shapes = [jax.ShapeDtypeStruct((WIRE, LANES), BF)] * 2
        specs = [whole((WIRE, LANES))] * 2
        scratch = [
            pltpu.VMEM((2, HID, 2 * CELLS), BF),
            pltpu.VMEM((2, 4, CP, 2 * CELLS), F32),
            pltpu.VMEM((2, HID, 2 * CELLS), BF),
            pltpu.VMEM((2, 4 * CP, 2 * CELLS), BF),
            pltpu.VMEM((HID, 4 * CP), F32),
            pltpu.SemaphoreType.DMA((2,)),
        ]
    else:
        shapes = [
            jax.ShapeDtypeStruct((2, HID, 2 * CELLS), BF),
            jax.ShapeDtypeStruct((2, 4, CP, 2 * CELLS), BF),
        ]
        specs = [
            pl.BlockSpec((2, HID, CELLS), lambda i, me, core: (0, 0, i)),
            pl.BlockSpec((2, 4, CP, CELLS), lambda i, me, core: (0, 0, 0, i)),
        ]
        scratch = []
    count = 8 if half else 4
    result = (HR, CP, LANES) if half else (2, HR, CP, LANES)
    place = piece
    if not half:
        place = pl.BlockSpec((2, SUB, CP, LANES), lambda i, me, core: (0, i, 0, 0))
    outs = pl.pallas_call(
        functools.partial(mlp_kernel, half),
        out_shape=[jax.ShapeDtypeStruct(result, BF)] * count + shapes,
        grid_spec=pltpu.PrefetchScalarGridSpec(
            num_scalar_prefetch=2,
            grid=(2,),
            in_specs=[piece] * 4
            + [later] * 4
            + [
                whole((HID, 4 * CP)),
                whole((4 * CP, HID)),
                whole((HID, 4 * CP)),
                whole((4 * CP, HID)),
                whole((4 * CP, 3)),
                whole((HID, 1)),
            ]
            + [any_space] * (len(saved) + len(after)),
            out_specs=[place] * count + specs,
            scratch_shapes=scratch,
        ),
        compiler_params=pltpu.CompilerParams(vmem_limit_bytes=VMEM),
        cost_estimate=cost(22 if half else 14),
        name="mlp_b" if half else "mlp_a",
    )(me, core, *xs, *gs, *weights, vec, bias_in, *saved, *after)
    return outs[:4], outs[4:count], outs[count:]


def update_kernel(me_ref, *refs):
    k = pl.program_id(0)
    state_ref, mask_ref, scale_ref, out_ref, held = refs[8:]

    def take(early, late):
        held[:HR] = early[...]
        held[HR:] = late[...]

    for i in range(4):
        pl.when(k == i)(lambda i=i: take(refs[i], refs[4 + i]))
    branch = jnp.swapaxes(held[...].astype(F32) * scale_ref[...][None], 0, 1)[:LC]
    mask = mask_ref[...].astype(F32)
    out_ref[...] = (mask[None] * (state_ref[...].astype(F32) + branch)).astype(BF)


def update(me, early, late, state, sea_mask, scale):
    whole = pl.BlockSpec((HR, CP, LANES), lambda i, me: (0, 0, 0), pipeline_mode=pl.Buffered(1))
    return pl.pallas_call(
        update_kernel,
        out_shape=jax.ShapeDtypeStruct((LC, ROWS, LANES), BF),
        grid_spec=pltpu.PrefetchScalarGridSpec(
            num_scalar_prefetch=1,
            grid=(4,),
            in_specs=[
                pl.BlockSpec(
                    (None, HR, CP, LANES),
                    lambda i, me: (1, 0, 0, 0),
                    pipeline_mode=pl.Buffered(1),
                )
            ]
            * 4
            + [whole] * 4
            + [
                pl.BlockSpec((LC, QR, LANES), lambda i, me: (0, me[0] ^ i, 0)),
                pl.BlockSpec((QR, LANES), lambda i, me: (me[0] ^ i, 0)),
                pl.BlockSpec((CP, 1), lambda i, me: (0, 0)),
            ],
            out_specs=pl.BlockSpec((LC, QR, LANES), lambda i, me: (0, me[0] ^ i, 0)),
            scratch_shapes=[pltpu.VMEM((QR, CP, LANES), BF)],
        ),
        compiler_params=pltpu.CompilerParams(vmem_limit_bytes=VMEM),
        cost_estimate=cost(4.4),
        name="update",
    )(me, *early, *late, state, sea_mask, scale)


def weights_kernel(one, two, pad, *refs):
    one_out, one_t, two_out, two_t = refs[-4:]
    for source, out, turned in ((one, one_out, one_t), (two, two_out, two_t)):
        padded = dotg(pad[...], source[...], 0, 0)
        out[...] = padded.astype(BF)
        turned[...] = padded.T.astype(BF)


def padded_weights(one, two, pad, after):
    flat = pltpu.HBM((4 * CP, HID), BF)
    turned = pltpu.HBM((HID, 4 * CP), BF)
    return pl.pallas_call(
        weights_kernel,
        out_shape=[flat, turned, flat, turned],
        grid=(1,),
        in_specs=[full((C, HID)), full((C, HID)), full((C, 4 * CP))]
        + [pl.BlockSpec(memory_space=pl.ANY)] * len(after),
        out_specs=[full(x.shape) for x in (flat, turned, flat, turned)],
        compiler_params=pltpu.CompilerParams(vmem_limit_bytes=32 << 20),
        cost_estimate=cost(5),
        name="padded_weights",
    )(one, two, pad, *after)


def tap_patterns(kernel):
    lane = jnp.arange(4 * LANES)
    tile, pos = lane // LANES, lane % LANES
    away = jnp.where(pos % ROWS < ROWS // 2, pos % ROWS, pos % ROWS - ROWS)
    side = ((pos - away) // ROWS) % 2
    col = 2 * tile + side
    tap = jnp.where((jnp.abs(away) <= RIM) & (col < KW), (away + RIM) * KW + col, -1)
    pick = (jnp.arange(KW * KW)[:, None] == tap[None, :]).astype(BF)
    return jnp.dot(kernel.astype(BF), pick, preferred_element_type=F32).reshape(LC, 4, LANES)


def edge_picks():
    row = jnp.arange(8)[:, None]
    lane = jnp.arange(LANES)[None, :]
    head = ((row < RIM) & (lane == row)).astype(BF)
    tail = ((row < RIM) & (lane == LANES - RIM + row)).astype(BF)
    return head, tail


def edge_kernel(cells, pick, *refs):
    refs[-1][...] = dotg(pick[...], cells[...], 1, 1).astype(BF)


def edge(cells2d, pick, after=()):
    return pl.pallas_call(
        edge_kernel,
        out_shape=jax.ShapeDtypeStruct((8, cells2d.shape[0]), BF),
        grid=(1,),
        in_specs=[full(cells2d.shape), full(pick.shape)]
        + [pl.BlockSpec(memory_space=pl.ANY)] * len(after),
        out_specs=full((8, cells2d.shape[0])),
        compiler_params=pltpu.CompilerParams(vmem_limit_bytes=32 << 20),
        cost_estimate=cost(1),
        name="edge",
    )(cells2d, pick, *after)


def piece_edges_kernel(pick, *refs):
    first, last = refs[8:]
    for i in range(8):
        cells = refs[i][...].reshape(HR * CP, LANES)
        both = dotg(pick[...], cells, 1, 1).astype(BF)
        first[i] = both[:8]
        last[i] = both[8:]


def piece_edges(picks, early, late):
    half = pl.BlockSpec((QR // 2, CP, LANES), lambda i: (0, 0, 0))
    whole = pl.BlockSpec((8, 8, HR * CP), lambda i: (0, 0, 0))
    out = pltpu.HBM((8, 8, HR * CP), BF)
    return pl.pallas_call(
        piece_edges_kernel,
        out_shape=[out, out],
        grid=(1,),
        in_specs=[pl.BlockSpec((16, LANES), lambda i: (0, 0))]
        + [pl.BlockSpec((None, HR, CP, LANES), lambda i: (0, 0, 0, 0))] * 4
        + [half] * 4,
        out_specs=[whole] * 2,
        compiler_params=pltpu.CompilerParams(vmem_limit_bytes=32 << 20),
        cost_estimate=cost(2),
        name="piece_edges",
    )(picks, *early, *late)


def piece_rims_kernel(pick, first, last, out):
    for i in range(8):
        both = jnp.concatenate([first[i], last[i]], axis=0)
        out[i] = dotg(both, pick[...], 0, 0).astype(BF).reshape(HR, CP, LANES)


def piece_rims(picks, first, last):
    return pl.pallas_call(
        piece_rims_kernel,
        out_shape=jax.ShapeDtypeStruct((8, HR, CP, LANES), BF),
        grid=(1,),
        in_specs=[full((16, LANES)), full((8, 8, HR * CP)), full((8, 8, HR * CP))],
        out_specs=full((8, HR, CP, LANES)),
        compiler_params=pltpu.CompilerParams(vmem_limit_bytes=32 << 20),
        cost_estimate=cost(2),
        name="piece_rims",
    )(picks, first, last)


def rims(first, last):
    both = jnp.concatenate([lon_shift(first, -1), lon_shift(last, 1)], 0)
    return dotg(both, jnp.concatenate(edge_picks(), 0), 0, 0).astype(BF)


PLANES = [[16 * half + i for i in range(16)] for half in range(2)]


def plane_exchange(pieces):
    return lax.all_to_all(pieces, "lon", 0, 0, axis_index_groups=PLANES)


def total_kernel(*refs):
    total = refs[0][0].astype(F32)
    for i in range(1, 16):
        total = total + refs[0][i].astype(F32)
    refs[-1][...] = total.astype(BF)


def plane_total(pieces, after):
    return pl.pallas_call(
        total_kernel,
        out_shape=jax.ShapeDtypeStruct((PIECE, LANES), BF),
        grid=(1,),
        in_specs=[full((16, PIECE, LANES))] + [pl.BlockSpec(memory_space=pl.ANY)] * len(after),
        out_specs=full((PIECE, LANES)),
        compiler_params=pltpu.CompilerParams(vmem_limit_bytes=32 << 20),
        cost_estimate=cost(1.2),
        name="plane_total",
    )(pieces, *after)


def copies_kernel(part, *refs):
    out = refs[-1]
    for i in range(16):
        out[i] = part[...]


def plane_copies(part, after):
    return pl.pallas_call(
        copies_kernel,
        out_shape=jax.ShapeDtypeStruct((16, PIECE, LANES), BF),
        grid=(1,),
        in_specs=[full((PIECE, LANES))] + [pl.BlockSpec(memory_space=pl.ANY)] * len(after),
        out_specs=full((16, PIECE, LANES)),
        compiler_params=pltpu.CompilerParams(vmem_limit_bytes=32 << 20),
        cost_estimate=cost(1),
        name="plane_copies",
    )(part, *after)


def reduce_gradients(mine, late, from_right, from_left):
    mine = plane_exchange(mine.reshape(16, PIECE, LANES))
    mine, from_right, from_left = lax.optimization_barrier((mine, from_right, from_left))
    wire = plane_total(mine, late)
    part = (
        (wire.astype(F32) + lon_swap(wire, 16).astype(F32))
        + (ch_swap(wire, 2).astype(F32) + both_swap(wire).astype(F32))
    ).astype(BF)
    return plane_exchange(plane_copies(part, ())).reshape(WIRE, LANES), from_right, from_left


def finish_kernel(core_ref, own, other, pad, grad_in, grad_out, held):
    core = core_ref[0]
    for wire, slot in ((own, core), (other, 1 - core)):
        for t in range(3):
            held[slot, :, t * LANES : (t + 1) * LANES] = wire[t * HID : (t + 1) * HID, :]
        rest = wire[3 * HID : 3 * HID + 400, :]
        for q in range(4):
            held[slot, q * 400 : (q + 1) * 400, 3 * LANES :] = rest[:, q * 32 : (q + 1) * 32]
    factor = 1.0 / math.sqrt(ROWS * LANES * 32)
    grad_in[...] = dotg(pad[...], held[0], 1, 1) * factor
    grad_out[...] = dotg(pad[...], held[1], 1, 1) * factor


def finish(core, own, other, pad):
    return pl.pallas_call(
        finish_kernel,
        out_shape=[
            jax.ShapeDtypeStruct((C, HID), F32),
            jax.ShapeDtypeStruct((C, HID), F32),
        ],
        grid=(1,),
        in_specs=[
            pl.BlockSpec(memory_space=pltpu.SMEM),
            full((WIRE, LANES)),
            full((WIRE, LANES)),
            full((C, 4 * CP)),
        ],
        out_specs=[full((C, HID))] * 2,
        scratch_shapes=[pltpu.VMEM((2, HID, 4 * CP), BF)],
        compiler_params=pltpu.CompilerParams(vmem_limit_bytes=32 << 20),
        cost_estimate=cost(6),
        name="finish",
    )(core, own, other, pad)


def both_swap(x):
    return lax.ppermute(x, ("lon", "ch"), [(i, i ^ (16 * 4 + 2)) for i in range(128)])


def body(
    ocean_state,
    sea_mask,
    kernel,
    conv_bias,
    norm_gain,
    norm_bias,
    weight_in,
    bias_in,
    weight_out,
    bias_out,
    layer_scale,
    cotangent,
):
    ch = lax.axis_index("ch")
    me = ch.reshape(1)
    core = (ch & 1).reshape(1)
    scale = jnp.pad(layer_scale, (0, CP - LC)).reshape(CP, 1)

    head, tail = edge_picks()
    state2d = ocean_state.reshape(LC * ROWS, LANES)
    sent = {}
    first = edge(state2d, head)
    sent[2] = branch_share(me, cotangent, sea_mask, scale, 2, (first,))
    last = edge(state2d, tail, (sent[2],))
    sent[3] = branch_share(me, cotangent, sea_mask, scale, 3, (last,))
    sent[1] = branch_share(me, cotangent, sea_mask, scale, 1, (sent[3],))
    sent[0] = branch_share(me, cotangent, sea_mask, scale, 0, (sent[1],))
    gs = [sent[0]] + [ch_swap(sent[k], k) for k in (1, 2, 3)]

    chan = jnp.arange(C)
    padded = jnp.arange(4 * CP)
    pad = ((chan // LC * CP + chan % LC)[:, None] == padded[None, :]).astype(BF)
    pad_own = (((chan // LC ^ ch) * CP + chan % LC)[:, None] == padded[None, :]).astype(BF)
    vec = jnp.stack([norm_gain, norm_bias, bias_out], 1).reshape(4, LC, 3)
    vec = jnp.pad(vec, ((0, 0), (0, CP - LC), (0, 0)))
    vec = jnp.concatenate([lax.dynamic_index_in_dim(vec, ch ^ k, 0, False) for k in range(4)], 0)

    state_rim = rims(first, last).reshape(LC, ROWS, LANES)
    bias = jnp.broadcast_to(conv_bias[:, None, None], (LC, 1, LANES))
    conv = conv_forward(me, ocean_state, state_rim, tap_patterns(kernel), bias)
    win, win_t, wout_t, wout = padded_weights(weight_in, weight_out.T, pad_own, conv[:1])
    weights, gs, second = lax.optimization_barrier(((win_t, win, wout, wout_t), gs, conv[4:]))
    xs = [
        [half[0]] + [ch_swap(half[k], k) for k in (1, 2, 3)] for half in (conv[:4], second)
    ]

    bias_rows = bias_in.reshape(HID, 1)
    early, _, (hid_a, cells_a) = mlp(0, me, core, xs[0], gs, weights, vec, bias_rows)
    early, second = lax.optimization_barrier((early, xs[1]))
    saved = (hid_a, cells_a.reshape(2, 4 * CP, 2 * CELLS))
    grad_b, branch_b, (keep, send) = mlp(
        1, me, core, second, gs, weights, vec, bias_rows, saved, early[:1]
    )
    early = [early[0]] + [ch_swap(early[k], k) for k in (1, 2, 3)]
    keep, send, early = lax.optimization_barrier((keep, send, early))
    grad_b = [grad_b[0]] + [ch_swap(grad_b[k], k) for k in (1, 2, 3)]
    mine = (keep.astype(F32) + ch_swap(send, 1).astype(F32)).astype(BF)
    mine, grad_b, branch_b = lax.optimization_barrier((mine, grad_b, branch_b))
    branch_b = [branch_b[0]] + [ch_swap(branch_b[k], k) for k in (1, 2, 3)]
    updated = update(me, early, branch_b, ocean_state, sea_mask, scale)
    picks = jnp.concatenate([head, tail], 0)
    first, last = piece_edges(picks, early, grad_b)
    from_right, from_left = lon_shift(first, -1), lon_shift(last, 1)
    own, from_right, from_left = reduce_gradients(mine, branch_b[1:], from_right, from_left)
    grad_rims = piece_rims(picks, from_right, from_left)

    grad_state = conv_backward(
        me,
        early,
        grad_b,
        grad_rims,
        tap_patterns(kernel[:, ::-1]),
        cotangent,
        sea_mask,
    )
    own, grad_state, updated = lax.optimization_barrier((own, grad_state, updated))
    grad_in, grad_out = finish(core, own, ch_swap(own, 1), pad)
    return updated, grad_state, grad_in, grad_out.T


def solution(mesh):
    return jax.shard_map(
        body,
        mesh=mesh,
        in_specs=(
            P("ch", None, "lon"),
            P(None, "lon"),
            P("ch", None),
            P("ch"),
            P(),
            P(),
            P(),
            P(),
            P(),
            P(),
            P("ch"),
            P("ch", None, "lon"),
        ),
        out_specs=(P("ch", None, "lon"), P("ch", None, "lon"), P(), P()),
        check_vma=False,
    )
```
